32 devices in a mesh: space: 8 (over y, x, core), mode: 4 (over z).
Axes of the slice: x: 2, y: 2, z: 4, core: 2. Of those that a mesh axis runs over, the one named last changes fastest.
Arguments:
- basis: bfloat16 [32, 5, 16384], P('mode', None, 'space'), may hold values from -144 to 144
- jacobian: bfloat16 [3, 5, 5, 16384], P(None, None, None, 'space'), may hold values from -1.5 to 1.5
- sample_list: int32 [8, 16], P('space'), may hold values from 0 to 127, as said below
- sample_weight: float32 [8, 16], P('space'), may hold values from 0.25 to 2
Outputs:
- update: float32 [32, 5, 16384], P('mode', None, 'space')
The draws below stay inside these ranges and needn't reach their ends.
Inputs may be any that keep to these rules, and one draw needn't show every extreme that they name: `sample_list`: row o holds 16 different tile numbers: exactly 4 from each of 4 different devices (device s holds tiles 16 * s to 16 * s + 15), one of which is device o itself, whose first and last tiles are in the row.
All inputs are finite; a program needn't handle non-finite values.
Results may differ from the reference program's by a relative error of at most 0.005.
Values may be sent and summed in bfloat16 or wider, within the bound.
No kernel may reach another device: no remote copies, remote signals or barrier semaphores. Data moves between devices by JAX's collectives and lax.ppermute only.
A program may use at most 64 MiB of HBM per device.

```python
import math
import jax
import jax.numpy as jnp
from jax import lax

F = 5
PANEL = 32
TILE = 128
TILES_DEV = 16
CAP = 4
LIST = 16
TILES = 128
CELLS = 16384
N_SPACE = 8


def draw_basis(key, part):
    value_key = jax.random.fold_in(key, 0)
    jitter_key = jax.random.fold_in(key, 1)
    field_key = jax.random.fold_in(key, 3)
    mode_index = jnp.arange(PANEL, dtype=jnp.float32)
    jitter = jax.random.uniform(jitter_key, (PANEL,), jnp.float32, 0.8, 1.25)
    mode_scale = 0.3 * jnp.power(10.0, mode_index / max(PANEL - 1, 1)) * jitter
    field_scale = jnp.exp(jax.random.uniform(field_key, (F,), jnp.float32, 0.0, 1.1))
    values_raw = jax.random.truncated_normal(value_key, -4.0, 4.0, (PANEL, F, CELLS), jnp.float32)
    cell_index = jnp.arange(CELLS, dtype=jnp.int32)
    block_start = cell_index % (TILES_DEV * TILE) == 0
    cell_boost = jnp.where(block_start, 6.0, 1.0).astype(jnp.float32)
    return (values_raw * mode_scale[:, None, None] * field_scale[None, :, None] * 0.5 * cell_boost[None, None, :]).astype(jnp.bfloat16)


def draw_sample_list(key, part):
    space_count = TILES // TILES_DEV
    groups = LIST // CAP
    hot_key, owner_key = jax.random.split(key, 2)
    hot_order = jax.random.permutation(hot_key, space_count)
    hot = (hot_order < max(space_count // 4, 1)).astype(jnp.int32)
    devices = jnp.arange(space_count, dtype=jnp.int32)

    def one_owner(owner_index):
        owner_seed = jax.random.fold_in(owner_key, owner_index)
        score_key, inner_key, other_key, shuffle_key = jax.random.split(owner_seed, 4)
        jitter_score = jax.random.randint(score_key, (space_count,), 0, 1000)
        scores = (jitter_score + 600 * hot) * space_count + devices
        scores = jnp.where(devices == owner_index, -1, scores)
        _, chosen = lax.top_k(scores, groups - 1)
        sources = jnp.concatenate([owner_index[None], chosen.astype(jnp.int32)])

        def group_tiles(group_index):
            middle_tiles = jax.random.permutation(jax.random.fold_in(inner_key, group_index), TILES_DEV - 2)[:CAP - 2] + 1
            forced = jnp.array([0, TILES_DEV - 1], jnp.int32)
            own_tiles = jnp.concatenate([forced, middle_tiles.astype(jnp.int32)])
            others = jax.random.permutation(jax.random.fold_in(other_key, group_index), TILES_DEV)[:CAP].astype(jnp.int32)
            return jnp.where(group_index == 0, own_tiles, others)
        group_picks = jax.vmap(group_tiles)(jnp.arange(groups, dtype=jnp.int32))
        tile_ids = (sources[:, None] * TILES_DEV + group_picks).reshape(-1)
        shuffle = jax.random.permutation(shuffle_key, LIST)
        return tile_ids[shuffle].astype(jnp.int32)
    return jax.vmap(one_owner)(devices)


def steps_of(own_key, extent, cuts, low, top_value):
    level, own = 1.0, jax.random.fold_in(own_key, 6)
    for dim, shards_of in cuts:
        steps = jnp.exp(jax.random.uniform(jax.random.fold_in(own, dim), (shards_of,), jnp.float32, low / len(cuts), top_value / len(cuts)))
        level = level * jnp.repeat(steps, extent[dim] // shards_of).reshape([-1 if axis == dim else 1 for axis in range(len(extent))])
    return level


def bell_draw(key, shape, spread, most, pieces=(), held_as=jnp.bfloat16):
    entries = spread * jax.random.normal(key, shape, jnp.float32)
    if pieces:
        entries = entries * steps_of(key, shape, pieces, -0.22, 0.18)
    return jnp.clip(entries, -most, most).astype(held_as)


def setup_inputs(seed: int = 0) -> dict:
    key_list = jax.random.split(jax.random.key(seed), 5)
    return {
        "basis": draw_basis(jax.random.fold_in(key_list[4], 71), 0),
        "jacobian": bell_draw(key_list[1], (3, F, F, CELLS), (3 * F) ** -0.5, 1.5, ((3, 8),)),
        "sample_list": draw_sample_list(jax.random.fold_in(key_list[4], 71), 0),
        "sample_weight": jnp.clip(jnp.exp(math.log(2.0) - 2.0794415 * jax.random.uniform(key_list[3], (N_SPACE, LIST), jnp.float32) ** steps_of(key_list[3], (N_SPACE, LIST), ((0, 8),), -0.2, 0.2)), 0.25, 2.0),
    }


def forward_apply(neighbor_link, field):
    values = field.astype(jnp.float32)
    edge_zeros = jnp.zeros((values.shape[0], 1), jnp.float32)
    western_cells = jnp.concatenate([edge_zeros, values[:, :-1]], axis=1)
    eastern_cells = jnp.concatenate([values[:, 1:], edge_zeros], axis=1)
    result = jnp.einsum('fgc,gc->fc', neighbor_link[0], values)
    result = result + jnp.einsum('fgc,gc->fc', neighbor_link[1], western_cells)
    return result + jnp.einsum('fgc,gc->fc', neighbor_link[2], eastern_cells)

def adjoint_apply(neighbor_link, quadrature_weight):
    edge_zeros = jnp.zeros((quadrature_weight.shape[0], 1), jnp.float32)
    center_stencil = jnp.einsum('pam,pm->am', neighbor_link[0], quadrature_weight)
    below_stencil = jnp.einsum('pam,pm->am', neighbor_link[1], quadrature_weight)
    above_stencil = jnp.einsum('pam,pm->am', neighbor_link[2], quadrature_weight)
    result = center_stencil + jnp.concatenate([below_stencil[:, 1:], edge_zeros], axis=1)
    return result + jnp.concatenate([edge_zeros, above_stencil[:, :-1]], axis=1)

def reference(basis, jacobian, sample_list, sample_weight):
    neighbor_link = jacobian.astype(jnp.float32)
    operator_result = lax.map(lambda field: forward_apply(neighbor_link, field).astype(jnp.bfloat16), basis)
    owners = sample_list.shape[0]
    tile_view = operator_result.reshape(PANEL, F, TILES, TILE)
    tile_ids = sample_list.reshape(-1).astype(jnp.int32)
    picked = jnp.take(tile_view, tile_ids, axis=2).reshape(PANEL, F, owners, LIST, TILE)
    sample_rows = jnp.einsum('pfolc,ol->opfc', picked.astype(jnp.float32), sample_weight)
    mean_square = lax.optimization_barrier(jnp.sum(sample_rows * sample_rows, axis=(1, 2))) / (PANEL * F)
    normalized = sample_rows * lax.rsqrt(mean_square + 1e-05)[:, None, None, :]
    scaled = (sample_weight[:, :, None, None, None] * normalized[:, None]).astype(jnp.bfloat16)
    flat_rows = scaled.reshape(owners * LIST, PANEL, F, TILE)

    def one_mode(mode_index):
        contribution = jax.ops.segment_sum(flat_rows[:, mode_index].astype(jnp.float32), tile_ids, num_segments=TILES)
        returned = contribution.transpose(1, 0, 2).reshape(F, CELLS)
        return basis[mode_index].astype(jnp.float32) + adjoint_apply(neighbor_link, returned)
    return lax.map(one_mode, jnp.arange(PANEL))
```

```python
import functools
import jax
import jax.numpy as jnp
from jax import lax
from jax.experimental import pallas as pl
from jax.experimental.pallas import tpu as pltpu
from jax.sharding import PartitionSpec as P

TILE = 128
ROWS = 8
EPS = 1e-05
F32 = jnp.float32
BF16 = jnp.bfloat16


def whole_block(shape):
    return pl.BlockSpec(shape, lambda i: (0,) * len(shape))


def edge_block(shape, last):
    lead = len(shape) - 1
    place = shape[-1] // TILE - 1 if last else 0
    return pl.BlockSpec(shape[:-1] + (TILE,), lambda i: (0,) * lead + (place,))


def edges_kernel(list_ref, weight_ref, b_head, b_tail, j_head, j_tail, out_ref):
    fields, modes, _ = b_head.shape
    length = list_ref.shape[1]
    lane = lax.broadcasted_iota(jnp.int32, (modes, TILE), 1)
    sub = lax.broadcasted_iota(jnp.int32, (modes, TILE), 0)
    lane1 = lax.broadcasted_iota(jnp.int32, (1, TILE), 1)

    def basis_row(ref, at):
        total = jnp.zeros((modes, TILE), F32)
        for g in range(fields):
            column = ref[g].astype(F32)[:, at : at + 1]
            total = total + jnp.where(lane == g * modes + sub, column, 0.0)
        return jnp.sum(total, axis=0, keepdims=True)

    def coupling_row(ref, kind, at):
        total = jnp.zeros((1, TILE), F32)
        for f in range(fields):
            for g in range(fields):
                value = ref[f, g].astype(F32)[kind : kind + 1, at : at + 1]
                total = jnp.where(lane1 == f * fields + g, value, total)
        return total

    out_ref[0] = jnp.zeros((ROWS, TILE), F32)
    out_ref[0, 0:1, 0:length] = list_ref[...].astype(F32)
    out_ref[0, 1:2, 0:length] = weight_ref[...]
    out_ref[0, 2:3, :] = basis_row(b_head, 0)
    out_ref[0, 3:4, :] = basis_row(b_tail, TILE - 1)
    out_ref[0, 4:5, :] = coupling_row(j_head, 1, 0)
    out_ref[0, 5:6, :] = coupling_row(j_tail, 2, TILE - 1)
    packed = out_ref[0]
    for d in range(1, out_ref.shape[0]):
        out_ref[d] = packed


def weight_matrix(shared_ref, modes, tiles_here, length, width):
    owners = shared_ref.shape[0]
    lists = shared_ref[:, 0, :]
    weights = shared_ref[:, 1, :]
    lane = lax.broadcasted_iota(jnp.int32, (owners, width), 1)
    tile = lane // modes
    base = lax.axis_index("space") * tiles_here
    tile = jnp.where(tile <= tiles_here, base + tile, jnp.where(tile == tiles_here + 1, base - 1, -2))
    tile = tile.astype(F32)
    total = jnp.zeros((owners, width), F32)
    for entry in range(length):
        total = total + jnp.where(lists[:, entry : entry + 1] == tile, weights[:, entry : entry + 1], 0.0)
    lane = lax.broadcasted_iota(jnp.int32, (modes, width), 1)
    sub = lax.broadcasted_iota(jnp.int32, (modes, width), 0)
    same = lane % modes == sub
    return jnp.concatenate([jnp.where(same, total[o : o + 1], 0.0) for o in range(owners)], axis=0)


def split(values):
    high = values.astype(BF16)
    return high, (values - high.astype(F32)).astype(BF16)


def applied_kernel(length, shared_ref, b_ref, j_ref, part_ref, w_ref, lower, upper, applied):
    fields, modes, cells = b_ref.shape
    owners = shared_ref.shape[0]
    tiles_here = cells // TILE
    me = lax.axis_index("space")
    before = jnp.maximum(me - 1, 0)
    after = jnp.minimum(me + 1, owners - 1)
    last_row = shared_ref[before, 3:4, :] * (me > 0).astype(F32)
    first_row = shared_ref[after, 2:3, :] * (me < owners - 1).astype(F32)
    lane = lax.broadcasted_iota(jnp.int32, (modes, TILE), 1)
    sub = lax.broadcasted_iota(jnp.int32, (modes, TILE), 0)
    wide = lax.broadcasted_iota(jnp.int32, (modes, cells), 1)
    for g in range(fields):
        mine = lane == g * modes + sub
        left = jnp.sum(jnp.where(mine, last_row, 0.0), axis=1, keepdims=True)
        right = jnp.sum(jnp.where(mine, first_row, 0.0), axis=1, keepdims=True)
        values = b_ref[g].astype(F32)
        lower[g] = jnp.where(wide == 0, left, pltpu.roll(values, 1, 1))
        upper[g] = jnp.where(wide == cells - 1, right, pltpu.roll(values, cells - 1, 1))
    for t in range(tiles_here):
        at = slice(t * TILE, (t + 1) * TILE)
        center = [b_ref[g, :, at].astype(F32) for g in range(fields)]
        below = [lower[g, :, at] for g in range(fields)]
        above = [upper[g, :, at] for g in range(fields)]
        for f in range(fields):
            total = jnp.zeros((modes, TILE), F32)
            for g in range(fields):
                link = j_ref[f, g, :, at].astype(F32)
                total = total + link[0:1] * center[g]
                total = total + link[1:2] * below[g]
                total = total + link[2:3] * above[g]
            applied[f, t * modes : (t + 1) * modes, :] = total
    matrix = weight_matrix(shared_ref, modes, tiles_here, length, w_ref.shape[1])
    w_ref[...] = matrix
    high, low = split(matrix[:, : tiles_here * modes])
    for f in range(fields):
        rows = applied[f].astype(BF16)
        part = jnp.dot(high, rows, preferred_element_type=F32) + jnp.dot(low, rows, preferred_element_type=F32)
        part_ref[f] = part.astype(BF16)


def rows_kernel(modes, parts_ref, rows_ref, square_ref):
    count, fields, height, _ = parts_ref.shape
    owners = height // modes
    squares = jnp.zeros((height, TILE), F32)
    for f in range(fields):
        total = parts_ref[0, f].astype(F32)
        for s in range(1, count):
            total = total + parts_ref[s, f].astype(F32)
        rows_ref[f] = total
        squares = squares + total * total
    for o in range(owners):
        square_ref[o : o + 1, :] = jnp.sum(squares[o * modes : (o + 1) * modes], axis=0, keepdims=True)


def update_kernel(samples, shared_ref, w_ref, rows_ref, b_ref, j_ref, *rest):
    square_refs = rest[:-4]
    out_ref, returned, lower, upper = rest[-4:]
    fields, modes, cells = b_ref.shape
    tiles_here = cells // TILE
    owners = square_refs[0].shape[0]
    me = lax.axis_index("space")
    before = jnp.maximum(me - 1, 0)
    after = jnp.minimum(me + 1, owners - 1)
    square = square_refs[0][...]
    for ref in square_refs[1:]:
        square = square + ref[...]
    factor = lax.rsqrt(square / samples + EPS)
    factor = jnp.concatenate(
        [jnp.broadcast_to(factor[o : o + 1], (modes, TILE)) for o in range(owners)], axis=0
    )
    high, low = split(jnp.transpose(w_ref[...]))
    for g in range(fields):
        normalized = (rows_ref[g] * factor).astype(BF16)
        returned[g] = jnp.dot(high, normalized, preferred_element_type=F32) + jnp.dot(
            low, normalized, preferred_element_type=F32
        )
    for t in range(tiles_here):
        at = slice(t * TILE, (t + 1) * TILE)
        values = [returned[g, t * modes : (t + 1) * modes, :] for g in range(fields)]
        for f in range(fields):
            center = b_ref[f, :, at].astype(F32)
            below = jnp.zeros((modes, TILE), F32)
            above = jnp.zeros((modes, TILE), F32)
            for g in range(fields):
                link = j_ref[g, f, :, at].astype(F32)
                center = center + link[0:1] * values[g]
                below = below + link[1:2] * values[g]
                above = above + link[2:3] * values[g]
            out_ref[f, :, at] = center
            lower[f, :, at] = below
            upper[f, :, at] = above
    wide = lax.broadcasted_iota(jnp.int32, (modes, cells), 1)
    nexts = slice(tiles_here * modes, (tiles_here + 1) * modes)
    lasts = slice((tiles_here + 1) * modes, (tiles_here + 2) * modes)
    for f in range(fields):
        head = jnp.zeros((modes, TILE), F32)
        tail = jnp.zeros((modes, TILE), F32)
        for g in range(fields):
            head = head + shared_ref[after, 4, g * fields + f] * returned[g, nexts, :]
            tail = tail + shared_ref[before, 5, g * fields + f] * returned[g, lasts, :]
        below = jnp.where(wide == cells - 1, head[:, 0:1], pltpu.roll(lower[f], cells - 1, 1))
        above = jnp.where(wide == 0, tail[:, TILE - 1 : TILE], pltpu.roll(upper[f], 1, 1))
        out_ref[f] = out_ref[f] + below + above


def shards(basis, jacobian, sample_list, sample_weight):
    space = lax.axis_size("space")
    mode = lax.axis_size("mode")
    modes, fields, cells = basis.shape
    length = sample_list.shape[1]
    tiles_here = cells // TILE
    height = space * modes
    width = pl.cdiv((tiles_here + 2) * modes, TILE) * TILE
    b = jnp.transpose(basis, (1, 0, 2))
    j = jnp.transpose(jacobian, (1, 2, 0, 3))

    packed = pl.pallas_call(
        edges_kernel,
        out_shape=jax.ShapeDtypeStruct((space, ROWS, TILE), F32),
        in_specs=[
            whole_block(sample_list.shape),
            whole_block(sample_weight.shape),
            edge_block(b.shape, False),
            edge_block(b.shape, True),
            edge_block(j.shape, False),
            edge_block(j.shape, True),
        ],
        out_specs=whole_block((space, ROWS, TILE)),
        grid=(1,),
        name="edges",
    )(sample_list, sample_weight, b, b, j, j)
    shared = lax.all_to_all(packed, "space", split_axis=0, concat_axis=0, tiled=True)

    parts, matrix = pl.pallas_call(
        functools.partial(applied_kernel, length),
        out_shape=(
            jax.ShapeDtypeStruct((fields, height, TILE), BF16),
            jax.ShapeDtypeStruct((height, width), F32),
        ),
        scratch_shapes=[
            pltpu.VMEM((fields, modes, cells), F32),
            pltpu.VMEM((fields, modes, cells), F32),
            pltpu.VMEM((fields, tiles_here * modes, TILE), F32),
        ],
        name="applied",
    )(shared, b, j)
    gathered = lax.all_gather(parts, "space", axis=0)

    rows, square = pl.pallas_call(
        functools.partial(rows_kernel, modes),
        out_shape=(
            jax.ShapeDtypeStruct((fields, height, TILE), F32),
            jax.ShapeDtypeStruct((space, TILE), F32),
        ),
        name="rows",
    )(gathered)
    squares = [square] + [
        lax.ppermute(square, "mode", [(i, (i + d) % mode) for i in range(mode)]) for d in range(1, mode)
    ]

    update = pl.pallas_call(
        functools.partial(update_kernel, mode * modes * fields),
        out_shape=jax.ShapeDtypeStruct((fields, modes, cells), F32),
        in_specs=[pl.BlockSpec(memory_space=pltpu.SMEM)] + [pl.BlockSpec(memory_space=pltpu.VMEM)] * (4 + mode),
        out_specs=pl.BlockSpec(memory_space=pltpu.VMEM),
        scratch_shapes=[
            pltpu.VMEM((fields, width, TILE), F32),
            pltpu.VMEM((fields, modes, cells), F32),
            pltpu.VMEM((fields, modes, cells), F32),
        ],
        name="update",
    )(shared, matrix, rows, b, j, *squares)
    return jnp.transpose(update, (1, 0, 2))


def solution(mesh):
    placed = (
        P("mode", None, "space"),
        P(None, None, None, "space"),
        P("space", None),
        P("space", None),
    )
    return jax.shard_map(
        shards, mesh=mesh, in_specs=placed, out_specs=P("mode", None, "space"), check_vma=False
    )
```

```python
import functools
import jax
import jax.numpy as jnp
from jax import lax
from jax.experimental import pallas as pl
from jax.experimental.pallas import tpu as pltpu
from jax.sharding import PartitionSpec as P

TILE = 128
EPS = 1e-05
F32 = jnp.float32
BF16 = jnp.bfloat16
CORES = 2


def over(values, by):
    return lax.shift_right_logical(values, by.bit_length() - 1) if by & (by - 1) == 0 else values // by


def modulo(values, by):
    return values & (by - 1) if by & (by - 1) == 0 else values % by


def layout(fields, modes, tiles_here):
    starts = [0]
    for rows in (fields * tiles_here * modes, fields * modes, fields * fields, 5):
        starts.append(pl.cdiv(starts[-1] + rows, 16) * 16)
    return starts


def split(values):
    high = values.astype(BF16)
    return high, (values - high.astype(F32)).astype(BF16)


def applied_kernel(list_ref, weight_ref, b_ref, j_ref, out_ref, lower, upper, applied):
    fields, modes, cells = b_ref.shape
    length = list_ref.shape[1]
    tiles_here = cells // TILE
    height = tiles_here * modes
    _, basis_at, link_at, list_at, _ = layout(fields, modes, tiles_here)
    wide = lax.broadcasted_iota(jnp.int32, (modes, cells), 1)
    half = lax.broadcasted_iota(jnp.int32, (modes, TILE), 1) < TILE // 2
    for g in range(fields):
        values = b_ref[g].astype(F32)
        below = pltpu.roll(values, 1, 1)
        above = pltpu.roll(values, cells - 1, 1)
        edge = jnp.where(half, below[:, :TILE], above[:, cells - TILE :])
        out_ref[basis_at + g * modes : basis_at + (g + 1) * modes, :] = edge.astype(BF16)
        lower[g] = jnp.where(wide == 0, 0.0, below)
        upper[g] = jnp.where(wide == cells - 1, 0.0, above)
    for t in range(tiles_here):
        at = slice(t * TILE, (t + 1) * TILE)
        center = [b_ref[g, :, at].astype(F32) for g in range(fields)]
        below = [lower[g, :, at] for g in range(fields)]
        above = [upper[g, :, at] for g in range(fields)]
        for f in range(fields):
            total = jnp.zeros((modes, TILE), F32)
            for g in range(fields):
                link = j_ref[f, g, :, at].astype(F32)
                total = total + link[0:1] * center[g]
                total = total + link[1:2] * below[g]
                total = total + link[2:3] * above[g]
            applied[f * height + t * modes : f * height + (t + 1) * modes, :] = total
    out_ref[0 : fields * height, :] = applied[...].astype(BF16)
    half = half[0:1]
    rows = []
    for f in range(fields):
        for g in range(fields):
            head = j_ref[f, g, :, 0:TILE].astype(F32)[1:2]
            tail = j_ref[f, g, :, cells - TILE :].astype(F32)[2:3]
            rows.append(jnp.where(half, head, tail))
    out_ref[link_at : link_at + fields * fields, :] = jnp.concatenate(rows, axis=0).astype(BF16)
    tiles = list_ref[...]
    device = over(tiles, tiles_here)
    high, low = split(weight_ref[...])
    rest = weight_ref[...] - high.astype(F32) - low.astype(F32)
    rows = [device.astype(F32), (tiles - device * tiles_here).astype(F32), high.astype(F32), low.astype(F32), rest]
    out_ref[list_at:, :] = jnp.zeros((out_ref.shape[0] - list_at, TILE), BF16)
    out_ref[list_at : list_at + 5, 0:length] = jnp.concatenate(rows, axis=0).astype(BF16)


def weight_rows(lists, weights, tile, modes, length):
    owners = lists.shape[0]
    width = tile.shape[1]
    total = jnp.zeros((owners, width), F32)
    for entry in range(length):
        total = total + jnp.where(lists[:, entry : entry + 1] == tile, weights[:, entry : entry + 1], 0.0)
    lane = lax.broadcasted_iota(jnp.int32, (modes, width), 1)
    sub = lax.broadcasted_iota(jnp.int32, (modes, width), 0)
    same = modulo(lane, modes) == sub
    return jnp.concatenate([jnp.where(same, total[o : o + 1], 0.0) for o in range(owners)], axis=0)


def rows_kernel(fields, modes, tiles_here, length, mine, other, rows_ref, square_ref, w_ref, link_ref, extra):
    chips = mine.shape[0]
    devices = chips * CORES
    height = tiles_here * modes
    _, basis_at, link_at, list_at, _ = layout(fields, modes, tiles_here)
    me = lax.axis_index("space")
    core = lax.rem(me, CORES)
    chip = lax.div(me, CORES)
    lane = lax.broadcasted_iota(jnp.int32, (modes, TILE), 1)
    sources = [(mine, other, q, core) for q in range(chips)] + [(other, mine, q, 1 - core) for q in range(chips)]

    lists, weights = [], []
    for ref, _, q, _ in sources:
        part = ref[q, list_at : list_at + 5, :].astype(F32)
        lists.append(part[0:1] * tiles_here + part[1:2])
        weights.append(part[2:3] + part[3:4] + part[4:5])
    lists = jnp.concatenate(lists, axis=0)
    weights = jnp.concatenate(weights, axis=0)

    def device_of(source):
        first = source < chips
        return CORES * jnp.where(first, source, source - chips) + jnp.where(first, core, 1 - core)

    inner = devices * height
    total = inner + devices * 2 * modes
    column = lax.broadcasted_iota(jnp.int32, (devices, total), 1)
    outer = column - inner
    tile = jnp.where(
        outer < 0,
        device_of(over(column, height)) * tiles_here + modulo(over(column, modes), tiles_here),
        device_of(over(outer, 2 * modes)) * tiles_here + modulo(over(outer, modes), 2) * (tiles_here - 1),
    )
    matrix = weight_rows(lists, weights, tile.astype(F32), modes, length)
    high, low = split(matrix)

    for index, (ref, opposite, q, kind) in enumerate(sources):
        place = CORES * q + kind
        before = opposite[jnp.maximum(q - 1 + kind, 0), basis_at : basis_at + fields * modes, :].astype(F32)
        after = opposite[jnp.minimum(q + kind, chips - 1), basis_at : basis_at + fields * modes, :].astype(F32)
        before = before * (place > 0).astype(F32)
        after = after * (place < devices - 1).astype(F32)
        links = ref[q, link_at : link_at + fields * fields, :].astype(F32)
        left = lane < TILE // 2
        near = [
            jnp.where(left, before[g * modes : (g + 1) * modes], after[g * modes : (g + 1) * modes])
            for g in range(fields)
        ]
        for f in range(fields):
            halo = jnp.zeros((modes, TILE), F32)
            for g in range(fields):
                halo = halo + links[f * fields + g : f * fields + g + 1] * near[g]
            at = index * 2 * modes
            extra[f, at : at + modes, :] = jnp.where(lane == 0, halo, 0.0)
            extra[f, at + modes : at + 2 * modes, :] = jnp.where(lane == TILE - 1, halo, 0.0)

    squares = jnp.zeros((devices * modes, TILE), F32)
    for f in range(fields):
        tiles = jnp.concatenate(
            [ref[q, f * height : (f + 1) * height, :] for ref, _, q, _ in sources] + [extra[f].astype(BF16)], axis=0
        )
        rows = jnp.dot(high, tiles, preferred_element_type=F32) + jnp.dot(low, tiles, preferred_element_type=F32)
        rows_ref[f] = rows
        squares = squares + rows * rows
    for o in range(devices):
        square_ref[o : o + 1, :] = jnp.sum(squares[o * modes : (o + 1) * modes], axis=0, keepdims=True)

    column = lax.broadcasted_iota(jnp.int32, (devices, w_ref.shape[1]), 1)
    local = over(column, modes)
    base = me * tiles_here
    tile = jnp.where(local <= tiles_here, base + local, jnp.where(local == tiles_here + 1, base - 1, -2))
    w_ref[...] = weight_rows(lists, weights, tile.astype(F32), modes, length)
    link_ref[0] = other[jnp.minimum(chip + core, chips - 1), link_at : link_at + fields * fields, :].astype(F32)
    link_ref[1] = other[jnp.maximum(chip - 1 + core, 0), link_at : link_at + fields * fields, :].astype(F32)


def update_kernel(factor_ref, w_ref, rows_ref, link_ref, b_ref, j_ref, out_ref, returned, lower, upper):
    fields, modes, cells = b_ref.shape
    tiles_here = cells // TILE
    owners = factor_ref.shape[0]
    factor = jnp.concatenate(
        [jnp.broadcast_to(factor_ref[o : o + 1, :], (modes, TILE)) for o in range(owners)], axis=0
    )
    high, low = split(jnp.transpose(w_ref[...]))
    for g in range(fields):
        normalized = (rows_ref[g] * factor).astype(BF16)
        returned[g] = jnp.dot(high, normalized, preferred_element_type=F32) + jnp.dot(
            low, normalized, preferred_element_type=F32
        )
    for t in range(tiles_here):
        at = slice(t * TILE, (t + 1) * TILE)
        values = [returned[g, t * modes : (t + 1) * modes, :] for g in range(fields)]
        for f in range(fields):
            center = b_ref[f, :, at].astype(F32)
            below = jnp.zeros((modes, TILE), F32)
            above = jnp.zeros((modes, TILE), F32)
            for g in range(fields):
                link = j_ref[g, f, :, at].astype(F32)
                center = center + link[0:1] * values[g]
                below = below + link[1:2] * values[g]
                above = above + link[2:3] * values[g]
            out_ref[f, :, at] = center
            lower[f, :, at] = below
            upper[f, :, at] = above
    wide = lax.broadcasted_iota(jnp.int32, (modes, cells), 1)
    nexts = slice(tiles_here * modes, (tiles_here + 1) * modes)
    lasts = slice((tiles_here + 1) * modes, (tiles_here + 2) * modes)
    for f in range(fields):
        head = jnp.zeros((modes, TILE), F32)
        tail = jnp.zeros((modes, TILE), F32)
        for g in range(fields):
            at = slice(g * fields + f, g * fields + f + 1)
            head = head + link_ref[0, at, :] * returned[g, nexts, :]
            tail = tail + link_ref[1, at, :] * returned[g, lasts, :]
        below = jnp.where(wide == cells - 1, head[:, 0:1], pltpu.roll(lower[f], cells - 1, 1))
        above = jnp.where(wide == 0, tail[:, TILE - 1 : TILE], pltpu.roll(upper[f], 1, 1))
        out_ref[f] = out_ref[f] + below + above


def shards(basis, jacobian, sample_list, sample_weight):
    space = lax.axis_size("space")
    mode = lax.axis_size("mode")
    modes, fields, cells = basis.shape
    length = sample_list.shape[1]
    tiles_here = cells // TILE
    height = space * modes
    width = pl.cdiv((tiles_here + 2) * modes, TILE) * TILE
    sent_rows = layout(fields, modes, tiles_here)[-1]
    b = jnp.transpose(basis, (1, 0, 2))
    j = jnp.transpose(jacobian, (1, 2, 0, 3))

    sent = pl.pallas_call(
        applied_kernel,
        out_shape=jax.ShapeDtypeStruct((sent_rows, TILE), BF16),
        scratch_shapes=[
            pltpu.VMEM((fields, modes, cells), F32),
            pltpu.VMEM((fields, modes, cells), F32),
            pltpu.VMEM((fields * tiles_here * modes, TILE), F32),
        ],
        name="applied",
    )(sample_list, sample_weight, b, j)
    chips = [[core + CORES * q for q in range(space // CORES)] for core in range(CORES)]
    mine = lax.all_gather(sent, "space", axis=0, axis_index_groups=chips)
    other = lax.ppermute(mine, "space", [(i, i ^ 1) for i in range(space)])

    rows, square, matrix, links = pl.pallas_call(
        functools.partial(rows_kernel, fields, modes, tiles_here, length),
        out_shape=(
            jax.ShapeDtypeStruct((fields, height, TILE), F32),
            jax.ShapeDtypeStruct((space, TILE), F32),
            jax.ShapeDtypeStruct((height, width), F32),
            jax.ShapeDtypeStruct((2, fields * fields, TILE), F32),
        ),
        scratch_shapes=[pltpu.VMEM((fields, space * 2 * modes, TILE), F32)],
        name="rows",
    )(mine, other)
    total = square
    for d in range(1, mode):
        total = total + lax.ppermute(square, "mode", [(i, (i + d) % mode) for i in range(mode)])
    factor = lax.rsqrt(total / (mode * modes * fields) + EPS)

    update = pl.pallas_call(
        update_kernel,
        out_shape=jax.ShapeDtypeStruct((fields, modes, cells), F32),
        scratch_shapes=[
            pltpu.VMEM((fields, width, TILE), F32),
            pltpu.VMEM((fields, modes, cells), F32),
            pltpu.VMEM((fields, modes, cells), F32),
        ],
        name="update",
    )(factor, matrix, rows, links, b, j)
    return jnp.transpose(update, (1, 0, 2))


def solution(mesh):
    placed = (
        P("mode", None, "space"),
        P(None, None, None, "space"),
        P("space", None),
        P("space", None),
    )
    return jax.shard_map(
        shards, mesh=mesh, in_specs=placed, out_specs=P("mode", None, "space"), check_vma=False
    )
```

```python
import functools
import jax
import jax.numpy as jnp
from jax import lax
from jax.experimental import pallas as pl
from jax.experimental.pallas import tpu as pltpu
from jax.sharding import PartitionSpec as P

TILE = 128
EPS = 1e-05
F32 = jnp.float32
BF16 = jnp.bfloat16
CORES = 2


def near(values):
    return pltpu.with_memory_space_constraint(values, pltpu.VMEM)


def over(values, by):
    return lax.shift_right_logical(values, by.bit_length() - 1) if by & (by - 1) == 0 else values // by


def modulo(values, by):
    return values & (by - 1) if by & (by - 1) == 0 else values % by


def layout(fields, modes, tiles_here):
    starts = [0]
    for rows in (fields * tiles_here * modes, fields * modes, fields * fields, 5):
        starts.append(pl.cdiv(starts[-1] + rows, 16) * 16)
    return starts


def split(values):
    high = values.astype(BF16)
    return high, (values - high.astype(F32)).astype(BF16)


def applied_kernel(list_ref, weight_ref, b_ref, j_ref, out_ref, lower, upper, applied):
    fields, modes, cells = b_ref.shape
    length = list_ref.shape[1]
    tiles_here = cells // TILE
    height = tiles_here * modes
    _, basis_at, link_at, list_at, _ = layout(fields, modes, tiles_here)
    wide = lax.broadcasted_iota(jnp.int32, (modes, cells), 1)
    half = lax.broadcasted_iota(jnp.int32, (modes, TILE), 1) < TILE // 2
    for g in range(fields):
        values = b_ref[g].astype(F32)
        below = pltpu.roll(values, 1, 1)
        above = pltpu.roll(values, cells - 1, 1)
        edge = jnp.where(half, below[:, :TILE], above[:, cells - TILE :])
        out_ref[basis_at + g * modes : basis_at + (g + 1) * modes, :] = edge.astype(BF16)
        lower[g] = jnp.where(wide == 0, 0.0, below)
        upper[g] = jnp.where(wide == cells - 1, 0.0, above)
    for t in range(tiles_here):
        at = slice(t * TILE, (t + 1) * TILE)
        center = [b_ref[g, :, at].astype(F32) for g in range(fields)]
        below = [lower[g, :, at] for g in range(fields)]
        above = [upper[g, :, at] for g in range(fields)]
        for f in range(fields):
            total = jnp.zeros((modes, TILE), F32)
            for g in range(fields):
                link = j_ref[f, g, :, at].astype(F32)
                total = total + link[0:1] * center[g]
                total = total + link[1:2] * below[g]
                total = total + link[2:3] * above[g]
            applied[f * height + t * modes : f * height + (t + 1) * modes, :] = total
    out_ref[0 : fields * height, :] = applied[...].astype(BF16)
    half = half[0:1]
    rows = []
    for f in range(fields):
        for g in range(fields):
            head = j_ref[f, g, :, 0:TILE].astype(F32)[1:2]
            tail = j_ref[f, g, :, cells - TILE :].astype(F32)[2:3]
            rows.append(jnp.where(half, head, tail))
    out_ref[link_at : link_at + fields * fields, :] = jnp.concatenate(rows, axis=0).astype(BF16)
    tiles = list_ref[...]
    device = over(tiles, tiles_here)
    high, low = split(weight_ref[...])
    rest = weight_ref[...] - high.astype(F32) - low.astype(F32)
    rows = [device.astype(F32), (tiles - device * tiles_here).astype(F32), high.astype(F32), low.astype(F32), rest]
    out_ref[list_at:, :] = jnp.zeros((out_ref.shape[0] - list_at, TILE), BF16)
    out_ref[list_at : list_at + 5, 0:length] = jnp.concatenate(rows, axis=0).astype(BF16)


def weight_rows(lists, weights, tile, modes, length):
    owners = lists.shape[0]
    width = tile.shape[1]
    total = jnp.zeros((owners, width), F32)
    for entry in range(length):
        total = total + jnp.where(lists[:, entry : entry + 1] == tile, weights[:, entry : entry + 1], 0.0)
    lane = lax.broadcasted_iota(jnp.int32, (modes, width), 1)
    sub = lax.broadcasted_iota(jnp.int32, (modes, width), 0)
    same = modulo(lane, modes) == sub
    return jnp.concatenate([jnp.where(same, total[o : o + 1], 0.0) for o in range(owners)], axis=0)


def rows_kernel(fields, modes, tiles_here, length, mine, other, rows_ref, square_ref, w_ref, link_ref, extra):
    chips = mine.shape[0]
    devices = chips * CORES
    height = tiles_here * modes
    _, basis_at, link_at, list_at, _ = layout(fields, modes, tiles_here)
    me = lax.axis_index("space")
    core = lax.rem(me, CORES)
    chip = lax.div(me, CORES)
    lane = lax.broadcasted_iota(jnp.int32, (modes, TILE), 1)
    sources = [(mine, other, q, core) for q in range(chips)] + [(other, mine, q, 1 - core) for q in range(chips)]

    lists, weights = [], []
    for ref, _, q, _ in sources:
        part = ref[q, list_at : list_at + 5, :].astype(F32)
        lists.append(part[0:1] * tiles_here + part[1:2])
        weights.append(part[2:3] + part[3:4] + part[4:5])
    lists = jnp.concatenate(lists, axis=0)
    weights = jnp.concatenate(weights, axis=0)

    def device_of(source):
        first = source < chips
        return CORES * jnp.where(first, source, source - chips) + jnp.where(first, core, 1 - core)

    inner = devices * height
    total = inner + devices * 2 * modes
    column = lax.broadcasted_iota(jnp.int32, (devices, total), 1)
    outer = column - inner
    tile = jnp.where(
        outer < 0,
        device_of(over(column, height)) * tiles_here + modulo(over(column, modes), tiles_here),
        device_of(over(outer, 2 * modes)) * tiles_here + modulo(over(outer, modes), 2) * (tiles_here - 1),
    )
    matrix = weight_rows(lists, weights, tile.astype(F32), modes, length)
    high, low = split(matrix)

    for index, (ref, opposite, q, kind) in enumerate(sources):
        place = CORES * q + kind
        before = opposite[jnp.maximum(q - 1 + kind, 0), basis_at : basis_at + fields * modes, :].astype(F32)
        after = opposite[jnp.minimum(q + kind, chips - 1), basis_at : basis_at + fields * modes, :].astype(F32)
        before = before * (place > 0).astype(F32)
        after = after * (place < devices - 1).astype(F32)
        links = ref[q, link_at : link_at + fields * fields, :].astype(F32)
        left = lane < TILE // 2
        near = [
            jnp.where(left, before[g * modes : (g + 1) * modes], after[g * modes : (g + 1) * modes])
            for g in range(fields)
        ]
        for f in range(fields):
            halo = jnp.zeros((modes, TILE), F32)
            for g in range(fields):
                halo = halo + links[f * fields + g : f * fields + g + 1] * near[g]
            at = index * 2 * modes
            extra[f, at : at + modes, :] = jnp.where(lane == 0, halo, 0.0)
            extra[f, at + modes : at + 2 * modes, :] = jnp.where(lane == TILE - 1, halo, 0.0)

    squares = jnp.zeros((devices * modes, TILE), F32)
    for f in range(fields):
        tiles = jnp.concatenate(
            [ref[q, f * height : (f + 1) * height, :] for ref, _, q, _ in sources] + [extra[f].astype(BF16)], axis=0
        )
        rows = jnp.dot(high, tiles, preferred_element_type=F32) + jnp.dot(low, tiles, preferred_element_type=F32)
        rows_ref[f] = rows
        squares = squares + rows * rows
    for o in range(devices):
        square_ref[o : o + 1, :] = jnp.sum(squares[o * modes : (o + 1) * modes], axis=0, keepdims=True)

    column = lax.broadcasted_iota(jnp.int32, (devices, w_ref.shape[1]), 1)
    local = over(column, modes)
    base = me * tiles_here
    tile = jnp.where(local <= tiles_here, base + local, jnp.where(local == tiles_here + 1, base - 1, -2))
    w_ref[...] = weight_rows(lists, weights, tile.astype(F32), modes, length)
    link_ref[0] = other[jnp.minimum(chip + core, chips - 1), link_at : link_at + fields * fields, :].astype(F32)
    link_ref[1] = other[jnp.maximum(chip - 1 + core, 0), link_at : link_at + fields * fields, :].astype(F32)


def update_kernel(samples, w_ref, rows_ref, link_ref, b_ref, j_ref, *rest):
    square_refs = rest[:-4]
    out_ref, returned, lower, upper = rest[-4:]
    fields, modes, cells = b_ref.shape
    tiles_here = cells // TILE
    owners = square_refs[0].shape[0]
    square = square_refs[0][...]
    for ref in square_refs[1:]:
        square = square + ref[...]
    factor = lax.rsqrt(square / samples + EPS)
    factor = jnp.concatenate([jnp.broadcast_to(factor[o : o + 1], (modes, TILE)) for o in range(owners)], axis=0)
    high, low = split(jnp.transpose(w_ref[...]))
    for g in range(fields):
        normalized = (rows_ref[g] * factor).astype(BF16)
        returned[g] = jnp.dot(high, normalized, preferred_element_type=F32) + jnp.dot(
            low, normalized, preferred_element_type=F32
        )
    for t in range(tiles_here):
        at = slice(t * TILE, (t + 1) * TILE)
        values = [returned[g, t * modes : (t + 1) * modes, :] for g in range(fields)]
        for f in range(fields):
            center = b_ref[f, :, at].astype(F32)
            below = jnp.zeros((modes, TILE), F32)
            above = jnp.zeros((modes, TILE), F32)
            for g in range(fields):
                link = j_ref[g, f, :, at].astype(F32)
                center = center + link[0:1] * values[g]
                below = below + link[1:2] * values[g]
                above = above + link[2:3] * values[g]
            out_ref[f, :, at] = center
            lower[f, :, at] = below
            upper[f, :, at] = above
    wide = lax.broadcasted_iota(jnp.int32, (modes, cells), 1)
    nexts = slice(tiles_here * modes, (tiles_here + 1) * modes)
    lasts = slice((tiles_here + 1) * modes, (tiles_here + 2) * modes)
    for f in range(fields):
        head = jnp.zeros((modes, TILE), F32)
        tail = jnp.zeros((modes, TILE), F32)
        for g in range(fields):
            at = slice(g * fields + f, g * fields + f + 1)
            head = head + link_ref[0, at, :] * returned[g, nexts, :]
            tail = tail + link_ref[1, at, :] * returned[g, lasts, :]
        below = jnp.where(wide == cells - 1, head[:, 0:1], pltpu.roll(lower[f], cells - 1, 1))
        above = jnp.where(wide == 0, tail[:, TILE - 1 : TILE], pltpu.roll(upper[f], 1, 1))
        out_ref[f] = out_ref[f] + below + above


def shards(basis, jacobian, sample_list, sample_weight):
    space = lax.axis_size("space")
    mode = lax.axis_size("mode")
    modes, fields, cells = basis.shape
    length = sample_list.shape[1]
    tiles_here = cells // TILE
    height = space * modes
    width = pl.cdiv((tiles_here + 2) * modes, TILE) * TILE
    sent_rows = layout(fields, modes, tiles_here)[-1]
    b = jnp.transpose(basis, (1, 0, 2))
    j = jnp.transpose(jacobian, (1, 2, 0, 3))

    sent = pl.pallas_call(
        applied_kernel,
        out_shape=pltpu.VMEM((sent_rows, TILE), BF16),
        scratch_shapes=[
            pltpu.VMEM((fields, modes, cells), F32),
            pltpu.VMEM((fields, modes, cells), F32),
            pltpu.VMEM((fields * tiles_here * modes, TILE), F32),
        ],
        name="applied",
    )(sample_list, sample_weight, b, j)
    chips = [[core + CORES * q for q in range(space // CORES)] for core in range(CORES)]
    mine = lax.all_gather(sent, "space", axis=0, axis_index_groups=chips)
    other = lax.ppermute(mine, "space", [(i, i ^ 1) for i in range(space)])

    rows, square, matrix, links = pl.pallas_call(
        functools.partial(rows_kernel, fields, modes, tiles_here, length),
        out_shape=(
            pltpu.VMEM((fields, height, TILE), F32),
            pltpu.VMEM((space, TILE), F32),
            pltpu.VMEM((height, width), F32),
            pltpu.VMEM((2, fields * fields, TILE), F32),
        ),
        scratch_shapes=[pltpu.VMEM((fields, space * 2 * modes, TILE), F32)],
        name="rows",
    )(near(mine), near(other))
    squares = [square] + [
        lax.ppermute(square, "mode", [(i, (i + d) % mode) for i in range(mode)]) for d in range(1, mode)
    ]

    update = pl.pallas_call(
        functools.partial(update_kernel, mode * modes * fields),
        out_shape=jax.ShapeDtypeStruct((fields, modes, cells), F32),
        scratch_shapes=[
            pltpu.VMEM((fields, width, TILE), F32),
            pltpu.VMEM((fields, modes, cells), F32),
            pltpu.VMEM((fields, modes, cells), F32),
        ],
        name="update",
    )(*(near(x) for x in (matrix, rows, links, b, j, *squares)))
    return jnp.transpose(update, (1, 0, 2))


def solution(mesh):
    placed = (
        P("mode", None, "space"),
        P(None, None, None, "space"),
        P("space", None),
        P("space", None),
    )
    return jax.shard_map(
        shards, mesh=mesh, in_specs=placed, out_specs=P("mode", None, "space"), check_vma=False
    )
```

```python
import functools
import jax
import jax.numpy as jnp
from jax import lax
from jax.experimental import pallas as pl
from jax.experimental.pallas import tpu as pltpu
from jax.sharding import PartitionSpec as P

TILE = 128
EPS = 1e-05
F32 = jnp.float32
BF16 = jnp.bfloat16
CORES = 2
LIST_AT = 32


def near(values):
    return pltpu.with_memory_space_constraint(values, pltpu.VMEM)


def over(values, by):
    return lax.shift_right_logical(values, by.bit_length() - 1) if by & (by - 1) == 0 else values // by


def modulo(values, by):
    return values & (by - 1) if by & (by - 1) == 0 else values % by


def layout(fields, modes, tiles_here):
    extra_at = fields * tiles_here * modes
    extra = max(fields * modes, fields * fields + 5)
    return extra_at, extra, pl.cdiv(extra_at + extra, 8) * 8


def split(values):
    high = values.astype(BF16)
    return high, (values - high.astype(F32)).astype(BF16)


def applied_kernel(list_ref, weight_ref, b_ref, j_ref, out_ref, lower, upper, applied, shared):
    fields, modes, cells = b_ref.shape
    length = list_ref.shape[1]
    tiles_here = cells // TILE
    height = tiles_here * modes
    extra_at, extra, total_rows = layout(fields, modes, tiles_here)
    wide = lax.broadcasted_iota(jnp.int32, (modes, cells), 1)
    half = lax.broadcasted_iota(jnp.int32, (modes, TILE), 1) < TILE // 2
    shared[...] = jnp.zeros(shared.shape, F32)
    for g in range(fields):
        values = b_ref[g].astype(F32)
        below = pltpu.roll(values, 1, 1)
        above = pltpu.roll(values, cells - 1, 1)
        edge = jnp.where(half, below[:, :TILE], above[:, cells - TILE :])
        shared[g * modes : (g + 1) * modes, :] = edge
        lower[g] = jnp.where(wide == 0, 0.0, below)
        upper[g] = jnp.where(wide == cells - 1, 0.0, above)
    for t in range(tiles_here):
        at = slice(t * TILE, (t + 1) * TILE)
        center = [b_ref[g, :, at].astype(F32) for g in range(fields)]
        below = [lower[g, :, at] for g in range(fields)]
        above = [upper[g, :, at] for g in range(fields)]
        for f in range(fields):
            total = jnp.zeros((modes, TILE), F32)
            for g in range(fields):
                link = j_ref[f, g, :, at].astype(F32)
                total = total + link[0:1] * center[g]
                total = total + link[1:2] * below[g]
                total = total + link[2:3] * above[g]
            applied[f * height + t * modes : f * height + (t + 1) * modes, :] = total
    out_ref[0 : fields * height, :] = applied[...].astype(BF16)
    half = half[0:1]
    rows = []
    for f in range(fields):
        for g in range(fields):
            head = j_ref[f, g, :, 0:TILE].astype(F32)[1:2]
            tail = j_ref[f, g, :, cells - TILE :].astype(F32)[2:3]
            rows.append(jnp.where(half, pltpu.roll(head, 1, 1), pltpu.roll(tail, TILE - 1, 1)))
    links = fields * fields
    lane = lax.broadcasted_iota(jnp.int32, shared.shape, 1)
    keep = jnp.where((lane == 0) | (lane == TILE - 1), shared[...], 0.0)
    shared[...] = keep
    lane = lane[0:links]
    beside = (lane == 1) | (lane == TILE - 2)
    shared[0:links, :] = jnp.where(beside, jnp.concatenate(rows, axis=0), keep[0:links])
    tiles = list_ref[...]
    device = over(tiles, tiles_here)
    high, low = split(weight_ref[...])
    rest = weight_ref[...] - high.astype(F32) - low.astype(F32)
    rows = [device.astype(F32), (tiles - device * tiles_here).astype(F32), high.astype(F32), low.astype(F32), rest]
    shared[links : links + 5, LIST_AT : LIST_AT + length] = jnp.concatenate(rows, axis=0)
    out_ref[extra_at:total_rows, :] = shared[...].astype(BF16)


def weight_rows(lists, weights, tile, modes, length):
    owners = lists.shape[0]
    width = tile.shape[1]
    total = jnp.zeros((owners, width), F32)
    for entry in range(length):
        total = total + jnp.where(lists[:, entry : entry + 1] == tile, weights[:, entry : entry + 1], 0.0)
    lane = lax.broadcasted_iota(jnp.int32, (modes, width), 1)
    sub = lax.broadcasted_iota(jnp.int32, (modes, width), 0)
    same = modulo(lane, modes) == sub
    return jnp.concatenate([jnp.where(same, total[o : o + 1], 0.0) for o in range(owners)], axis=0)


def rows_kernel(fields, modes, tiles_here, length, mine, other, rows_ref, square_ref, w_ref, link_ref, extra):
    chips = mine.shape[0]
    devices = chips * CORES
    height = tiles_here * modes
    extra_at, _, _ = layout(fields, modes, tiles_here)
    link_rows = slice(extra_at, extra_at + fields * fields)
    basis_rows = slice(extra_at, extra_at + fields * modes)
    list_rows = slice(extra_at + fields * fields, extra_at + fields * fields + 5)
    me = lax.axis_index("space")
    core = lax.rem(me, CORES)
    chip = lax.div(me, CORES)
    lane = lax.broadcasted_iota(jnp.int32, (modes, TILE), 1)
    sources = [(mine, other, q, core) for q in range(chips)] + [(other, mine, q, 1 - core) for q in range(chips)]

    lists, weights = [], []
    for ref, _, q, _ in sources:
        part = pltpu.roll(ref[q, list_rows, :].astype(F32), TILE - LIST_AT, 1)
        lists.append(part[0:1] * tiles_here + part[1:2])
        weights.append(part[2:3] + part[3:4] + part[4:5])
    lists = jnp.concatenate(lists, axis=0)
    weights = jnp.concatenate(weights, axis=0)

    def coupling(ref, q):
        values = ref[q, link_rows, :].astype(F32)
        first = lax.broadcasted_iota(jnp.int32, values.shape, 1) < TILE // 2
        return jnp.where(first, pltpu.roll(values, TILE - 1, 1), pltpu.roll(values, 1, 1))

    def device_of(source):
        first = source < chips
        return CORES * jnp.where(first, source, source - chips) + jnp.where(first, core, 1 - core)

    inner = devices * height
    total = inner + devices * 2 * modes
    column = lax.broadcasted_iota(jnp.int32, (devices, total), 1)
    outer = column - inner
    tile = jnp.where(
        outer < 0,
        device_of(over(column, height)) * tiles_here + modulo(over(column, modes), tiles_here),
        device_of(over(outer, 2 * modes)) * tiles_here + modulo(over(outer, modes), 2) * (tiles_here - 1),
    )
    matrix = weight_rows(lists, weights, tile.astype(F32), modes, length)
    high, low = split(matrix)

    for index, (ref, opposite, q, kind) in enumerate(sources):
        place = CORES * q + kind
        before = opposite[jnp.maximum(q - 1 + kind, 0), basis_rows, :].astype(F32)
        after = opposite[jnp.minimum(q + kind, chips - 1), basis_rows, :].astype(F32)
        before = before * (place > 0).astype(F32)
        after = after * (place < devices - 1).astype(F32)
        links = coupling(ref, q)
        left = lane < TILE // 2
        near = [
            jnp.where(left, before[g * modes : (g + 1) * modes], after[g * modes : (g + 1) * modes])
            for g in range(fields)
        ]
        for f in range(fields):
            halo = jnp.zeros((modes, TILE), F32)
            for g in range(fields):
                halo = halo + links[f * fields + g : f * fields + g + 1] * near[g]
            at = index * 2 * modes
            extra[f, at : at + modes, :] = jnp.where(lane == 0, halo, 0.0)
            extra[f, at + modes : at + 2 * modes, :] = jnp.where(lane == TILE - 1, halo, 0.0)

    squares = jnp.zeros((devices * modes, TILE), F32)
    for f in range(fields):
        tiles = jnp.concatenate(
            [ref[q, f * height : (f + 1) * height, :] for ref, _, q, _ in sources] + [extra[f].astype(BF16)], axis=0
        )
        rows = jnp.dot(high, tiles, preferred_element_type=F32) + jnp.dot(low, tiles, preferred_element_type=F32)
        rows_ref[f] = rows
        squares = squares + rows * rows
    for o in range(devices):
        square_ref[o : o + 1, :] = jnp.sum(squares[o * modes : (o + 1) * modes], axis=0, keepdims=True)

    column = lax.broadcasted_iota(jnp.int32, (devices, w_ref.shape[1]), 1)
    local = over(column, modes)
    base = me * tiles_here
    tile = jnp.where(local <= tiles_here, base + local, jnp.where(local == tiles_here + 1, base - 1, -2))
    w_ref[...] = weight_rows(lists, weights, tile.astype(F32), modes, length)
    link_ref[0] = coupling(other, jnp.minimum(chip + core, chips - 1))
    link_ref[1] = coupling(other, jnp.maximum(chip - 1 + core, 0))


def update_kernel(samples, w_ref, rows_ref, link_ref, b_ref, j_ref, *rest):
    square_refs = rest[:-4]
    out_ref, returned, lower, upper = rest[-4:]
    fields, modes, cells = b_ref.shape
    tiles_here = cells // TILE
    owners = square_refs[0].shape[0]
    square = square_refs[0][...]
    for ref in square_refs[1:]:
        square = square + ref[...]
    factor = lax.rsqrt(square / samples + EPS)
    factor = jnp.concatenate([jnp.broadcast_to(factor[o : o + 1], (modes, TILE)) for o in range(owners)], axis=0)
    high, low = split(jnp.transpose(w_ref[...]))
    for g in range(fields):
        normalized = (rows_ref[g] * factor).astype(BF16)
        returned[g] = jnp.dot(high, normalized, preferred_element_type=F32) + jnp.dot(
            low, normalized, preferred_element_type=F32
        )
    for t in range(tiles_here):
        at = slice(t * TILE, (t + 1) * TILE)
        values = [returned[g, t * modes : (t + 1) * modes, :] for g in range(fields)]
        for f in range(fields):
            center = b_ref[f, :, at].astype(F32)
            below = jnp.zeros((modes, TILE), F32)
            above = jnp.zeros((modes, TILE), F32)
            for g in range(fields):
                link = j_ref[g, f, :, at].astype(F32)
                center = center + link[0:1] * values[g]
                below = below + link[1:2] * values[g]
                above = above + link[2:3] * values[g]
            out_ref[f, :, at] = center
            lower[f, :, at] = below
            upper[f, :, at] = above
    wide = lax.broadcasted_iota(jnp.int32, (modes, cells), 1)
    nexts = slice(tiles_here * modes, (tiles_here + 1) * modes)
    lasts = slice((tiles_here + 1) * modes, (tiles_here + 2) * modes)
    for f in range(fields):
        head = jnp.zeros((modes, TILE), F32)
        tail = jnp.zeros((modes, TILE), F32)
        for g in range(fields):
            at = slice(g * fields + f, g * fields + f + 1)
            head = head + link_ref[0, at, :] * returned[g, nexts, :]
            tail = tail + link_ref[1, at, :] * returned[g, lasts, :]
        below = jnp.where(wide == cells - 1, head[:, 0:1], pltpu.roll(lower[f], cells - 1, 1))
        above = jnp.where(wide == 0, tail[:, TILE - 1 : TILE], pltpu.roll(upper[f], 1, 1))
        out_ref[f] = out_ref[f] + below + above


def shards(basis, jacobian, sample_list, sample_weight):
    space = lax.axis_size("space")
    mode = lax.axis_size("mode")
    modes, fields, cells = basis.shape
    length = sample_list.shape[1]
    tiles_here = cells // TILE
    height = space * modes
    width = pl.cdiv((tiles_here + 2) * modes, TILE) * TILE
    sent_rows = layout(fields, modes, tiles_here)[-1]
    b = jnp.transpose(basis, (1, 0, 2))
    j = jnp.transpose(jacobian, (1, 2, 0, 3))

    sent = pl.pallas_call(
        applied_kernel,
        out_shape=pltpu.VMEM((sent_rows, TILE), BF16),
        scratch_shapes=[
            pltpu.VMEM((fields, modes, cells), F32),
            pltpu.VMEM((fields, modes, cells), F32),
            pltpu.VMEM((fields * tiles_here * modes, TILE), F32),
            pltpu.VMEM((sent_rows - fields * tiles_here * modes, TILE), F32),
        ],
        name="applied",
    )(sample_list, sample_weight, b, j)
    chips = [[core + CORES * q for q in range(space // CORES)] for core in range(CORES)]
    mine = lax.all_gather(sent, "space", axis=0, axis_index_groups=chips)
    other = lax.ppermute(mine, "space", [(i, i ^ 1) for i in range(space)])

    rows, square, matrix, links = pl.pallas_call(
        functools.partial(rows_kernel, fields, modes, tiles_here, length),
        out_shape=(
            pltpu.VMEM((fields, height, TILE), F32),
            pltpu.VMEM((space, TILE), F32),
            pltpu.VMEM((height, width), F32),
            pltpu.VMEM((2, fields * fields, TILE), F32),
        ),
        scratch_shapes=[pltpu.VMEM((fields, space * 2 * modes, TILE), F32)],
        name="rows",
    )(near(mine), near(other))
    even = mode & (mode - 1) == 0
    squares = [square] + [
        lax.ppermute(square, "mode", [(i, i ^ d if even else (i + d) % mode) for i in range(mode)])
        for d in range(1, mode)
    ]

    update = pl.pallas_call(
        functools.partial(update_kernel, mode * modes * fields),
        out_shape=jax.ShapeDtypeStruct((fields, modes, cells), F32),
        scratch_shapes=[
            pltpu.VMEM((fields, width, TILE), F32),
            pltpu.VMEM((fields, modes, cells), F32),
            pltpu.VMEM((fields, modes, cells), F32),
        ],
        name="update",
    )(*(near(x) for x in (matrix, rows, links, b, j, *squares)))
    return jnp.transpose(update, (1, 0, 2))


def solution(mesh):
    placed = (
        P("mode", None, "space"),
        P(None, None, None, "space"),
        P("space", None),
        P("space", None),
    )
    return jax.shard_map(
        shards, mesh=mesh, in_specs=placed, out_specs=P("mode", None, "space"), check_vma=False
    )
```

```python
import functools
import jax
import jax.numpy as jnp
from jax import lax
from jax.experimental import pallas as pl
from jax.experimental.pallas import tpu as pltpu
from jax.sharding import PartitionSpec as P

TILE = 128
EPS = 1e-05
F32 = jnp.float32
BF16 = jnp.bfloat16
CORES = 2
PAIRED = 4
LIST_AT = 32


def near(values):
    return pltpu.with_memory_space_constraint(values, pltpu.VMEM)


def over(values, by):
    return lax.shift_right_logical(values, by.bit_length() - 1) if by & (by - 1) == 0 else values // by


def modulo(values, by):
    return values & (by - 1) if by & (by - 1) == 0 else values % by


def layout(fields, modes, tiles_here):
    extra_at = fields * tiles_here * modes
    extra = max(fields * modes, fields * fields + 5)
    return extra_at, extra, pl.cdiv(extra_at + extra, 8) * 8


def split(values):
    high = values.astype(BF16)
    return high, (values - high.astype(F32)).astype(BF16)


def applied_kernel(list_ref, weight_ref, b_ref, j_ref, out_ref, lower, upper, applied, shared):
    fields, modes, cells = b_ref.shape
    length = list_ref.shape[1]
    tiles_here = cells // TILE
    height = tiles_here * modes
    extra_at, extra, total_rows = layout(fields, modes, tiles_here)
    wide = lax.broadcasted_iota(jnp.int32, (modes, cells), 1)
    half = lax.broadcasted_iota(jnp.int32, (modes, TILE), 1) < TILE // 2
    shared[...] = jnp.zeros(shared.shape, F32)
    for g in range(fields):
        values = b_ref[g].astype(F32)
        below = pltpu.roll(values, 1, 1)
        above = pltpu.roll(values, cells - 1, 1)
        edge = jnp.where(half, below[:, :TILE], above[:, cells - TILE :])
        shared[g * modes : (g + 1) * modes, :] = edge
        lower[g] = jnp.where(wide == 0, 0.0, below)
        upper[g] = jnp.where(wide == cells - 1, 0.0, above)
    for t in range(tiles_here):
        at = slice(t * TILE, (t + 1) * TILE)
        center = [b_ref[g, :, at].astype(F32) for g in range(fields)]
        below = [lower[g, :, at] for g in range(fields)]
        above = [upper[g, :, at] for g in range(fields)]
        for f in range(fields):
            total = jnp.zeros((modes, TILE), F32)
            for g in range(fields):
                link = j_ref[f, g, :, at].astype(F32)
                total = total + link[0:1] * center[g]
                total = total + link[1:2] * below[g]
                total = total + link[2:3] * above[g]
            applied[f * height + t * modes : f * height + (t + 1) * modes, :] = total
    out_ref[0 : fields * height, :] = applied[...].astype(BF16)
    half = half[0:1]
    rows = []
    for f in range(fields):
        for g in range(fields):
            head = j_ref[f, g, :, 0:TILE].astype(F32)[1:2]
            tail = j_ref[f, g, :, cells - TILE :].astype(F32)[2:3]
            rows.append(jnp.where(half, pltpu.roll(head, 1, 1), pltpu.roll(tail, TILE - 1, 1)))
    links = fields * fields
    lane = lax.broadcasted_iota(jnp.int32, shared.shape, 1)
    keep = jnp.where((lane == 0) | (lane == TILE - 1), shared[...], 0.0)
    shared[...] = keep
    lane = lane[0:links]
    beside = (lane == 1) | (lane == TILE - 2)
    shared[0:links, :] = jnp.where(beside, jnp.concatenate(rows, axis=0), keep[0:links])
    tiles = list_ref[...]
    device = over(tiles, tiles_here)
    high, low = split(weight_ref[...])
    rest = weight_ref[...] - high.astype(F32) - low.astype(F32)
    rows = [device.astype(F32), (tiles - device * tiles_here).astype(F32), high.astype(F32), low.astype(F32), rest]
    shared[links : links + 5, LIST_AT : LIST_AT + length] = jnp.concatenate(rows, axis=0)
    out_ref[extra_at:total_rows, :] = shared[...].astype(BF16)


def weight_rows(lists, weights, tile, modes, length):
    owners = lists.shape[0]
    width = tile.shape[1]
    total = jnp.zeros((owners, width), F32)
    for entry in range(length):
        total = total + jnp.where(lists[:, entry : entry + 1] == tile, weights[:, entry : entry + 1], 0.0)
    lane = lax.broadcasted_iota(jnp.int32, (modes, width), 1)
    sub = lax.broadcasted_iota(jnp.int32, (modes, width), 0)
    same = modulo(lane, modes) == sub
    return jnp.concatenate([jnp.where(same, total[o : o + 1], 0.0) for o in range(owners)], axis=0)


def rows_kernel(fields, modes, tiles_here, length, devices, paired, *refs):
    parts = refs[:-6]
    rows_ref, square_ref, w_ref, link_ref, extra, edges = refs[-6:]
    chips = devices // CORES
    height = tiles_here * modes
    extra_at, _, _ = layout(fields, modes, tiles_here)
    edge_rows = slice(extra_at, extra_at + edges.shape[2])
    list_rows = slice(extra_at + fields * fields, extra_at + fields * fields + 5)
    me = lax.axis_index("space")
    core = lax.rem(me, CORES)
    chip = lax.div(me, CORES)
    lane = lax.broadcasted_iota(jnp.int32, (modes, TILE), 1)
    kinds = (core, 1 - core)
    sources = []
    for which, kind in enumerate(kinds):
        for q in range(chips):
            if paired:
                sources.append((parts[which * chips + q].at[...], jnp.bitwise_xor(chip, q), which))
            else:
                sources.append((parts[which].at[q], q, which))

    lists, weights = [], []
    for ref, place, which in sources:
        part = pltpu.roll(ref[list_rows, :].astype(F32), TILE - LIST_AT, 1)
        lists.append(part[0:1] * tiles_here + part[1:2])
        weights.append(part[2:3] + part[3:4] + part[4:5])
        edges[which, place] = ref[edge_rows, :].astype(F32)
    lists = jnp.concatenate(lists, axis=0)
    weights = jnp.concatenate(weights, axis=0)

    def coupling(which, place):
        values = edges[which, place, 0 : fields * fields, :]
        first = lax.broadcasted_iota(jnp.int32, values.shape, 1) < TILE // 2
        return jnp.where(first, pltpu.roll(values, TILE - 1, 1), pltpu.roll(values, 1, 1))

    def device_of(source, mixed):
        first = source < chips
        place = jnp.where(first, source, source - chips)
        if mixed:
            place = jnp.bitwise_xor(place, chip)
        return CORES * place + jnp.where(first, core, 1 - core)

    inner = devices * height
    total = inner + devices * 2 * modes
    column = lax.broadcasted_iota(jnp.int32, (devices, total), 1)
    outer = column - inner
    tile = jnp.where(
        outer < 0,
        device_of(over(column, height), paired) * tiles_here + modulo(over(column, modes), tiles_here),
        device_of(over(outer, 2 * modes), False) * tiles_here + modulo(over(outer, modes), 2) * (tiles_here - 1),
    )
    matrix = weight_rows(lists, weights, tile.astype(F32), modes, length)
    high, low = split(matrix)

    for index in range(devices):
        which, q = divmod(index, chips)
        kind = kinds[which]
        place = CORES * q + kind
        before = edges[1 - which, jnp.maximum(q - 1 + kind, 0), 0 : fields * modes, :]
        after = edges[1 - which, jnp.minimum(q + kind, chips - 1), 0 : fields * modes, :]
        before = before * (place > 0).astype(F32)
        after = after * (place < devices - 1).astype(F32)
        links = coupling(which, q)
        left = lane < TILE // 2
        near = [
            jnp.where(left, before[g * modes : (g + 1) * modes], after[g * modes : (g + 1) * modes])
            for g in range(fields)
        ]
        for f in range(fields):
            halo = jnp.zeros((modes, TILE), F32)
            for g in range(fields):
                halo = halo + links[f * fields + g : f * fields + g + 1] * near[g]
            at = index * 2 * modes
            extra[f, at : at + modes, :] = jnp.where(lane == 0, halo, 0.0)
            extra[f, at + modes : at + 2 * modes, :] = jnp.where(lane == TILE - 1, halo, 0.0)

    squares = jnp.zeros((devices * modes, TILE), F32)
    for f in range(fields):
        tiles = jnp.concatenate(
            [ref[f * height : (f + 1) * height, :] for ref, _, _ in sources] + [extra[f].astype(BF16)], axis=0
        )
        rows = jnp.dot(high, tiles, preferred_element_type=F32) + jnp.dot(low, tiles, preferred_element_type=F32)
        rows_ref[f] = rows
        squares = squares + rows * rows
    for o in range(devices):
        square_ref[o : o + 1, :] = jnp.sum(squares[o * modes : (o + 1) * modes], axis=0, keepdims=True)

    column = lax.broadcasted_iota(jnp.int32, (devices, w_ref.shape[1]), 1)
    local = over(column, modes)
    base = me * tiles_here
    tile = jnp.where(local <= tiles_here, base + local, jnp.where(local == tiles_here + 1, base - 1, -2))
    w_ref[...] = weight_rows(lists, weights, tile.astype(F32), modes, length)
    link_ref[0] = coupling(1, jnp.minimum(chip + core, chips - 1))
    link_ref[1] = coupling(1, jnp.maximum(chip - 1 + core, 0))


def update_kernel(samples, w_ref, rows_ref, link_ref, b_ref, j_ref, *rest):
    square_refs = rest[:-4]
    out_ref, returned, lower, upper = rest[-4:]
    fields, modes, cells = b_ref.shape
    tiles_here = cells // TILE
    owners = square_refs[0].shape[0]
    square = square_refs[0][...]
    for ref in square_refs[1:]:
        square = square + ref[...]
    factor = lax.rsqrt(square / samples + EPS)
    factor = jnp.concatenate([jnp.broadcast_to(factor[o : o + 1], (modes, TILE)) for o in range(owners)], axis=0)
    high, low = split(jnp.transpose(w_ref[...]))
    for g in range(fields):
        normalized = (rows_ref[g] * factor).astype(BF16)
        returned[g] = jnp.dot(high, normalized, preferred_element_type=F32) + jnp.dot(
            low, normalized, preferred_element_type=F32
        )
    for t in range(tiles_here):
        at = slice(t * TILE, (t + 1) * TILE)
        values = [returned[g, t * modes : (t + 1) * modes, :] for g in range(fields)]
        for f in range(fields):
            center = b_ref[f, :, at].astype(F32)
            below = jnp.zeros((modes, TILE), F32)
            above = jnp.zeros((modes, TILE), F32)
            for g in range(fields):
                link = j_ref[g, f, :, at].astype(F32)
                center = center + link[0:1] * values[g]
                below = below + link[1:2] * values[g]
                above = above + link[2:3] * values[g]
            out_ref[f, :, at] = center
            lower[f, :, at] = below
            upper[f, :, at] = above
    wide = lax.broadcasted_iota(jnp.int32, (modes, cells), 1)
    nexts = slice(tiles_here * modes, (tiles_here + 1) * modes)
    lasts = slice((tiles_here + 1) * modes, (tiles_here + 2) * modes)
    for f in range(fields):
        head = jnp.zeros((modes, TILE), F32)
        tail = jnp.zeros((modes, TILE), F32)
        for g in range(fields):
            at = slice(g * fields + f, g * fields + f + 1)
            head = head + link_ref[0, at, :] * returned[g, nexts, :]
            tail = tail + link_ref[1, at, :] * returned[g, lasts, :]
        below = jnp.where(wide == cells - 1, head[:, 0:1], pltpu.roll(lower[f], cells - 1, 1))
        above = jnp.where(wide == 0, tail[:, TILE - 1 : TILE], pltpu.roll(upper[f], 1, 1))
        out_ref[f] = out_ref[f] + below + above


def shards(basis, jacobian, sample_list, sample_weight):
    space = lax.axis_size("space")
    mode = lax.axis_size("mode")
    modes, fields, cells = basis.shape
    length = sample_list.shape[1]
    tiles_here = cells // TILE
    height = space * modes
    width = pl.cdiv((tiles_here + 2) * modes, TILE) * TILE
    sent_rows = layout(fields, modes, tiles_here)[-1]
    b = jnp.transpose(basis, (1, 0, 2))
    j = jnp.transpose(jacobian, (1, 2, 0, 3))

    sent = pl.pallas_call(
        applied_kernel,
        out_shape=pltpu.VMEM((sent_rows, TILE), BF16),
        scratch_shapes=[
            pltpu.VMEM((fields, modes, cells), F32),
            pltpu.VMEM((fields, modes, cells), F32),
            pltpu.VMEM((fields * tiles_here * modes, TILE), F32),
            pltpu.VMEM((sent_rows - fields * tiles_here * modes, TILE), F32),
        ],
        name="applied",
    )(sample_list, sample_weight, b, j)
    chips = space // CORES
    paired = chips <= PAIRED and chips & (chips - 1) == 0
    if paired:
        parts = [sent] + [
            lax.ppermute(sent, "space", [(i, i ^ (CORES * d)) for i in range(space)]) for d in range(1, chips)
        ]
    else:
        groups = [[core + CORES * q for q in range(chips)] for core in range(CORES)]
        parts = [lax.all_gather(sent, "space", axis=0, axis_index_groups=groups)]
    parts = parts + [lax.ppermute(part, "space", [(i, i ^ 1) for i in range(space)]) for part in parts]

    rows, square, matrix, links = pl.pallas_call(
        functools.partial(rows_kernel, fields, modes, tiles_here, length, space, paired),
        out_shape=(
            pltpu.VMEM((fields, height, TILE), F32),
            pltpu.VMEM((space, TILE), F32),
            pltpu.VMEM((height, width), F32),
            pltpu.VMEM((2, fields * fields, TILE), F32),
        ),
        scratch_shapes=[
            pltpu.VMEM((fields, space * 2 * modes, TILE), F32),
            pltpu.VMEM((CORES, chips, layout(fields, modes, tiles_here)[1], TILE), F32),
        ],
        name="rows",
    )(*(near(part) for part in parts))
    squares = [square]
    if mode & (mode - 1) == 0:
        step = 1
        while step < mode:
            square = sum(squares)
            squares = [square, lax.ppermute(square, "mode", [(i, i ^ step) for i in range(mode)])]
            step *= 2
    else:
        for step in range(1, mode):
            squares.append(lax.ppermute(square, "mode", [(i, (i + step) % mode) for i in range(mode)]))

    update = pl.pallas_call(
        functools.partial(update_kernel, mode * modes * fields),
        out_shape=jax.ShapeDtypeStruct((fields, modes, cells), F32),
        scratch_shapes=[
            pltpu.VMEM((fields, width, TILE), F32),
            pltpu.VMEM((fields, modes, cells), F32),
            pltpu.VMEM((fields, modes, cells), F32),
        ],
        name="update",
    )(*(near(x) for x in (matrix, rows, links, b, j, *squares)))
    return jnp.transpose(update, (1, 0, 2))


def solution(mesh):
    placed = (
        P("mode", None, "space"),
        P(None, None, None, "space"),
        P("space", None),
        P("space", None),
    )
    return jax.shard_map(
        shards, mesh=mesh, in_specs=placed, out_specs=P("mode", None, "space"), check_vma=False
    )
```

```python
import functools
import jax
import jax.numpy as jnp
from jax import lax
from jax.experimental import pallas as pl
from jax.experimental.pallas import tpu as pltpu
from jax.sharding import PartitionSpec as P

TILE = 128
EPS = 1e-05
F32 = jnp.float32
BF16 = jnp.bfloat16
CORES = 2
PAIRED = 4
LIST_AT = 32


def near(values):
    return pltpu.with_memory_space_constraint(values, pltpu.VMEM)


def over(values, by):
    return lax.shift_right_logical(values, by.bit_length() - 1) if by & (by - 1) == 0 else values // by


def modulo(values, by):
    return values & (by - 1) if by & (by - 1) == 0 else values % by


def layout(fields, modes, tiles_here):
    extra_at = fields * tiles_here * modes
    extra = max(fields * modes, fields * fields + 5)
    return extra_at, extra, pl.cdiv(extra_at + extra, 8) * 8


def split(values):
    high = values.astype(BF16)
    return high, (values - high.astype(F32)).astype(BF16)


def applied_kernel(list_ref, weight_ref, b_ref, j_ref, out_ref, lower, upper, applied, shared):
    fields, modes, cells = b_ref.shape
    length = list_ref.shape[1]
    tiles_here = cells // TILE
    height = tiles_here * modes
    extra_at, extra, total_rows = layout(fields, modes, tiles_here)
    wide = lax.broadcasted_iota(jnp.int32, (modes, cells), 1)
    half = lax.broadcasted_iota(jnp.int32, (modes, TILE), 1) < TILE // 2
    shared[...] = jnp.zeros(shared.shape, F32)
    for g in range(fields):
        values = b_ref[g].astype(F32)
        below = pltpu.roll(values, 1, 1)
        above = pltpu.roll(values, cells - 1, 1)
        edge = jnp.where(half, below[:, :TILE], above[:, cells - TILE :])
        shared[g * modes : (g + 1) * modes, :] = edge
        lower[g] = jnp.where(wide == 0, 0.0, below)
        upper[g] = jnp.where(wide == cells - 1, 0.0, above)
    for t in range(tiles_here):
        at = slice(t * TILE, (t + 1) * TILE)
        center = [b_ref[g, :, at].astype(F32) for g in range(fields)]
        below = [lower[g, :, at] for g in range(fields)]
        above = [upper[g, :, at] for g in range(fields)]
        for f in range(fields):
            total = jnp.zeros((modes, TILE), F32)
            for g in range(fields):
                link = j_ref[f, g, :, at].astype(F32)
                total = total + link[0:1] * center[g]
                total = total + link[1:2] * below[g]
                total = total + link[2:3] * above[g]
            applied[f * height + t * modes : f * height + (t + 1) * modes, :] = total
    out_ref[0 : fields * height, :] = applied[...].astype(BF16)
    half = half[0:1]
    rows = []
    for f in range(fields):
        for g in range(fields):
            head = j_ref[f, g, :, 0:TILE].astype(F32)[1:2]
            tail = j_ref[f, g, :, cells - TILE :].astype(F32)[2:3]
            rows.append(jnp.where(half, pltpu.roll(head, 1, 1), pltpu.roll(tail, TILE - 1, 1)))
    links = fields * fields
    lane = lax.broadcasted_iota(jnp.int32, shared.shape, 1)
    keep = jnp.where((lane == 0) | (lane == TILE - 1), shared[...], 0.0)
    shared[...] = keep
    lane = lane[0:links]
    beside = (lane == 1) | (lane == TILE - 2)
    shared[0:links, :] = jnp.where(beside, jnp.concatenate(rows, axis=0), keep[0:links])
    tiles = list_ref[...]
    device = over(tiles, tiles_here)
    high, low = split(weight_ref[...])
    rest = weight_ref[...] - high.astype(F32) - low.astype(F32)
    rows = [device.astype(F32), (tiles - device * tiles_here).astype(F32), high.astype(F32), low.astype(F32), rest]
    shared[links : links + 5, LIST_AT : LIST_AT + length] = jnp.concatenate(rows, axis=0)
    out_ref[extra_at:total_rows, :] = shared[...].astype(BF16)


def weight_rows(lists, weights, tile, modes, length):
    owners = lists.shape[0]
    width = tile.shape[1]
    total = jnp.zeros((owners, width), F32)
    for entry in range(length):
        total = total + jnp.where(lists[:, entry : entry + 1] == tile, weights[:, entry : entry + 1], 0.0)
    lane = lax.broadcasted_iota(jnp.int32, (modes, width), 1)
    sub = lax.broadcasted_iota(jnp.int32, (modes, width), 0)
    same = modulo(lane, modes) == sub
    return jnp.concatenate([jnp.where(same, total[o : o + 1], 0.0) for o in range(owners)], axis=0)


def rows_kernel(fields, modes, tiles_here, length, devices, paired, *refs):
    parts = refs[:-6]
    rows_ref, square_ref, w_ref, link_ref, extra, edges = refs[-6:]
    chips = devices // CORES
    height = tiles_here * modes
    extra_at, _, _ = layout(fields, modes, tiles_here)
    edge_rows = slice(extra_at, extra_at + edges.shape[2])
    list_rows = slice(extra_at + fields * fields, extra_at + fields * fields + 5)
    me = lax.axis_index("space")
    core = lax.rem(me, CORES)
    chip = lax.div(me, CORES)
    lane = lax.broadcasted_iota(jnp.int32, (modes, TILE), 1)
    kinds = (core, 1 - core)
    sources = []
    for which, kind in enumerate(kinds):
        for q in range(chips):
            if paired:
                sources.append((parts[which * chips + q].at[...], jnp.bitwise_xor(chip, q), which))
            else:
                sources.append((parts[which].at[q], q, which))

    lists, weights = [], []
    for ref, place, which in sources:
        part = pltpu.roll(ref[list_rows, :].astype(F32), TILE - LIST_AT, 1)
        lists.append(part[0:1] * tiles_here + part[1:2])
        weights.append(part[2:3] + part[3:4] + part[4:5])
        edges[which, place] = ref[edge_rows, :].astype(F32)
    lists = jnp.concatenate(lists, axis=0)
    weights = jnp.concatenate(weights, axis=0)

    def coupling(which, place):
        values = edges[which, place, 0 : fields * fields, :]
        first = lax.broadcasted_iota(jnp.int32, values.shape, 1) < TILE // 2
        return jnp.where(first, pltpu.roll(values, TILE - 1, 1), pltpu.roll(values, 1, 1))

    def device_of(source, mixed):
        first = source < chips
        place = jnp.where(first, source, source - chips)
        if mixed:
            place = jnp.bitwise_xor(place, chip)
        return CORES * place + jnp.where(first, core, 1 - core)

    inner = devices * height
    total = inner + devices * 2 * modes
    column = lax.broadcasted_iota(jnp.int32, (devices, total), 1)
    outer = column - inner
    tile = jnp.where(
        outer < 0,
        device_of(over(column, height), paired) * tiles_here + modulo(over(column, modes), tiles_here),
        device_of(over(outer, 2 * modes), False) * tiles_here + modulo(over(outer, modes), 2) * (tiles_here - 1),
    )
    matrix = weight_rows(lists, weights, tile.astype(F32), modes, length)
    high, low = split(matrix)

    for index in range(devices):
        which, q = divmod(index, chips)
        kind = kinds[which]
        place = CORES * q + kind
        before = edges[1 - which, jnp.maximum(q - 1 + kind, 0), 0 : fields * modes, :]
        after = edges[1 - which, jnp.minimum(q + kind, chips - 1), 0 : fields * modes, :]
        before = before * (place > 0).astype(F32)
        after = after * (place < devices - 1).astype(F32)
        links = coupling(which, q)
        left = lane < TILE // 2
        near = [
            jnp.where(left, before[g * modes : (g + 1) * modes], after[g * modes : (g + 1) * modes])
            for g in range(fields)
        ]
        for f in range(fields):
            halo = jnp.zeros((modes, TILE), F32)
            for g in range(fields):
                halo = halo + links[f * fields + g : f * fields + g + 1] * near[g]
            at = index * 2 * modes
            extra[f, at : at + modes, :] = jnp.where(lane == 0, halo, 0.0)
            extra[f, at + modes : at + 2 * modes, :] = jnp.where(lane == TILE - 1, halo, 0.0)

    squares = jnp.zeros((devices * modes, TILE), F32)
    for f in range(fields):
        tiles = jnp.concatenate(
            [ref[f * height : (f + 1) * height, :] for ref, _, _ in sources] + [extra[f].astype(BF16)], axis=0
        )
        rows = jnp.dot(high, tiles, preferred_element_type=F32) + jnp.dot(low, tiles, preferred_element_type=F32)
        rows_ref[f] = rows
        squares = squares + rows * rows
    for o in range(devices):
        square_ref[o : o + 1, :] = jnp.sum(squares[o * modes : (o + 1) * modes], axis=0, keepdims=True)

    column = lax.broadcasted_iota(jnp.int32, (devices, w_ref.shape[1]), 1)
    local = over(column, modes)
    base = me * tiles_here
    tile = jnp.where(local <= tiles_here, base + local, jnp.where(local == tiles_here + 1, base - 1, -2))
    w_ref[...] = weight_rows(lists, weights, tile.astype(F32), modes, length)
    link_ref[0] = coupling(1, jnp.minimum(chip + core, chips - 1))
    link_ref[1] = coupling(1, jnp.maximum(chip - 1 + core, 0))


def update_kernel(samples, w_ref, rows_ref, link_ref, b_ref, j_ref, total_ref, handed_ref, out_ref, returned, lower, upper):
    fields, modes, cells = b_ref.shape
    tiles_here = cells // TILE
    owners = total_ref.shape[0]
    carrier = lax.rem(lax.axis_index("space"), CORES) == CORES - 1
    handed = jnp.concatenate([handed_ref[owners // CORES :], handed_ref[: owners // CORES]], axis=0)
    square = jnp.where(carrier, total_ref[...], handed)
    factor = lax.rsqrt(square / samples + EPS)
    factor = jnp.concatenate([jnp.broadcast_to(factor[o : o + 1], (modes, TILE)) for o in range(owners)], axis=0)
    high, low = split(jnp.transpose(w_ref[...]))
    for g in range(fields):
        normalized = (rows_ref[g] * factor).astype(BF16)
        returned[g] = jnp.dot(high, normalized, preferred_element_type=F32) + jnp.dot(
            low, normalized, preferred_element_type=F32
        )
    for t in range(tiles_here):
        at = slice(t * TILE, (t + 1) * TILE)
        values = [returned[g, t * modes : (t + 1) * modes, :] for g in range(fields)]
        for f in range(fields):
            center = b_ref[f, :, at].astype(F32)
            below = jnp.zeros((modes, TILE), F32)
            above = jnp.zeros((modes, TILE), F32)
            for g in range(fields):
                link = j_ref[g, f, :, at].astype(F32)
                center = center + link[0:1] * values[g]
                below = below + link[1:2] * values[g]
                above = above + link[2:3] * values[g]
            out_ref[f, :, at] = center
            lower[f, :, at] = below
            upper[f, :, at] = above
    wide = lax.broadcasted_iota(jnp.int32, (modes, cells), 1)
    nexts = slice(tiles_here * modes, (tiles_here + 1) * modes)
    lasts = slice((tiles_here + 1) * modes, (tiles_here + 2) * modes)
    for f in range(fields):
        head = jnp.zeros((modes, TILE), F32)
        tail = jnp.zeros((modes, TILE), F32)
        for g in range(fields):
            at = slice(g * fields + f, g * fields + f + 1)
            head = head + link_ref[0, at, :] * returned[g, nexts, :]
            tail = tail + link_ref[1, at, :] * returned[g, lasts, :]
        below = jnp.where(wide == cells - 1, head[:, 0:1], pltpu.roll(lower[f], cells - 1, 1))
        above = jnp.where(wide == 0, tail[:, TILE - 1 : TILE], pltpu.roll(upper[f], 1, 1))
        out_ref[f] = out_ref[f] + below + above


def shards(basis, jacobian, sample_list, sample_weight):
    space = lax.axis_size("space")
    mode = lax.axis_size("mode")
    modes, fields, cells = basis.shape
    length = sample_list.shape[1]
    tiles_here = cells // TILE
    height = space * modes
    width = pl.cdiv((tiles_here + 2) * modes, TILE) * TILE
    sent_rows = layout(fields, modes, tiles_here)[-1]
    b = jnp.transpose(basis, (1, 0, 2))
    j = jnp.transpose(jacobian, (1, 2, 0, 3))

    sent = pl.pallas_call(
        applied_kernel,
        out_shape=pltpu.VMEM((sent_rows, TILE), BF16),
        scratch_shapes=[
            pltpu.VMEM((fields, modes, cells), F32),
            pltpu.VMEM((fields, modes, cells), F32),
            pltpu.VMEM((fields * tiles_here * modes, TILE), F32),
            pltpu.VMEM((sent_rows - fields * tiles_here * modes, TILE), F32),
        ],
        name="applied",
    )(sample_list, sample_weight, b, j)
    chips = space // CORES
    paired = chips <= PAIRED and chips & (chips - 1) == 0
    if paired:
        parts = [sent] + [
            lax.ppermute(sent, "space", [(i, i ^ (CORES * d)) for i in range(space)]) for d in range(1, chips)
        ]
    else:
        groups = [[core + CORES * q for q in range(chips)] for core in range(CORES)]
        parts = [lax.all_gather(sent, "space", axis=0, axis_index_groups=groups)]
    parts = parts + [lax.ppermute(part, "space", [(i, i ^ 1) for i in range(space)]) for part in parts]

    rows, square, matrix, links = pl.pallas_call(
        functools.partial(rows_kernel, fields, modes, tiles_here, length, space, paired),
        out_shape=(
            pltpu.VMEM((fields, height, TILE), F32),
            pltpu.VMEM((space, TILE), F32),
            pltpu.VMEM((height, width), F32),
            pltpu.VMEM((2, fields * fields, TILE), F32),
        ),
        scratch_shapes=[
            pltpu.VMEM((fields, space * 2 * modes, TILE), F32),
            pltpu.VMEM((CORES, chips, layout(fields, modes, tiles_here)[1], TILE), F32),
        ],
        name="rows",
    )(*(near(part) for part in parts))
    far_core = CORES - 1
    carriers = [s for s in range(space) if s % CORES == far_core]
    total = square
    for step in range(1, mode):
        total = total + lax.ppermute(
            square,
            ("space", "mode"),
            [
                (s * mode + i, s * mode + (i ^ step if mode & (mode - 1) == 0 else (i + step) % mode))
                for s in carriers
                for i in range(mode)
            ],
        )
    handed = lax.ppermute(total, "space", [(s, s - far_core) for s in carriers])

    update = pl.pallas_call(
        functools.partial(update_kernel, mode * modes * fields),
        out_shape=jax.ShapeDtypeStruct((fields, modes, cells), F32),
        scratch_shapes=[
            pltpu.VMEM((fields, width, TILE), F32),
            pltpu.VMEM((fields, modes, cells), F32),
            pltpu.VMEM((fields, modes, cells), F32),
        ],
        name="update",
    )(*(near(x) for x in (matrix, rows, links, b, j, total, handed)))
    return jnp.transpose(update, (1, 0, 2))


def solution(mesh):
    placed = (
        P("mode", None, "space"),
        P(None, None, None, "space"),
        P("space", None),
        P("space", None),
    )
    return jax.shard_map(
        shards, mesh=mesh, in_specs=placed, out_specs=P("mode", None, "space"), check_vma=False
    )
```

```python
import functools
import jax
import jax.numpy as jnp
from jax import lax
from jax.experimental import pallas as pl
from jax.experimental.pallas import tpu as pltpu
from jax.sharding import PartitionSpec as P

TILE = 128
EPS = 1e-05
F32 = jnp.float32
BF16 = jnp.bfloat16
CORES = 2
PAIRED = 4
LIST_AT = 32


def near(values):
    return pltpu.with_memory_space_constraint(values, pltpu.VMEM)


def over(values, by):
    return lax.shift_right_logical(values, by.bit_length() - 1) if by & (by - 1) == 0 else values // by


def modulo(values, by):
    return values & (by - 1) if by & (by - 1) == 0 else values % by


def layout(fields, modes, tiles_here):
    extra_at = fields * tiles_here * modes
    extra = max(fields * modes, fields * fields + 5)
    return extra_at, extra, pl.cdiv(extra_at + extra, 8) * 8


def split(values):
    high = values.astype(BF16)
    return high, (values - high.astype(F32)).astype(BF16)


def applied_kernel(list_ref, weight_ref, b_ref, j_ref, out_ref, lower, upper, applied, shared):
    fields, modes, cells = b_ref.shape
    length = list_ref.shape[1]
    tiles_here = cells // TILE
    height = tiles_here * modes
    extra_at, extra, total_rows = layout(fields, modes, tiles_here)
    wide = lax.broadcasted_iota(jnp.int32, (modes, cells), 1)
    half = lax.broadcasted_iota(jnp.int32, (modes, TILE), 1) < TILE // 2
    shared[...] = jnp.zeros(shared.shape, F32)
    for g in range(fields):
        values = b_ref[g].astype(F32)
        below = pltpu.roll(values, 1, 1)
        above = pltpu.roll(values, cells - 1, 1)
        edge = jnp.where(half, below[:, :TILE], above[:, cells - TILE :])
        shared[g * modes : (g + 1) * modes, :] = edge
        lower[g] = jnp.where(wide == 0, 0.0, below)
        upper[g] = jnp.where(wide == cells - 1, 0.0, above)
    for t in range(tiles_here):
        at = slice(t * TILE, (t + 1) * TILE)
        center = [b_ref[g, :, at].astype(F32) for g in range(fields)]
        below = [lower[g, :, at] for g in range(fields)]
        above = [upper[g, :, at] for g in range(fields)]
        for f in range(fields):
            total = jnp.zeros((modes, TILE), F32)
            for g in range(fields):
                link = j_ref[f, g, :, at].astype(F32)
                total = total + link[0:1] * center[g]
                total = total + link[1:2] * below[g]
                total = total + link[2:3] * above[g]
            applied[f * height + t * modes : f * height + (t + 1) * modes, :] = total
    out_ref[0 : fields * height, :] = applied[...].astype(BF16)
    half = half[0:1]
    rows = []
    for f in range(fields):
        for g in range(fields):
            head = j_ref[f, g, :, 0:TILE].astype(F32)[1:2]
            tail = j_ref[f, g, :, cells - TILE :].astype(F32)[2:3]
            rows.append(jnp.where(half, pltpu.roll(head, 1, 1), pltpu.roll(tail, TILE - 1, 1)))
    links = fields * fields
    lane = lax.broadcasted_iota(jnp.int32, shared.shape, 1)
    keep = jnp.where((lane == 0) | (lane == TILE - 1), shared[...], 0.0)
    shared[...] = keep
    lane = lane[0:links]
    beside = (lane == 1) | (lane == TILE - 2)
    shared[0:links, :] = jnp.where(beside, jnp.concatenate(rows, axis=0), keep[0:links])
    tiles = list_ref[...]
    device = over(tiles, tiles_here)
    high, low = split(weight_ref[...])
    rest = weight_ref[...] - high.astype(F32) - low.astype(F32)
    rows = [device.astype(F32), (tiles - device * tiles_here).astype(F32), high.astype(F32), low.astype(F32), rest]
    shared[links : links + 5, LIST_AT : LIST_AT + length] = jnp.concatenate(rows, axis=0)
    out_ref[extra_at:total_rows, :] = shared[...].astype(BF16)


def weight_rows(lists, weights, tile, modes, length):
    owners = lists.shape[0]
    width = tile.shape[1]
    total = jnp.zeros((owners, width), F32)
    for entry in range(length):
        total = total + jnp.where(lists[:, entry : entry + 1] == tile, weights[:, entry : entry + 1], 0.0)
    lane = lax.broadcasted_iota(jnp.int32, (modes, width), 1)
    sub = lax.broadcasted_iota(jnp.int32, (modes, width), 0)
    same = modulo(lane, modes) == sub
    return jnp.concatenate([jnp.where(same, total[o : o + 1], 0.0) for o in range(owners)], axis=0)


def rows_kernel(fields, modes, tiles_here, length, devices, paired, *refs):
    parts = refs[:-6]
    rows_ref, square_ref, w_ref, link_ref, extra, edges = refs[-6:]
    chips = devices // CORES
    height = tiles_here * modes
    extra_at, _, _ = layout(fields, modes, tiles_here)
    edge_rows = slice(extra_at, extra_at + edges.shape[2])
    list_rows = slice(extra_at + fields * fields, extra_at + fields * fields + 5)
    me = lax.axis_index("space")
    core = lax.rem(me, CORES)
    chip = lax.div(me, CORES)
    lane = lax.broadcasted_iota(jnp.int32, (modes, TILE), 1)
    kinds = (core, 1 - core)
    sources = []
    for which, kind in enumerate(kinds):
        for q in range(chips):
            if paired:
                sources.append((parts[which * chips + q].at[...], jnp.bitwise_xor(chip, q), which))
            else:
                sources.append((parts[which].at[q], q, which))

    lists, weights = [], []
    for ref, place, which in sources:
        part = pltpu.roll(ref[list_rows, :].astype(F32), TILE - LIST_AT, 1)
        lists.append(part[0:1] * tiles_here + part[1:2])
        weights.append(part[2:3] + part[3:4] + part[4:5])
        edges[which, place] = ref[edge_rows, :].astype(F32)
    lists = jnp.concatenate(lists, axis=0)
    weights = jnp.concatenate(weights, axis=0)

    def coupling(which, place):
        values = edges[which, place, 0 : fields * fields, :]
        first = lax.broadcasted_iota(jnp.int32, values.shape, 1) < TILE // 2
        return jnp.where(first, pltpu.roll(values, TILE - 1, 1), pltpu.roll(values, 1, 1))

    def device_of(source, mixed):
        first = source < chips
        place = jnp.where(first, source, source - chips)
        if mixed:
            place = jnp.bitwise_xor(place, chip)
        return CORES * place + jnp.where(first, core, 1 - core)

    inner = devices * height
    total = inner + devices * 2 * modes
    column = lax.broadcasted_iota(jnp.int32, (devices, total), 1)
    outer = column - inner
    tile = jnp.where(
        outer < 0,
        device_of(over(column, height), paired) * tiles_here + modulo(over(column, modes), tiles_here),
        device_of(over(outer, 2 * modes), False) * tiles_here + modulo(over(outer, modes), 2) * (tiles_here - 1),
    )
    matrix = weight_rows(lists, weights, tile.astype(F32), modes, length)
    high, low = split(matrix)

    for index in range(devices):
        which, q = divmod(index, chips)
        kind = kinds[which]
        place = CORES * q + kind
        before = edges[1 - which, jnp.maximum(q - 1 + kind, 0), 0 : fields * modes, :]
        after = edges[1 - which, jnp.minimum(q + kind, chips - 1), 0 : fields * modes, :]
        before = before * (place > 0).astype(F32)
        after = after * (place < devices - 1).astype(F32)
        links = coupling(which, q)
        left = lane < TILE // 2
        near = [
            jnp.where(left, before[g * modes : (g + 1) * modes], after[g * modes : (g + 1) * modes])
            for g in range(fields)
        ]
        for f in range(fields):
            halo = jnp.zeros((modes, TILE), F32)
            for g in range(fields):
                halo = halo + links[f * fields + g : f * fields + g + 1] * near[g]
            at = index * 2 * modes
            extra[f, at : at + modes, :] = jnp.where(lane == 0, halo, 0.0)
            extra[f, at + modes : at + 2 * modes, :] = jnp.where(lane == TILE - 1, halo, 0.0)

    squares = jnp.zeros((devices * modes, TILE), F32)
    for f in range(fields):
        tiles = jnp.concatenate(
            [ref[f * height : (f + 1) * height, :] for ref, _, _ in sources] + [extra[f].astype(BF16)], axis=0
        )
        rows = jnp.dot(high, tiles, preferred_element_type=F32) + jnp.dot(low, tiles, preferred_element_type=F32)
        rows_ref[f] = rows
        squares = squares + rows * rows
    for o in range(devices):
        square_ref[o : o + 1, :] = jnp.sum(squares[o * modes : (o + 1) * modes], axis=0, keepdims=True)

    column = lax.broadcasted_iota(jnp.int32, (devices, w_ref.shape[1]), 1)
    local = over(column, modes)
    base = me * tiles_here
    tile = jnp.where(local <= tiles_here, base + local, jnp.where(local == tiles_here + 1, base - 1, -2))
    w_ref[...] = weight_rows(lists, weights, tile.astype(F32), modes, length)
    link_ref[0] = coupling(1, jnp.minimum(chip + core, chips - 1))
    link_ref[1] = coupling(1, jnp.maximum(chip - 1 + core, 0))


def update_kernel(samples, w_ref, rows_ref, link_ref, b_ref, j_ref, total_ref, handed_ref, out_ref, returned, lower, upper):
    fields, modes, cells = b_ref.shape
    tiles_here = cells // TILE
    owners = total_ref.shape[0]
    carrier = lax.rem(lax.axis_index("space"), CORES) == CORES - 1
    handed = jnp.concatenate([handed_ref[owners // CORES :], handed_ref[: owners // CORES]], axis=0)
    square = jnp.where(carrier, total_ref[...], handed)
    factor = lax.rsqrt(square / samples + EPS)
    factor = jnp.concatenate([jnp.broadcast_to(factor[o : o + 1], (modes, TILE)) for o in range(owners)], axis=0)
    high, low = split(jnp.transpose(w_ref[...]))
    for g in range(fields):
        normalized = (rows_ref[g] * factor).astype(BF16)
        returned[g] = jnp.dot(high, normalized, preferred_element_type=F32) + jnp.dot(
            low, normalized, preferred_element_type=F32
        )
    for t in range(tiles_here):
        at = slice(t * TILE, (t + 1) * TILE)
        values = [returned[g, t * modes : (t + 1) * modes, :] for g in range(fields)]
        for f in range(fields):
            center = b_ref[f, :, at].astype(F32)
            below = jnp.zeros((modes, TILE), F32)
            above = jnp.zeros((modes, TILE), F32)
            for g in range(fields):
                link = j_ref[g, f, :, at].astype(F32)
                center = center + link[0:1] * values[g]
                below = below + link[1:2] * values[g]
                above = above + link[2:3] * values[g]
            out_ref[f, :, at] = center
            lower[f, :, at] = below
            upper[f, :, at] = above
    wide = lax.broadcasted_iota(jnp.int32, (modes, cells), 1)
    nexts = slice(tiles_here * modes, (tiles_here + 1) * modes)
    lasts = slice((tiles_here + 1) * modes, (tiles_here + 2) * modes)
    for f in range(fields):
        head = jnp.zeros((modes, TILE), F32)
        tail = jnp.zeros((modes, TILE), F32)
        for g in range(fields):
            at = slice(g * fields + f, g * fields + f + 1)
            head = head + link_ref[0, at, :] * returned[g, nexts, :]
            tail = tail + link_ref[1, at, :] * returned[g, lasts, :]
        below = jnp.where(wide == cells - 1, head[:, 0:1], pltpu.roll(lower[f], cells - 1, 1))
        above = jnp.where(wide == 0, tail[:, TILE - 1 : TILE], pltpu.roll(upper[f], 1, 1))
        out_ref[f] = out_ref[f] + below + above


def shards(basis, jacobian, sample_list, sample_weight):
    space = lax.axis_size("space")
    mode = lax.axis_size("mode")
    modes, fields, cells = basis.shape
    length = sample_list.shape[1]
    tiles_here = cells // TILE
    height = space * modes
    width = pl.cdiv((tiles_here + 2) * modes, TILE) * TILE
    sent_rows = layout(fields, modes, tiles_here)[-1]
    b = jnp.transpose(basis, (1, 0, 2))
    j = jnp.transpose(jacobian, (1, 2, 0, 3))

    sent = pl.pallas_call(
        applied_kernel,
        out_shape=pltpu.VMEM((sent_rows, TILE), BF16),
        scratch_shapes=[
            pltpu.VMEM((fields, modes, cells), F32),
            pltpu.VMEM((fields, modes, cells), F32),
            pltpu.VMEM((fields * tiles_here * modes, TILE), F32),
            pltpu.VMEM((sent_rows - fields * tiles_here * modes, TILE), F32),
        ],
        name="applied",
    )(sample_list, sample_weight, b, j)
    chips = space // CORES
    paired = chips <= PAIRED and chips & (chips - 1) == 0
    if paired:
        parts = [sent] + [
            lax.ppermute(sent, "space", [(i, i ^ (CORES * d)) for i in range(space)]) for d in range(1, chips)
        ]
    else:
        groups = [[core + CORES * q for q in range(chips)] for core in range(CORES)]
        parts = [lax.all_gather(sent, "space", axis=0, axis_index_groups=groups)]
    parts = parts + [lax.ppermute(part, "space", [(i, i ^ 1) for i in range(space)]) for part in parts]

    rows, square, matrix, links = pl.pallas_call(
        functools.partial(rows_kernel, fields, modes, tiles_here, length, space, paired),
        out_shape=(
            pltpu.VMEM((fields, height, TILE), F32),
            pltpu.VMEM((space, TILE), F32),
            pltpu.VMEM((height, width), F32),
            pltpu.VMEM((2, fields * fields, TILE), F32),
        ),
        scratch_shapes=[
            pltpu.VMEM((fields, space * 2 * modes, TILE), F32),
            pltpu.VMEM((CORES, chips, layout(fields, modes, tiles_here)[1], TILE), F32),
        ],
        name="rows",
    )(*(near(part) for part in parts))
    far_core = CORES - 1
    carriers = [s for s in range(space) if s % CORES == far_core]
    total = square
    for step in range(1, mode):
        total = total + lax.ppermute(
            square,
            ("space", "mode"),
            [
                (s * mode + i, s * mode + ((i ^ step if mode & (mode - 1) == 0 else (i + step) % mode) if s in carriers else i))
                for s in range(space)
                for i in range(mode)
            ],
        )
    handed = lax.ppermute(total, "space", [(s, s ^ 1) for s in range(space)])

    update = pl.pallas_call(
        functools.partial(update_kernel, mode * modes * fields),
        out_shape=jax.ShapeDtypeStruct((fields, modes, cells), F32),
        scratch_shapes=[
            pltpu.VMEM((fields, width, TILE), F32),
            pltpu.VMEM((fields, modes, cells), F32),
            pltpu.VMEM((fields, modes, cells), F32),
        ],
        name="update",
    )(*(near(x) for x in (matrix, rows, links, b, j, total, handed)))
    return jnp.transpose(update, (1, 0, 2))


def solution(mesh):
    placed = (
        P("mode", None, "space"),
        P(None, None, None, "space"),
        P("space", None),
        P("space", None),
    )
    return jax.shard_map(
        shards, mesh=mesh, in_specs=placed, out_specs=P("mode", None, "space"), check_vma=False
    )
```

```python
import functools
import jax
import jax.numpy as jnp
from jax import lax
from jax.experimental import pallas as pl
from jax.experimental.pallas import tpu as pltpu
from jax.sharding import PartitionSpec as P

TILE = 128
EPS = 1e-05
F32 = jnp.float32
BF16 = jnp.bfloat16
CORES = 2
PAIRED = 4
LIST_AT = 32


def near(values):
    return pltpu.with_memory_space_constraint(values, pltpu.VMEM)


def over(values, by):
    return lax.shift_right_logical(values, by.bit_length() - 1) if by & (by - 1) == 0 else values // by


def modulo(values, by):
    return values & (by - 1) if by & (by - 1) == 0 else values % by


def layout(fields, modes, tiles_here):
    extra_at = fields * tiles_here * modes
    extra = max(fields * modes, fields * fields + 5)
    return extra_at, extra, pl.cdiv(extra_at + extra, 8) * 8


def split(values):
    high = values.astype(BF16)
    return high, (values - high.astype(F32)).astype(BF16)


def applied_kernel(list_ref, weight_ref, b_ref, j_ref, out_ref, lower, upper, applied, shared):
    fields, modes, cells = b_ref.shape
    length = list_ref.shape[1]
    tiles_here = cells // TILE
    height = tiles_here * modes
    extra_at, extra, total_rows = layout(fields, modes, tiles_here)
    wide = lax.broadcasted_iota(jnp.int32, (modes, cells), 1)
    half = lax.broadcasted_iota(jnp.int32, (modes, TILE), 1) < TILE // 2
    shared[...] = jnp.zeros(shared.shape, F32)
    for g in range(fields):
        values = b_ref[g].astype(F32)
        below = pltpu.roll(values, 1, 1)
        above = pltpu.roll(values, cells - 1, 1)
        edge = jnp.where(half, below[:, :TILE], above[:, cells - TILE :])
        shared[g * modes : (g + 1) * modes, :] = edge
        lower[g] = jnp.where(wide == 0, 0.0, below)
        upper[g] = jnp.where(wide == cells - 1, 0.0, above)
    for t in range(tiles_here):
        at = slice(t * TILE, (t + 1) * TILE)
        center = [b_ref[g, :, at].astype(F32) for g in range(fields)]
        below = [lower[g, :, at] for g in range(fields)]
        above = [upper[g, :, at] for g in range(fields)]
        for f in range(fields):
            total = jnp.zeros((modes, TILE), F32)
            for g in range(fields):
                link = j_ref[f, g, :, at].astype(F32)
                total = total + link[0:1] * center[g]
                total = total + link[1:2] * below[g]
                total = total + link[2:3] * above[g]
            applied[f * height + t * modes : f * height + (t + 1) * modes, :] = total
    out_ref[0 : fields * height, :] = applied[...].astype(BF16)
    half = half[0:1]
    rows = []
    for f in range(fields):
        for g in range(fields):
            head = j_ref[f, g, :, 0:TILE].astype(F32)[1:2]
            tail = j_ref[f, g, :, cells - TILE :].astype(F32)[2:3]
            rows.append(jnp.where(half, pltpu.roll(head, 1, 1), pltpu.roll(tail, TILE - 1, 1)))
    links = fields * fields
    lane = lax.broadcasted_iota(jnp.int32, shared.shape, 1)
    keep = jnp.where((lane == 0) | (lane == TILE - 1), shared[...], 0.0)
    shared[...] = keep
    lane = lane[0:links]
    beside = (lane == 1) | (lane == TILE - 2)
    shared[0:links, :] = jnp.where(beside, jnp.concatenate(rows, axis=0), keep[0:links])
    tiles = list_ref[...]
    device = over(tiles, tiles_here)
    high, low = split(weight_ref[...])
    rest = weight_ref[...] - high.astype(F32) - low.astype(F32)
    rows = [device.astype(F32), (tiles - device * tiles_here).astype(F32), high.astype(F32), low.astype(F32), rest]
    shared[links : links + 5, LIST_AT : LIST_AT + length] = jnp.concatenate(rows, axis=0)
    out_ref[extra_at:total_rows, :] = shared[...].astype(BF16)


def weight_rows(lists, weights, tile, modes, length):
    owners = lists.shape[0]
    width = tile.shape[1]
    total = jnp.zeros((owners, width), F32)
    for entry in range(length):
        total = total + jnp.where(lists[:, entry : entry + 1] == tile, weights[:, entry : entry + 1], 0.0)
    lane = lax.broadcasted_iota(jnp.int32, (modes, width), 1)
    sub = lax.broadcasted_iota(jnp.int32, (modes, width), 0)
    same = modulo(lane, modes) == sub
    return jnp.concatenate([jnp.where(same, total[o : o + 1], 0.0) for o in range(owners)], axis=0)


def rows_kernel(fields, modes, tiles_here, length, devices, paired, *refs):
    parts = refs[:-6]
    rows_ref, square_ref, w_ref, link_ref, extra, edges = refs[-6:]
    chips = devices // CORES
    height = tiles_here * modes
    extra_at, _, _ = layout(fields, modes, tiles_here)
    edge_rows = slice(extra_at, extra_at + edges.shape[2])
    list_rows = slice(extra_at + fields * fields, extra_at + fields * fields + 5)
    me = lax.axis_index("space")
    core = lax.rem(me, CORES)
    chip = lax.div(me, CORES)
    lane = lax.broadcasted_iota(jnp.int32, (modes, TILE), 1)
    kinds = (core, 1 - core)
    sources = []
    for which, kind in enumerate(kinds):
        for q in range(chips):
            if paired:
                sources.append((parts[which * chips + q].at[...], jnp.bitwise_xor(chip, q), which))
            else:
                sources.append((parts[which].at[q], q, which))

    lists, weights = [], []
    for ref, place, which in sources:
        part = pltpu.roll(ref[list_rows, :].astype(F32), TILE - LIST_AT, 1)
        lists.append(part[0:1] * tiles_here + part[1:2])
        weights.append(part[2:3] + part[3:4] + part[4:5])
        edges[which, place] = ref[edge_rows, :].astype(F32)
    lists = jnp.concatenate(lists, axis=0)
    weights = jnp.concatenate(weights, axis=0)

    def coupling(which, place):
        values = edges[which, place, 0 : fields * fields, :]
        first = lax.broadcasted_iota(jnp.int32, values.shape, 1) < TILE // 2
        return jnp.where(first, pltpu.roll(values, TILE - 1, 1), pltpu.roll(values, 1, 1))

    def device_of(source, mixed):
        first = source < chips
        place = jnp.where(first, source, source - chips)
        if mixed:
            place = jnp.bitwise_xor(place, chip)
        return CORES * place + jnp.where(first, core, 1 - core)

    inner = devices * height
    total = inner + devices * 2 * modes
    column = lax.broadcasted_iota(jnp.int32, (devices, total), 1)
    outer = column - inner
    tile = jnp.where(
        outer < 0,
        device_of(over(column, height), paired) * tiles_here + modulo(over(column, modes), tiles_here),
        device_of(over(outer, 2 * modes), False) * tiles_here + modulo(over(outer, modes), 2) * (tiles_here - 1),
    )
    matrix = weight_rows(lists, weights, tile.astype(F32), modes, length)
    high, low = split(matrix)

    for index in range(devices):
        which, q = divmod(index, chips)
        kind = kinds[which]
        place = CORES * q + kind
        before = edges[1 - which, jnp.maximum(q - 1 + kind, 0), 0 : fields * modes, :]
        after = edges[1 - which, jnp.minimum(q + kind, chips - 1), 0 : fields * modes, :]
        before = before * (place > 0).astype(F32)
        after = after * (place < devices - 1).astype(F32)
        links = coupling(which, q)
        left = lane < TILE // 2
        near = [
            jnp.where(left, before[g * modes : (g + 1) * modes], after[g * modes : (g + 1) * modes])
            for g in range(fields)
        ]
        for f in range(fields):
            halo = jnp.zeros((modes, TILE), F32)
            for g in range(fields):
                halo = halo + links[f * fields + g : f * fields + g + 1] * near[g]
            at = index * 2 * modes
            extra[f, at : at + modes, :] = jnp.where(lane == 0, halo, 0.0)
            extra[f, at + modes : at + 2 * modes, :] = jnp.where(lane == TILE - 1, halo, 0.0)

    squares = jnp.zeros((devices * modes, TILE), F32)
    for f in range(fields):
        tiles = jnp.concatenate(
            [ref[f * height : (f + 1) * height, :] for ref, _, _ in sources] + [extra[f].astype(BF16)], axis=0
        )
        rows = jnp.dot(high, tiles, preferred_element_type=F32) + jnp.dot(low, tiles, preferred_element_type=F32)
        rows_ref[f] = rows
        squares = squares + rows * rows
    for o in range(devices):
        square_ref[o : o + 1, :] = jnp.sum(squares[o * modes : (o + 1) * modes], axis=0, keepdims=True)

    column = lax.broadcasted_iota(jnp.int32, (devices, w_ref.shape[1]), 1)
    local = over(column, modes)
    base = me * tiles_here
    tile = jnp.where(local <= tiles_here, base + local, jnp.where(local == tiles_here + 1, base - 1, -2))
    w_ref[...] = weight_rows(lists, weights, tile.astype(F32), modes, length)
    link_ref[0] = coupling(1, jnp.minimum(chip + core, chips - 1))
    link_ref[1] = coupling(1, jnp.maximum(chip - 1 + core, 0))


def update_kernel(samples, w_ref, rows_ref, link_ref, b_ref, j_ref, *rest):
    square_refs = rest[:-4]
    out_ref, returned, lower, upper = rest[-4:]
    fields, modes, cells = b_ref.shape
    tiles_here = cells // TILE
    owners = square_refs[0].shape[0]
    square = square_refs[0][...]
    for ref in square_refs[1:]:
        square = square + ref[...]
    factor = lax.rsqrt(square / samples + EPS)
    factor = jnp.concatenate([jnp.broadcast_to(factor[o : o + 1], (modes, TILE)) for o in range(owners)], axis=0)
    high, low = split(jnp.transpose(w_ref[...]))
    for g in range(fields):
        normalized = (rows_ref[g] * factor).astype(BF16)
        returned[g] = jnp.dot(high, normalized, preferred_element_type=F32) + jnp.dot(
            low, normalized, preferred_element_type=F32
        )
    for t in range(tiles_here):
        at = slice(t * TILE, (t + 1) * TILE)
        values = [returned[g, t * modes : (t + 1) * modes, :] for g in range(fields)]
        for f in range(fields):
            center = b_ref[f, :, at].astype(F32)
            below = jnp.zeros((modes, TILE), F32)
            above = jnp.zeros((modes, TILE), F32)
            for g in range(fields):
                link = j_ref[g, f, :, at].astype(F32)
                center = center + link[0:1] * values[g]
                below = below + link[1:2] * values[g]
                above = above + link[2:3] * values[g]
            out_ref[f, :, at] = center
            lower[f, :, at] = below
            upper[f, :, at] = above
    wide = lax.broadcasted_iota(jnp.int32, (modes, cells), 1)
    nexts = slice(tiles_here * modes, (tiles_here + 1) * modes)
    lasts = slice((tiles_here + 1) * modes, (tiles_here + 2) * modes)
    for f in range(fields):
        head = jnp.zeros((modes, TILE), F32)
        tail = jnp.zeros((modes, TILE), F32)
        for g in range(fields):
            at = slice(g * fields + f, g * fields + f + 1)
            head = head + link_ref[0, at, :] * returned[g, nexts, :]
            tail = tail + link_ref[1, at, :] * returned[g, lasts, :]
        below = jnp.where(wide == cells - 1, head[:, 0:1], pltpu.roll(lower[f], cells - 1, 1))
        above = jnp.where(wide == 0, tail[:, TILE - 1 : TILE], pltpu.roll(upper[f], 1, 1))
        out_ref[f] = out_ref[f] + below + above


def shards(basis, jacobian, sample_list, sample_weight):
    space = lax.axis_size("space")
    mode = lax.axis_size("mode")
    modes, fields, cells = basis.shape
    length = sample_list.shape[1]
    tiles_here = cells // TILE
    height = space * modes
    width = pl.cdiv((tiles_here + 2) * modes, TILE) * TILE
    sent_rows = layout(fields, modes, tiles_here)[-1]
    b = jnp.transpose(basis, (1, 0, 2))
    j = jnp.transpose(jacobian, (1, 2, 0, 3))

    sent = pl.pallas_call(
        applied_kernel,
        out_shape=pltpu.VMEM((sent_rows, TILE), BF16),
        scratch_shapes=[
            pltpu.VMEM((fields, modes, cells), F32),
            pltpu.VMEM((fields, modes, cells), F32),
            pltpu.VMEM((fields * tiles_here * modes, TILE), F32),
            pltpu.VMEM((sent_rows - fields * tiles_here * modes, TILE), F32),
        ],
        name="applied",
    )(sample_list, sample_weight, b, j)
    chips = space // CORES
    paired = chips <= PAIRED and chips & (chips - 1) == 0
    if paired:
        parts = [sent] + [
            lax.ppermute(sent, "space", [(i, i ^ (CORES * d)) for i in range(space)]) for d in range(1, chips)
        ]
    else:
        groups = [[core + CORES * q for q in range(chips)] for core in range(CORES)]
        parts = [lax.all_gather(sent, "space", axis=0, axis_index_groups=groups)]
    parts = parts + [lax.ppermute(part, "space", [(i, i ^ 1) for i in range(space)]) for part in parts]

    rows, square, matrix, links = pl.pallas_call(
        functools.partial(rows_kernel, fields, modes, tiles_here, length, space, paired),
        out_shape=(
            pltpu.VMEM((fields, height, TILE), F32),
            pltpu.VMEM((space, TILE), F32),
            pltpu.VMEM((height, width), F32),
            pltpu.VMEM((2, fields * fields, TILE), F32),
        ),
        scratch_shapes=[
            pltpu.VMEM((fields, space * 2 * modes, TILE), F32),
            pltpu.VMEM((CORES, chips, layout(fields, modes, tiles_here)[1], TILE), F32),
        ],
        name="rows",
    )(*(near(part) for part in parts))
    even = mode & (mode - 1) == 0
    squares = [square] + [
        lax.ppermute(square, "mode", [(i, i ^ step if even else (i + step) % mode) for i in range(mode)])
        for step in range(1, mode)
    ]

    update = pl.pallas_call(
        functools.partial(update_kernel, mode * modes * fields),
        out_shape=jax.ShapeDtypeStruct((fields, modes, cells), F32),
        scratch_shapes=[
            pltpu.VMEM((fields, width, TILE), F32),
            pltpu.VMEM((fields, modes, cells), F32),
            pltpu.VMEM((fields, modes, cells), F32),
        ],
        name="update",
    )(*(near(x) for x in (matrix, rows, links, b, j, *squares)))
    return jnp.transpose(update, (1, 0, 2))


def solution(mesh):
    placed = (
        P("mode", None, "space"),
        P(None, None, None, "space"),
        P("space", None),
        P("space", None),
    )
    return jax.shard_map(
        shards, mesh=mesh, in_specs=placed, out_specs=P("mode", None, "space"), check_vma=False
    )
```

```python
import functools
import jax
import jax.numpy as jnp
from jax import lax
from jax.experimental import pallas as pl
from jax.experimental.pallas import tpu as pltpu
from jax.sharding import PartitionSpec as P

TILE = 128
EPS = 1e-05
F32 = jnp.float32
BF16 = jnp.bfloat16
CORES = 2
PAIRED = 4
LIST_AT = 32


def near(values):
    return pltpu.with_memory_space_constraint(values, pltpu.VMEM)


def over(values, by):
    return lax.shift_right_logical(values, by.bit_length() - 1) if by & (by - 1) == 0 else values // by


def modulo(values, by):
    return values & (by - 1) if by & (by - 1) == 0 else values % by


def layout(fields, modes, tiles_here):
    extra_at = fields * tiles_here * modes
    extra = max(fields * modes, fields * fields + 5)
    return extra_at, extra, pl.cdiv(extra_at + extra, 8) * 8


def split(values):
    high = values.astype(BF16)
    return high, (values - high.astype(F32)).astype(BF16)


def applied_kernel(list_ref, weight_ref, b_ref, j_ref, out_ref, lower, upper, applied, shared):
    fields, modes, cells = b_ref.shape
    length = list_ref.shape[1]
    tiles_here = cells // TILE
    height = tiles_here * modes
    extra_at, extra, total_rows = layout(fields, modes, tiles_here)
    wide = lax.broadcasted_iota(jnp.int32, (modes, cells), 1)
    half = lax.broadcasted_iota(jnp.int32, (modes, TILE), 1) < TILE // 2
    shared[...] = jnp.zeros(shared.shape, F32)
    for g in range(fields):
        values = b_ref[g].astype(F32)
        below = pltpu.roll(values, 1, 1)
        above = pltpu.roll(values, cells - 1, 1)
        edge = jnp.where(half, below[:, :TILE], above[:, cells - TILE :])
        shared[g * modes : (g + 1) * modes, :] = edge
        lower[g] = jnp.where(wide == 0, 0.0, below)
        upper[g] = jnp.where(wide == cells - 1, 0.0, above)
    for t in range(tiles_here):
        at = slice(t * TILE, (t + 1) * TILE)
        center = [b_ref[g, :, at].astype(F32) for g in range(fields)]
        below = [lower[g, :, at] for g in range(fields)]
        above = [upper[g, :, at] for g in range(fields)]
        for f in range(fields):
            total = jnp.zeros((modes, TILE), F32)
            for g in range(fields):
                link = j_ref[f, g, :, at].astype(F32)
                total = total + link[0:1] * center[g]
                total = total + link[1:2] * below[g]
                total = total + link[2:3] * above[g]
            applied[f * height + t * modes : f * height + (t + 1) * modes, :] = total
    out_ref[0 : fields * height, :] = applied[...].astype(BF16)
    half = half[0:1]
    rows = []
    for f in range(fields):
        for g in range(fields):
            head = j_ref[f, g, :, 0:TILE].astype(F32)[1:2]
            tail = j_ref[f, g, :, cells - TILE :].astype(F32)[2:3]
            rows.append(jnp.where(half, pltpu.roll(head, 1, 1), pltpu.roll(tail, TILE - 1, 1)))
    links = fields * fields
    lane = lax.broadcasted_iota(jnp.int32, shared.shape, 1)
    keep = jnp.where((lane == 0) | (lane == TILE - 1), shared[...], 0.0)
    shared[...] = keep
    lane = lane[0:links]
    beside = (lane == 1) | (lane == TILE - 2)
    shared[0:links, :] = jnp.where(beside, jnp.concatenate(rows, axis=0), keep[0:links])
    tiles = list_ref[...]
    device = over(tiles, tiles_here)
    high, low = split(weight_ref[...])
    rest = weight_ref[...] - high.astype(F32) - low.astype(F32)
    rows = [device.astype(F32), (tiles - device * tiles_here).astype(F32), high.astype(F32), low.astype(F32), rest]
    shared[links : links + 5, LIST_AT : LIST_AT + length] = jnp.concatenate(rows, axis=0)
    out_ref[extra_at:total_rows, :] = shared[...].astype(BF16)


def weight_rows(lists, weights, tile, modes, length):
    owners = lists.shape[0]
    width = tile.shape[1]
    total = jnp.zeros((owners, width), F32)
    for entry in range(length):
        total = total + jnp.where(lists[:, entry : entry + 1] == tile, weights[:, entry : entry + 1], 0.0)
    lane = lax.broadcasted_iota(jnp.int32, (modes, width), 1)
    sub = lax.broadcasted_iota(jnp.int32, (modes, width), 0)
    same = modulo(lane, modes) == sub
    return jnp.concatenate([jnp.where(same, total[o : o + 1], 0.0) for o in range(owners)], axis=0)


def rows_kernel(fields, modes, tiles_here, length, devices, paired, *refs):
    parts = refs[:-6]
    rows_ref, square_ref, w_ref, link_ref, extra, edges = refs[-6:]
    chips = devices // CORES
    height = tiles_here * modes
    extra_at, _, _ = layout(fields, modes, tiles_here)
    edge_rows = slice(extra_at, extra_at + edges.shape[2])
    list_rows = slice(extra_at + fields * fields, extra_at + fields * fields + 5)
    me = lax.axis_index("space")
    core = lax.rem(me, CORES)
    chip = lax.div(me, CORES)
    lane = lax.broadcasted_iota(jnp.int32, (modes, TILE), 1)
    kinds = (core, 1 - core)
    sources = []
    for which, kind in enumerate(kinds):
        for q in range(chips):
            if paired:
                sources.append((parts[which * chips + q].at[...], jnp.bitwise_xor(chip, -q % chips), which))
            else:
                sources.append((parts[which].at[q], q, which))

    lists, weights = [], []
    for ref, place, which in sources:
        part = pltpu.roll(ref[list_rows, :].astype(F32), TILE - LIST_AT, 1)
        lists.append(part[0:1] * tiles_here + part[1:2])
        weights.append(part[2:3] + part[3:4] + part[4:5])
        edges[which, place] = ref[edge_rows, :].astype(F32)
    lists = jnp.concatenate(lists, axis=0)
    weights = jnp.concatenate(weights, axis=0)

    def coupling(which, place):
        values = edges[which, place, 0 : fields * fields, :]
        first = lax.broadcasted_iota(jnp.int32, values.shape, 1) < TILE // 2
        return jnp.where(first, pltpu.roll(values, TILE - 1, 1), pltpu.roll(values, 1, 1))

    def device_of(source, mixed):
        first = source < chips
        place = jnp.where(first, source, source - chips)
        if mixed:
            place = jnp.bitwise_xor(modulo(chips - place, chips), chip)
        return CORES * place + jnp.where(first, core, 1 - core)

    inner = devices * height
    total = inner + devices * 2 * modes
    column = lax.broadcasted_iota(jnp.int32, (devices, total), 1)
    outer = column - inner
    tile = jnp.where(
        outer < 0,
        device_of(over(column, height), paired) * tiles_here + modulo(over(column, modes), tiles_here),
        device_of(over(outer, 2 * modes), False) * tiles_here + modulo(over(outer, modes), 2) * (tiles_here - 1),
    )
    matrix = weight_rows(lists, weights, tile.astype(F32), modes, length)
    high, low = split(matrix)

    for index in range(devices):
        which, q = divmod(index, chips)
        kind = kinds[which]
        place = CORES * q + kind
        before = edges[1 - which, jnp.maximum(q - 1 + kind, 0), 0 : fields * modes, :]
        after = edges[1 - which, jnp.minimum(q + kind, chips - 1), 0 : fields * modes, :]
        before = before * (place > 0).astype(F32)
        after = after * (place < devices - 1).astype(F32)
        links = coupling(which, q)
        left = lane < TILE // 2
        near = [
            jnp.where(left, before[g * modes : (g + 1) * modes], after[g * modes : (g + 1) * modes])
            for g in range(fields)
        ]
        for f in range(fields):
            halo = jnp.zeros((modes, TILE), F32)
            for g in range(fields):
                halo = halo + links[f * fields + g : f * fields + g + 1] * near[g]
            at = index * 2 * modes
            extra[f, at : at + modes, :] = jnp.where(lane == 0, halo, 0.0)
            extra[f, at + modes : at + 2 * modes, :] = jnp.where(lane == TILE - 1, halo, 0.0)

    squares = jnp.zeros((devices * modes, TILE), F32)
    for f in range(fields):
        tiles = jnp.concatenate(
            [ref[f * height : (f + 1) * height, :] for ref, _, _ in sources] + [extra[f].astype(BF16)], axis=0
        )
        rows = jnp.dot(high, tiles, preferred_element_type=F32) + jnp.dot(low, tiles, preferred_element_type=F32)
        rows_ref[f] = rows
        squares = squares + rows * rows
    for o in range(devices):
        square_ref[o : o + 1, :] = jnp.sum(squares[o * modes : (o + 1) * modes], axis=0, keepdims=True)

    column = lax.broadcasted_iota(jnp.int32, (devices, w_ref.shape[1]), 1)
    local = over(column, modes)
    base = me * tiles_here
    tile = jnp.where(local <= tiles_here, base + local, jnp.where(local == tiles_here + 1, base - 1, -2))
    w_ref[...] = weight_rows(lists, weights, tile.astype(F32), modes, length)
    link_ref[0] = coupling(1, jnp.minimum(chip + core, chips - 1))
    link_ref[1] = coupling(1, jnp.maximum(chip - 1 + core, 0))


def update_kernel(samples, w_ref, rows_ref, link_ref, b_ref, j_ref, *rest):
    square_refs = rest[:-4]
    out_ref, returned, lower, upper = rest[-4:]
    fields, modes, cells = b_ref.shape
    tiles_here = cells // TILE
    owners = square_refs[0].shape[0]
    square = square_refs[0][...]
    for ref in square_refs[1:]:
        square = square + ref[...]
    factor = lax.rsqrt(square / samples + EPS)
    factor = jnp.concatenate([jnp.broadcast_to(factor[o : o + 1], (modes, TILE)) for o in range(owners)], axis=0)
    high, low = split(jnp.transpose(w_ref[...]))
    for g in range(fields):
        normalized = (rows_ref[g] * factor).astype(BF16)
        returned[g] = jnp.dot(high, normalized, preferred_element_type=F32) + jnp.dot(
            low, normalized, preferred_element_type=F32
        )
    for t in range(tiles_here):
        at = slice(t * TILE, (t + 1) * TILE)
        values = [returned[g, t * modes : (t + 1) * modes, :] for g in range(fields)]
        for f in range(fields):
            center = b_ref[f, :, at].astype(F32)
            below = jnp.zeros((modes, TILE), F32)
            above = jnp.zeros((modes, TILE), F32)
            for g in range(fields):
                link = j_ref[g, f, :, at].astype(F32)
                center = center + link[0:1] * values[g]
                below = below + link[1:2] * values[g]
                above = above + link[2:3] * values[g]
            out_ref[f, :, at] = center
            lower[f, :, at] = below
            upper[f, :, at] = above
    wide = lax.broadcasted_iota(jnp.int32, (modes, cells), 1)
    nexts = slice(tiles_here * modes, (tiles_here + 1) * modes)
    lasts = slice((tiles_here + 1) * modes, (tiles_here + 2) * modes)
    for f in range(fields):
        head = jnp.zeros((modes, TILE), F32)
        tail = jnp.zeros((modes, TILE), F32)
        for g in range(fields):
            at = slice(g * fields + f, g * fields + f + 1)
            head = head + link_ref[0, at, :] * returned[g, nexts, :]
            tail = tail + link_ref[1, at, :] * returned[g, lasts, :]
        below = jnp.where(wide == cells - 1, head[:, 0:1], pltpu.roll(lower[f], cells - 1, 1))
        above = jnp.where(wide == 0, tail[:, TILE - 1 : TILE], pltpu.roll(upper[f], 1, 1))
        out_ref[f] = out_ref[f] + below + above


def shards(basis, jacobian, sample_list, sample_weight):
    space = lax.axis_size("space")
    mode = lax.axis_size("mode")
    modes, fields, cells = basis.shape
    length = sample_list.shape[1]
    tiles_here = cells // TILE
    height = space * modes
    width = pl.cdiv((tiles_here + 2) * modes, TILE) * TILE
    sent_rows = layout(fields, modes, tiles_here)[-1]
    b = jnp.transpose(basis, (1, 0, 2))
    j = jnp.transpose(jacobian, (1, 2, 0, 3))

    sent = pl.pallas_call(
        applied_kernel,
        out_shape=pltpu.VMEM((sent_rows, TILE), BF16),
        scratch_shapes=[
            pltpu.VMEM((fields, modes, cells), F32),
            pltpu.VMEM((fields, modes, cells), F32),
            pltpu.VMEM((fields * tiles_here * modes, TILE), F32),
            pltpu.VMEM((sent_rows - fields * tiles_here * modes, TILE), F32),
        ],
        name="applied",
    )(sample_list, sample_weight, b, j)
    chips = space // CORES
    paired = chips <= PAIRED and chips & (chips - 1) == 0
    if paired:
        parts = [sent] + [
            lax.ppermute(sent, "space", [(i, i ^ (CORES * d)) for i in range(space)]) for d in range(chips - 1, 0, -1)
        ]
    else:
        groups = [[core + CORES * q for q in range(chips)] for core in range(CORES)]
        parts = [lax.all_gather(sent, "space", axis=0, axis_index_groups=groups)]
    parts = parts + [lax.ppermute(part, "space", [(i, i ^ 1) for i in range(space)]) for part in parts]

    rows, square, matrix, links = pl.pallas_call(
        functools.partial(rows_kernel, fields, modes, tiles_here, length, space, paired),
        out_shape=(
            pltpu.VMEM((fields, height, TILE), F32),
            pltpu.VMEM((space, TILE), F32),
            pltpu.VMEM((height, width), F32),
            pltpu.VMEM((2, fields * fields, TILE), F32),
        ),
        scratch_shapes=[
            pltpu.VMEM((fields, space * 2 * modes, TILE), F32),
            pltpu.VMEM((CORES, chips, layout(fields, modes, tiles_here)[1], TILE), F32),
        ],
        name="rows",
    )(*(near(part) for part in parts))
    ring = list(range(0, mode, 2))[:1] + list(range(1, mode, 2)) + list(range(0, mode, 2))[:0:-1]
    squares = [square] + [
        lax.ppermute(square, "mode", [(ring[i], ring[(i + step) % mode]) for i in range(mode)])
        for step in range(mode - 1, 0, -1)
    ]

    update = pl.pallas_call(
        functools.partial(update_kernel, mode * modes * fields),
        out_shape=jax.ShapeDtypeStruct((fields, modes, cells), F32),
        scratch_shapes=[
            pltpu.VMEM((fields, width, TILE), F32),
            pltpu.VMEM((fields, modes, cells), F32),
            pltpu.VMEM((fields, modes, cells), F32),
        ],
        name="update",
    )(*(near(x) for x in (matrix, rows, links, b, j, *squares)))
    return jnp.transpose(update, (1, 0, 2))


def solution(mesh):
    placed = (
        P("mode", None, "space"),
        P(None, None, None, "space"),
        P("space", None),
        P("space", None),
    )
    return jax.shard_map(
        shards, mesh=mesh, in_specs=placed, out_specs=P("mode", None, "space"), check_vma=False
    )
```

```python
import functools
import jax
import jax.numpy as jnp
from jax import lax
from jax.experimental import pallas as pl
from jax.experimental.pallas import tpu as pltpu
from jax.sharding import PartitionSpec as P

TILE = 128
EPS = 1e-05
F32 = jnp.float32
BF16 = jnp.bfloat16
CORES = 2
PAIRED = 4
PIECES = 4
LIST_AT = 32


def near(values):
    return pltpu.with_memory_space_constraint(values, pltpu.VMEM)


def over(values, by):
    return lax.shift_right_logical(values, by.bit_length() - 1) if by & (by - 1) == 0 else values // by


def modulo(values, by):
    return values & (by - 1) if by & (by - 1) == 0 else values % by


def layout(fields, modes, tiles_here):
    extra_at = fields * tiles_here * modes
    extra = max(fields * modes, fields * fields + 5)
    return extra_at, extra, pl.cdiv(extra_at + extra, 8) * 8


def split(values):
    high = values.astype(BF16)
    return high, (values - high.astype(F32)).astype(BF16)


def pieces(cells):
    count = PIECES if cells % (PIECES * TILE) == 0 else 1
    return [slice(c * (cells // count), (c + 1) * (cells // count)) for c in range(count)]


def applied_kernel(
    list_hbm, weight_hbm, b_hbm, j_hbm, out_ref, list_ref, weight_ref, b_ref, j_ref, lower, upper, applied, shared, sems
):
    fields, modes, cells = b_ref.shape
    first = pltpu.make_async_copy(b_hbm, b_ref, sems.at[0])
    links_in = [
        pltpu.make_async_copy(j_hbm.at[:, :, :, part], j_ref.at[:, :, :, part], sems.at[3 + c])
        for c, part in enumerate(pieces(cells))
    ]
    list_in = pltpu.make_async_copy(list_hbm, list_ref, sems.at[1])
    weight_in = pltpu.make_async_copy(weight_hbm, weight_ref, sems.at[2])
    first.start()
    for copy in links_in:
        copy.start()
    list_in.start()
    weight_in.start()
    first.wait()
    length = list_ref.shape[1]
    tiles_here = cells // TILE
    height = tiles_here * modes
    extra_at, extra, total_rows = layout(fields, modes, tiles_here)
    wide = lax.broadcasted_iota(jnp.int32, (modes, cells), 1)
    half = lax.broadcasted_iota(jnp.int32, (modes, TILE), 1) < TILE // 2
    shared[...] = jnp.zeros(shared.shape, F32)
    for g in range(fields):
        values = b_ref[g].astype(F32)
        below = pltpu.roll(values, 1, 1)
        above = pltpu.roll(values, cells - 1, 1)
        edge = jnp.where(half, below[:, :TILE], above[:, cells - TILE :])
        shared[g * modes : (g + 1) * modes, :] = edge
        lower[g] = jnp.where(wide == 0, 0.0, below)
        upper[g] = jnp.where(wide == cells - 1, 0.0, above)
    for t in range(tiles_here):
        at = slice(t * TILE, (t + 1) * TILE)
        for copy, part in zip(links_in, pieces(cells)):
            if part.start == at.start:
                copy.wait()
        center = [b_ref[g, :, at].astype(F32) for g in range(fields)]
        below = [lower[g, :, at] for g in range(fields)]
        above = [upper[g, :, at] for g in range(fields)]
        for f in range(fields):
            total = jnp.zeros((modes, TILE), F32)
            for g in range(fields):
                link = j_ref[f, g, :, at].astype(F32)
                total = total + link[0:1] * center[g]
                total = total + link[1:2] * below[g]
                total = total + link[2:3] * above[g]
            applied[f * height + t * modes : f * height + (t + 1) * modes, :] = total
    out_ref[0 : fields * height, :] = applied[...].astype(BF16)
    half = half[0:1]
    rows = []
    for f in range(fields):
        for g in range(fields):
            head = j_ref[f, g, :, 0:TILE].astype(F32)[1:2]
            tail = j_ref[f, g, :, cells - TILE :].astype(F32)[2:3]
            rows.append(jnp.where(half, pltpu.roll(head, 1, 1), pltpu.roll(tail, TILE - 1, 1)))
    links = fields * fields
    lane = lax.broadcasted_iota(jnp.int32, shared.shape, 1)
    keep = jnp.where((lane == 0) | (lane == TILE - 1), shared[...], 0.0)
    shared[...] = keep
    lane = lane[0:links]
    beside = (lane == 1) | (lane == TILE - 2)
    shared[0:links, :] = jnp.where(beside, jnp.concatenate(rows, axis=0), keep[0:links])
    list_in.wait()
    weight_in.wait()
    tiles = list_ref[...]
    device = over(tiles, tiles_here)
    high, low = split(weight_ref[...])
    rest = weight_ref[...] - high.astype(F32) - low.astype(F32)
    rows = [device.astype(F32), (tiles - device * tiles_here).astype(F32), high.astype(F32), low.astype(F32), rest]
    shared[links : links + 5, LIST_AT : LIST_AT + length] = jnp.concatenate(rows, axis=0)
    out_ref[extra_at:total_rows, :] = shared[...].astype(BF16)


def weight_rows(lists, weights, tile, modes, length):
    owners = lists.shape[0]
    width = tile.shape[1]
    total = jnp.zeros((owners, width), F32)
    for entry in range(length):
        total = total + jnp.where(lists[:, entry : entry + 1] == tile, weights[:, entry : entry + 1], 0.0)
    lane = lax.broadcasted_iota(jnp.int32, (modes, width), 1)
    sub = lax.broadcasted_iota(jnp.int32, (modes, width), 0)
    same = modulo(lane, modes) == sub
    return jnp.concatenate([jnp.where(same, total[o : o + 1], 0.0) for o in range(owners)], axis=0)


def rows_kernel(fields, modes, tiles_here, length, devices, paired, *refs):
    parts = refs[:-6]
    rows_ref, square_ref, w_ref, link_ref, extra, edges = refs[-6:]
    chips = devices // CORES
    height = tiles_here * modes
    extra_at, _, _ = layout(fields, modes, tiles_here)
    edge_rows = slice(extra_at, extra_at + edges.shape[2])
    list_rows = slice(extra_at + fields * fields, extra_at + fields * fields + 5)
    me = lax.axis_index("space")
    core = lax.rem(me, CORES)
    chip = lax.div(me, CORES)
    lane = lax.broadcasted_iota(jnp.int32, (modes, TILE), 1)
    kinds = (core, 1 - core)
    sources = []
    for which, kind in enumerate(kinds):
        for q in range(chips):
            if paired:
                sources.append((parts[which * chips + q].at[...], jnp.bitwise_xor(chip, q), which))
            else:
                sources.append((parts[which].at[q], q, which))

    lists, weights = [], []
    for ref, place, which in sources:
        part = pltpu.roll(ref[list_rows, :].astype(F32), TILE - LIST_AT, 1)
        lists.append(part[0:1] * tiles_here + part[1:2])
        weights.append(part[2:3] + part[3:4] + part[4:5])
        edges[which, place] = ref[edge_rows, :].astype(F32)
    lists = jnp.concatenate(lists, axis=0)
    weights = jnp.concatenate(weights, axis=0)

    def coupling(which, place):
        values = edges[which, place, 0 : fields * fields, :]
        first = lax.broadcasted_iota(jnp.int32, values.shape, 1) < TILE // 2
        return jnp.where(first, pltpu.roll(values, TILE - 1, 1), pltpu.roll(values, 1, 1))

    def device_of(source, mixed):
        first = source < chips
        place = jnp.where(first, source, source - chips)
        if mixed:
            place = jnp.bitwise_xor(place, chip)
        return CORES * place + jnp.where(first, core, 1 - core)

    inner = devices * height
    total = inner + devices * 2 * modes
    column = lax.broadcasted_iota(jnp.int32, (devices, total), 1)
    outer = column - inner
    tile = jnp.where(
        outer < 0,
        device_of(over(column, height), paired) * tiles_here + modulo(over(column, modes), tiles_here),
        device_of(over(outer, 2 * modes), False) * tiles_here + modulo(over(outer, modes), 2) * (tiles_here - 1),
    )
    matrix = weight_rows(lists, weights, tile.astype(F32), modes, length)
    high, low = split(matrix)

    for index in range(devices):
        which, q = divmod(index, chips)
        kind = kinds[which]
        place = CORES * q + kind
        before = edges[1 - which, jnp.maximum(q - 1 + kind, 0), 0 : fields * modes, :]
        after = edges[1 - which, jnp.minimum(q + kind, chips - 1), 0 : fields * modes, :]
        before = before * (place > 0).astype(F32)
        after = after * (place < devices - 1).astype(F32)
        links = coupling(which, q)
        left = lane < TILE // 2
        near = [
            jnp.where(left, before[g * modes : (g + 1) * modes], after[g * modes : (g + 1) * modes])
            for g in range(fields)
        ]
        for f in range(fields):
            halo = jnp.zeros((modes, TILE), F32)
            for g in range(fields):
                halo = halo + links[f * fields + g : f * fields + g + 1] * near[g]
            at = index * 2 * modes
            extra[f, at : at + modes, :] = jnp.where(lane == 0, halo, 0.0)
            extra[f, at + modes : at + 2 * modes, :] = jnp.where(lane == TILE - 1, halo, 0.0)

    squares = jnp.zeros((devices * modes, TILE), F32)
    for f in range(fields):
        tiles = jnp.concatenate(
            [ref[f * height : (f + 1) * height, :] for ref, _, _ in sources] + [extra[f].astype(BF16)], axis=0
        )
        rows = jnp.dot(high, tiles, preferred_element_type=F32) + jnp.dot(low, tiles, preferred_element_type=F32)
        rows_ref[f] = rows
        squares = squares + rows * rows
    for o in range(devices):
        square_ref[o : o + 1, :] = jnp.sum(squares[o * modes : (o + 1) * modes], axis=0, keepdims=True)

    column = lax.broadcasted_iota(jnp.int32, (devices, w_ref.shape[1]), 1)
    local = over(column, modes)
    base = me * tiles_here
    tile = jnp.where(local <= tiles_here, base + local, jnp.where(local == tiles_here + 1, base - 1, -2))
    w_ref[...] = weight_rows(lists, weights, tile.astype(F32), modes, length)
    link_ref[0] = coupling(1, jnp.minimum(chip + core, chips - 1))
    link_ref[1] = coupling(1, jnp.maximum(chip - 1 + core, 0))


def update_kernel(samples, w_ref, rows_ref, link_ref, b_ref, j_ref, *rest):
    square_refs = rest[:-4]
    out_hbm, returned, out_ref, sems = rest[-4:]
    fields, modes, cells = b_ref.shape
    tiles_here = cells // TILE
    owners = square_refs[0].shape[0]
    square = square_refs[0][...]
    for ref in square_refs[1:]:
        square = square + ref[...]
    factor = lax.rsqrt(square / samples + EPS)
    factor = jnp.concatenate([jnp.broadcast_to(factor[o : o + 1], (modes, TILE)) for o in range(owners)], axis=0)
    high, low = split(jnp.transpose(w_ref[...]))
    for g in range(fields):
        normalized = (rows_ref[g] * factor).astype(BF16)
        returned[g] = jnp.dot(high, normalized, preferred_element_type=F32) + jnp.dot(
            low, normalized, preferred_element_type=F32
        )
    nexts = slice(tiles_here * modes, (tiles_here + 1) * modes)
    lasts = slice((tiles_here + 1) * modes, (tiles_here + 2) * modes)
    head, tail = [], []
    for f in range(fields):
        head.append(jnp.zeros((modes, TILE), F32))
        tail.append(jnp.zeros((modes, TILE), F32))
        for g in range(fields):
            at = slice(g * fields + f, g * fields + f + 1)
            head[f] = head[f] + link_ref[0, at, :] * returned[g, nexts, :]
            tail[f] = tail[f] + link_ref[1, at, :] * returned[g, lasts, :]
    lane = lax.broadcasted_iota(jnp.int32, (modes, TILE), 1)
    parts = pieces(cells)
    copies = [
        pltpu.make_async_copy(out_ref.at[:, :, part], out_hbm.at[:, :, part], sems.at[c])
        for c, part in enumerate(parts)
    ]

    def finish(t, center, before, here, after):
        at = slice(t * TILE, (t + 1) * TILE)
        for f in range(fields):
            below = pltpu.roll(jnp.where(lane == 0, after[f], here[0][f]), TILE - 1, 1)
            above = pltpu.roll(jnp.where(lane == TILE - 1, before[f], here[1][f]), 1, 1)
            out_ref[f, :, at] = center[f] + below + above
        for copy, part in zip(copies, parts):
            if part.stop == at.stop:
                copy.start()

    before, waiting = tail, None
    for t in range(tiles_here):
        at = slice(t * TILE, (t + 1) * TILE)
        values = [returned[g, t * modes : (t + 1) * modes, :] for g in range(fields)]
        center, below, above = [], [], []
        for f in range(fields):
            center.append(b_ref[f, :, at].astype(F32))
            below.append(jnp.zeros((modes, TILE), F32))
            above.append(jnp.zeros((modes, TILE), F32))
            for g in range(fields):
                link = j_ref[g, f, :, at].astype(F32)
                center[f] = center[f] + link[0:1] * values[g]
                below[f] = below[f] + link[1:2] * values[g]
                above[f] = above[f] + link[2:3] * values[g]
        if waiting is not None:
            finish(t - 1, waiting[0], before, waiting[1:], below)
            before = waiting[2]
        waiting = (center, below, above)
    finish(tiles_here - 1, waiting[0], before, waiting[1:], head)
    for copy in copies:
        copy.wait()


def shards(basis, jacobian, sample_list, sample_weight):
    space = lax.axis_size("space")
    mode = lax.axis_size("mode")
    modes, fields, cells = basis.shape
    length = sample_list.shape[1]
    tiles_here = cells // TILE
    height = space * modes
    width = pl.cdiv((tiles_here + 2) * modes, TILE) * TILE
    sent_rows = layout(fields, modes, tiles_here)[-1]
    b = jnp.transpose(basis, (1, 0, 2))
    j = jnp.transpose(jacobian, (1, 2, 0, 3))

    sent = pl.pallas_call(
        applied_kernel,
        out_shape=pltpu.VMEM((sent_rows, TILE), BF16),
        in_specs=[pl.BlockSpec(memory_space=pl.ANY)] * 4,
        scratch_shapes=[
            pltpu.VMEM(sample_list.shape, sample_list.dtype),
            pltpu.VMEM(sample_weight.shape, F32),
            pltpu.VMEM(b.shape, BF16),
            pltpu.VMEM(j.shape, BF16),
            pltpu.VMEM((fields, modes, cells), F32),
            pltpu.VMEM((fields, modes, cells), F32),
            pltpu.VMEM((fields * tiles_here * modes, TILE), F32),
            pltpu.VMEM((sent_rows - fields * tiles_here * modes, TILE), F32),
            pltpu.SemaphoreType.DMA((3 + len(pieces(cells)),)),
        ],
        name="applied",
    )(sample_list, sample_weight, b, j)
    chips = space // CORES
    paired = chips <= PAIRED and chips & (chips - 1) == 0
    if paired:
        parts = [sent] + [
            lax.ppermute(sent, "space", [(i, i ^ (CORES * d)) for i in range(space)]) for d in range(1, chips)
        ]
    else:
        groups = [[core + CORES * q for q in range(chips)] for core in range(CORES)]
        parts = [lax.all_gather(sent, "space", axis=0, axis_index_groups=groups)]
    parts = parts + [lax.ppermute(part, "space", [(i, i ^ 1) for i in range(space)]) for part in parts]

    rows, square, matrix, links = pl.pallas_call(
        functools.partial(rows_kernel, fields, modes, tiles_here, length, space, paired),
        out_shape=(
            pltpu.VMEM((fields, height, TILE), F32),
            pltpu.VMEM((space, TILE), F32),
            pltpu.VMEM((height, width), F32),
            pltpu.VMEM((2, fields * fields, TILE), F32),
        ),
        scratch_shapes=[
            pltpu.VMEM((fields, space * 2 * modes, TILE), F32),
            pltpu.VMEM((CORES, chips, layout(fields, modes, tiles_here)[1], TILE), F32),
        ],
        name="rows",
    )(*(near(part) for part in parts))
    ring = list(range(0, mode, 2))[:1] + list(range(1, mode, 2)) + list(range(0, mode, 2))[:0:-1]
    squares = [square] + [
        lax.ppermute(square, "mode", [(ring[i], ring[(i + step) % mode]) for i in range(mode)])
        for step in range(mode - 1, 0, -1)
    ]

    update = pl.pallas_call(
        functools.partial(update_kernel, mode * modes * fields),
        out_shape=jax.ShapeDtypeStruct((fields, modes, cells), F32),
        out_specs=pl.BlockSpec(memory_space=pl.ANY),
        scratch_shapes=[
            pltpu.VMEM((fields, width, TILE), F32),
            pltpu.VMEM((fields, modes, cells), F32),
            pltpu.SemaphoreType.DMA((len(pieces(cells)),)),
        ],
        name="update",
    )(*(near(x) for x in (matrix, rows, links, b, j, *squares)))
    return jnp.transpose(update, (1, 0, 2))


def solution(mesh):
    placed = (
        P("mode", None, "space"),
        P(None, None, None, "space"),
        P("space", None),
        P("space", None),
    )
    return jax.shard_map(
        shards, mesh=mesh, in_specs=placed, out_specs=P("mode", None, "space"), check_vma=False
    )
```

```python
import functools
import jax
import jax.numpy as jnp
from jax import lax
from jax.experimental import pallas as pl
from jax.experimental.pallas import tpu as pltpu
from jax.sharding import PartitionSpec as P

TILE = 128
EPS = 1e-05
F32 = jnp.float32
BF16 = jnp.bfloat16
CORES = 2
PAIRED = 4
LIST_AT = 32


def near(values):
    return pltpu.with_memory_space_constraint(values, pltpu.VMEM)


def over(values, by):
    return lax.shift_right_logical(values, by.bit_length() - 1) if by & (by - 1) == 0 else values // by


def modulo(values, by):
    return values & (by - 1) if by & (by - 1) == 0 else values % by


def layout(fields, modes, tiles_here):
    extra_at = fields * tiles_here * modes
    extra = max(fields * modes, fields * fields + 5)
    return extra_at, extra, pl.cdiv(extra_at + extra, 8) * 8


def split(values):
    high = values.astype(BF16)
    return high, (values - high.astype(F32)).astype(BF16)


def product(both, values):
    parts = jnp.dot(both, values, preferred_element_type=F32)
    height = parts.shape[0] // 2
    return parts[:height] + parts[height:]


def applied_kernel(list_ref, weight_ref, b_ref, j_ref, out_ref, link_ref, lower, upper, applied, shared):
    fields, modes, cells = b_ref.shape
    length = list_ref.shape[1]
    tiles_here = cells // TILE
    height = tiles_here * modes
    extra_at, extra, total_rows = layout(fields, modes, tiles_here)
    wide = lax.broadcasted_iota(jnp.int32, (modes, cells), 1)
    half = lax.broadcasted_iota(jnp.int32, (modes, TILE), 1) < TILE // 2
    shared[...] = jnp.zeros(shared.shape, F32)
    for f in range(fields):
        for g in range(fields):
            link_ref[f * fields + g] = j_ref[f, g].astype(F32)
    for g in range(fields):
        values = b_ref[g].astype(F32)
        below = pltpu.roll(values, 1, 1)
        above = pltpu.roll(values, cells - 1, 1)
        edge = jnp.where(half, below[:, :TILE], above[:, cells - TILE :])
        shared[g * modes : (g + 1) * modes, :] = edge
        lower[g] = jnp.where(wide == 0, 0.0, below)
        upper[g] = jnp.where(wide == cells - 1, 0.0, above)
    for t in range(tiles_here):
        at = slice(t * TILE, (t + 1) * TILE)
        center = [b_ref[g, :, at].astype(F32) for g in range(fields)]
        below = [lower[g, :, at] for g in range(fields)]
        above = [upper[g, :, at] for g in range(fields)]
        for f in range(fields):
            total = jnp.zeros((modes, TILE), F32)
            for g in range(fields):
                total = total + link_ref[f * fields + g, 0:1, at] * center[g]
                total = total + link_ref[f * fields + g, 1:2, at] * below[g]
                total = total + link_ref[f * fields + g, 2:3, at] * above[g]
            applied[f * height + t * modes : f * height + (t + 1) * modes, :] = total
    out_ref[0 : fields * height, :] = applied[...].astype(BF16)
    half = half[0:1]
    rows = []
    for f in range(fields):
        for g in range(fields):
            head = link_ref[f * fields + g, 1:2, 0:TILE]
            tail = link_ref[f * fields + g, 2:3, cells - TILE :]
            rows.append(jnp.where(half, pltpu.roll(head, 1, 1), pltpu.roll(tail, TILE - 1, 1)))
    links = fields * fields
    lane = lax.broadcasted_iota(jnp.int32, shared.shape, 1)
    keep = jnp.where((lane == 0) | (lane == TILE - 1), shared[...], 0.0)
    shared[...] = keep
    lane = lane[0:links]
    beside = (lane == 1) | (lane == TILE - 2)
    shared[0:links, :] = jnp.where(beside, jnp.concatenate(rows, axis=0), keep[0:links])
    tiles = list_ref[...]
    device = over(tiles, tiles_here)
    high, low = split(weight_ref[...])
    rest = weight_ref[...] - high.astype(F32) - low.astype(F32)
    rows = [device.astype(F32), (tiles - device * tiles_here).astype(F32), high.astype(F32), low.astype(F32), rest]
    shared[links : links + 5, LIST_AT : LIST_AT + length] = jnp.concatenate(rows, axis=0)
    out_ref[extra_at:total_rows, :] = shared[...].astype(BF16)


def weight_rows(lists, weights, tile, modes, length):
    owners = lists.shape[0]
    width = tile.shape[1]
    total = jnp.zeros((owners, width), F32)
    for entry in range(length):
        total = total + jnp.where(lists[:, entry : entry + 1] == tile, weights[:, entry : entry + 1], 0.0)
    lane = lax.broadcasted_iota(jnp.int32, (modes, width), 1)
    sub = lax.broadcasted_iota(jnp.int32, (modes, width), 0)
    same = modulo(lane, modes) == sub
    return jnp.concatenate([jnp.where(same, total[o : o + 1], 0.0) for o in range(owners)], axis=0)


def rows_kernel(fields, modes, tiles_here, length, devices, paired, *refs):
    parts = refs[:-6]
    rows_ref, square_ref, w_ref, link_ref, extra, edges = refs[-6:]
    chips = devices // CORES
    height = tiles_here * modes
    extra_at, _, _ = layout(fields, modes, tiles_here)
    edge_rows = slice(extra_at, extra_at + edges.shape[2])
    list_rows = slice(extra_at + fields * fields, extra_at + fields * fields + 5)
    me = lax.axis_index("space")
    core = lax.rem(me, CORES)
    chip = lax.div(me, CORES)
    lane = lax.broadcasted_iota(jnp.int32, (modes, TILE), 1)
    kinds = (core, 1 - core)
    sources = []
    for which, kind in enumerate(kinds):
        for q in range(chips):
            if paired:
                sources.append((parts[which * chips + q].at[...], jnp.bitwise_xor(chip, q), which))
            else:
                sources.append((parts[which].at[q], q, which))

    lists, weights = [], []
    for ref, place, which in sources:
        part = pltpu.roll(ref[list_rows, :].astype(F32), TILE - LIST_AT, 1)
        lists.append(part[0:1] * tiles_here + part[1:2])
        weights.append(part[2:3] + part[3:4] + part[4:5])
        edges[which, place] = ref[edge_rows, :].astype(F32)
    lists = jnp.concatenate(lists, axis=0)
    weights = jnp.concatenate(weights, axis=0)

    def coupling(which, place):
        values = edges[which, place, 0 : fields * fields, :]
        first = lax.broadcasted_iota(jnp.int32, values.shape, 1) < TILE // 2
        return jnp.where(first, pltpu.roll(values, TILE - 1, 1), pltpu.roll(values, 1, 1))

    def device_of(source, mixed):
        first = source < chips
        place = jnp.where(first, source, source - chips)
        if mixed:
            place = jnp.bitwise_xor(place, chip)
        return CORES * place + jnp.where(first, core, 1 - core)

    inner = devices * height
    total = inner + devices * 2 * modes
    column = lax.broadcasted_iota(jnp.int32, (devices, total), 1)
    outer = column - inner
    tile = jnp.where(
        outer < 0,
        device_of(over(column, height), paired) * tiles_here + modulo(over(column, modes), tiles_here),
        device_of(over(outer, 2 * modes), False) * tiles_here + modulo(over(outer, modes), 2) * (tiles_here - 1),
    )
    matrix = weight_rows(lists, weights, tile.astype(F32), modes, length)
    both = jnp.concatenate(split(matrix), axis=0)

    for index in range(devices):
        which, q = divmod(index, chips)
        kind = kinds[which]
        place = CORES * q + kind
        before = edges[1 - which, jnp.maximum(q - 1 + kind, 0), 0 : fields * modes, :]
        after = edges[1 - which, jnp.minimum(q + kind, chips - 1), 0 : fields * modes, :]
        before = before * (place > 0).astype(F32)
        after = after * (place < devices - 1).astype(F32)
        links = coupling(which, q)
        left = lane < TILE // 2
        near = [
            jnp.where(left, before[g * modes : (g + 1) * modes], after[g * modes : (g + 1) * modes])
            for g in range(fields)
        ]
        for f in range(fields):
            halo = jnp.zeros((modes, TILE), F32)
            for g in range(fields):
                halo = halo + links[f * fields + g : f * fields + g + 1] * near[g]
            at = index * 2 * modes
            extra[f, at : at + modes, :] = jnp.where(lane == 0, halo, 0.0)
            extra[f, at + modes : at + 2 * modes, :] = jnp.where(lane == TILE - 1, halo, 0.0)

    squares = jnp.zeros((devices * modes, TILE), F32)
    for f in range(fields):
        tiles = jnp.concatenate(
            [ref[f * height : (f + 1) * height, :] for ref, _, _ in sources] + [extra[f].astype(BF16)], axis=0
        )
        rows = product(both, tiles)
        rows_ref[f] = rows
        squares = squares + rows * rows
    for o in range(devices):
        square_ref[o : o + 1, :] = jnp.sum(squares[o * modes : (o + 1) * modes], axis=0, keepdims=True)

    column = lax.broadcasted_iota(jnp.int32, (devices, w_ref.shape[1]), 1)
    local = over(column, modes)
    base = me * tiles_here
    tile = jnp.where(local <= tiles_here, base + local, jnp.where(local == tiles_here + 1, base - 1, -2))
    w_ref[...] = weight_rows(lists, weights, tile.astype(F32), modes, length)
    link_ref[0] = coupling(1, jnp.minimum(chip + core, chips - 1))
    link_ref[1] = coupling(1, jnp.maximum(chip - 1 + core, 0))


def update_kernel(samples, w_ref, rows_ref, link_ref, b_ref, j_ref, *rest):
    square_refs = rest[:-4]
    out_ref, returned, lower, upper = rest[-4:]
    fields, modes, cells = b_ref.shape
    tiles_here = cells // TILE
    owners = square_refs[0].shape[0]
    square = square_refs[0][...]
    for ref in square_refs[1:]:
        square = square + ref[...]
    factor = lax.rsqrt(square / samples + EPS)
    factor = jnp.concatenate([jnp.broadcast_to(factor[o : o + 1], (modes, TILE)) for o in range(owners)], axis=0)
    both = jnp.concatenate(split(jnp.transpose(w_ref[...])), axis=0)
    for g in range(fields):
        normalized = (rows_ref[g] * factor).astype(BF16)
        returned[g] = product(both, normalized)
    for t in range(tiles_here):
        at = slice(t * TILE, (t + 1) * TILE)
        values = [returned[g, t * modes : (t + 1) * modes, :] for g in range(fields)]
        for f in range(fields):
            center = b_ref[f, :, at].astype(F32)
            below = jnp.zeros((modes, TILE), F32)
            above = jnp.zeros((modes, TILE), F32)
            for g in range(fields):
                center = center + j_ref[g * fields + f, 0:1, at] * values[g]
                below = below + j_ref[g * fields + f, 1:2, at] * values[g]
                above = above + j_ref[g * fields + f, 2:3, at] * values[g]
            out_ref[f, :, at] = center
            lower[f, :, at] = below
            upper[f, :, at] = above
    wide = lax.broadcasted_iota(jnp.int32, (modes, cells), 1)
    nexts = slice(tiles_here * modes, (tiles_here + 1) * modes)
    lasts = slice((tiles_here + 1) * modes, (tiles_here + 2) * modes)
    for f in range(fields):
        head = jnp.zeros((modes, TILE), F32)
        tail = jnp.zeros((modes, TILE), F32)
        for g in range(fields):
            at = slice(g * fields + f, g * fields + f + 1)
            head = head + link_ref[0, at, :] * returned[g, nexts, :]
            tail = tail + link_ref[1, at, :] * returned[g, lasts, :]
        below = jnp.where(wide == cells - 1, head[:, 0:1], pltpu.roll(lower[f], cells - 1, 1))
        above = jnp.where(wide == 0, tail[:, TILE - 1 : TILE], pltpu.roll(upper[f], 1, 1))
        out_ref[f] = out_ref[f] + below + above


def shards(basis, jacobian, sample_list, sample_weight):
    space = lax.axis_size("space")
    mode = lax.axis_size("mode")
    modes, fields, cells = basis.shape
    length = sample_list.shape[1]
    tiles_here = cells // TILE
    height = space * modes
    width = pl.cdiv((tiles_here + 2) * modes, TILE) * TILE
    sent_rows = layout(fields, modes, tiles_here)[-1]
    b = jnp.transpose(basis, (1, 0, 2))
    j = jnp.transpose(jacobian, (1, 2, 0, 3))

    sent, wide = pl.pallas_call(
        applied_kernel,
        out_shape=(pltpu.VMEM((sent_rows, TILE), BF16), pltpu.VMEM((fields * fields, 3, cells), F32)),
        scratch_shapes=[
            pltpu.VMEM((fields, modes, cells), F32),
            pltpu.VMEM((fields, modes, cells), F32),
            pltpu.VMEM((fields * tiles_here * modes, TILE), F32),
            pltpu.VMEM((sent_rows - fields * tiles_here * modes, TILE), F32),
        ],
        name="applied",
    )(sample_list, sample_weight, b, j)
    chips = space // CORES
    paired = chips <= PAIRED and chips & (chips - 1) == 0
    if paired:
        parts = [sent] + [
            lax.ppermute(sent, "space", [(i, i ^ (CORES * d)) for i in range(space)]) for d in range(1, chips)
        ]
    else:
        groups = [[core + CORES * q for q in range(chips)] for core in range(CORES)]
        parts = [lax.all_gather(sent, "space", axis=0, axis_index_groups=groups)]
    parts = parts + [lax.ppermute(part, "space", [(i, i ^ 1) for i in range(space)]) for part in parts]

    rows, square, matrix, links = pl.pallas_call(
        functools.partial(rows_kernel, fields, modes, tiles_here, length, space, paired),
        out_shape=(
            pltpu.VMEM((fields, height, TILE), F32),
            pltpu.VMEM((space, TILE), F32),
            pltpu.VMEM((height, width), F32),
            pltpu.VMEM((2, fields * fields, TILE), F32),
        ),
        scratch_shapes=[
            pltpu.VMEM((fields, space * 2 * modes, TILE), F32),
            pltpu.VMEM((CORES, chips, layout(fields, modes, tiles_here)[1], TILE), F32),
        ],
        name="rows",
    )(*(near(part) for part in parts))
    ring = list(range(0, mode, 2))[:1] + list(range(1, mode, 2)) + list(range(0, mode, 2))[:0:-1]
    squares = [square] + [
        lax.ppermute(square, "mode", [(ring[i], ring[(i + step) % mode]) for i in range(mode)])
        for step in range(mode - 1, 0, -1)
    ]

    update = pl.pallas_call(
        functools.partial(update_kernel, mode * modes * fields),
        out_shape=jax.ShapeDtypeStruct((fields, modes, cells), F32),
        scratch_shapes=[
            pltpu.VMEM((fields, width, TILE), F32),
            pltpu.VMEM((fields, modes, cells), F32),
            pltpu.VMEM((fields, modes, cells), F32),
        ],
        name="update",
    )(*(near(x) for x in (matrix, rows, links, b, wide, *squares)))
    return jnp.transpose(update, (1, 0, 2))


def solution(mesh):
    placed = (
        P("mode", None, "space"),
        P(None, None, None, "space"),
        P("space", None),
        P("space", None),
    )
    return jax.shard_map(
        shards, mesh=mesh, in_specs=placed, out_specs=P("mode", None, "space"), check_vma=False
    )
```

```python
import functools
import jax
import jax.numpy as jnp
from jax import lax
from jax.experimental import pallas as pl
from jax.experimental.pallas import tpu as pltpu
from jax.sharding import PartitionSpec as P

TILE = 128
EPS = 1e-05
F32 = jnp.float32
BF16 = jnp.bfloat16
CORES = 2
PAIRED = 4
LINK_AT = 32
LIST_AT = 64


def near(values):
    return pltpu.with_memory_space_constraint(values, pltpu.VMEM)


def over(values, by):
    return lax.shift_right_logical(values, by.bit_length() - 1) if by & (by - 1) == 0 else values // by


def modulo(values, by):
    return values & (by - 1) if by & (by - 1) == 0 else values % by


def layout(fields, modes, tiles_here):
    extra_at = fields * tiles_here * modes
    extra = pl.cdiv(max(modes, fields, 5), 8) * 8
    return extra_at, extra, extra_at + extra


def split(values):
    high = values.astype(BF16)
    return high, (values - high.astype(F32)).astype(BF16)


def product(both, values):
    parts = jnp.dot(both, values, preferred_element_type=F32)
    height = parts.shape[0] // 2
    return parts[:height] + parts[height:]


def applied_kernel(list_ref, weight_ref, b_ref, j_ref, out_ref, link_ref, lower, upper, applied, shared):
    fields, modes, cells = b_ref.shape
    length = list_ref.shape[1]
    tiles_here = cells // TILE
    height = tiles_here * modes
    extra_at, extra, total_rows = layout(fields, modes, tiles_here)
    wide = lax.broadcasted_iota(jnp.int32, (modes, cells), 1)
    lane = lax.broadcasted_iota(jnp.int32, (modes, TILE), 1)
    edge = jnp.zeros((modes, TILE), F32)
    shared[...] = jnp.zeros(shared.shape, F32)
    for f in range(fields):
        for g in range(fields):
            link_ref[f * fields + g] = j_ref[f, g].astype(F32)
    for g in range(fields):
        values = b_ref[g].astype(F32)
        below = pltpu.roll(values, 1, 1)
        above = pltpu.roll(values, cells - 1, 1)
        edge = jnp.where(lane == 2 * g, values[:, cells - 1 :], edge)
        edge = jnp.where(lane == 2 * g + 1, values[:, 0:1], edge)
        lower[g] = jnp.where(wide == 0, 0.0, below)
        upper[g] = jnp.where(wide == cells - 1, 0.0, above)
    for t in range(tiles_here):
        at = slice(t * TILE, (t + 1) * TILE)
        center = [b_ref[g, :, at].astype(F32) for g in range(fields)]
        below = [lower[g, :, at] for g in range(fields)]
        above = [upper[g, :, at] for g in range(fields)]
        for f in range(fields):
            total = jnp.zeros((modes, TILE), F32)
            for g in range(fields):
                total = total + link_ref[f * fields + g, 0:1, at] * center[g]
                total = total + link_ref[f * fields + g, 1:2, at] * below[g]
                total = total + link_ref[f * fields + g, 2:3, at] * above[g]
            applied[f * height + t * modes : f * height + (t + 1) * modes, :] = total
    out_ref[0 : fields * height, :] = applied[...].astype(BF16)
    lane = lane[0:1]
    rows = []
    for f in range(fields):
        row = jnp.zeros((1, TILE), F32)
        for g in range(fields):
            row = jnp.where(lane == LINK_AT + 2 * g, link_ref[f * fields + g, 1:2, 0:1], row)
            row = jnp.where(lane == LINK_AT + 2 * g + 1, link_ref[f * fields + g, 2:3, cells - 1 :], row)
        rows.append(row)
    shared[0:modes, :] = edge
    shared[0:fields, :] = shared[0:fields, :] + jnp.concatenate(rows, axis=0)
    tiles = list_ref[...]
    device = over(tiles, tiles_here)
    high, low = split(weight_ref[...])
    rest = weight_ref[...] - high.astype(F32) - low.astype(F32)
    rows = [device.astype(F32), (tiles - device * tiles_here).astype(F32), high.astype(F32), low.astype(F32), rest]
    shared[0:5, LIST_AT : LIST_AT + length] = jnp.concatenate(rows, axis=0)
    out_ref[extra_at:total_rows, :] = shared[...].astype(BF16)


def weight_rows(lists, weights, tile, modes, length):
    owners = lists.shape[0]
    width = tile.shape[1]
    total = jnp.zeros((owners, width), F32)
    for entry in range(length):
        total = total + jnp.where(lists[:, entry : entry + 1] == tile, weights[:, entry : entry + 1], 0.0)
    lane = lax.broadcasted_iota(jnp.int32, (modes, width), 1)
    sub = lax.broadcasted_iota(jnp.int32, (modes, width), 0)
    same = modulo(lane, modes) == sub
    return jnp.concatenate([jnp.where(same, total[o : o + 1], 0.0) for o in range(owners)], axis=0)


def rows_kernel(fields, modes, tiles_here, length, devices, paired, *refs):
    parts = refs[:-6]
    rows_ref, square_ref, w_ref, link_ref, extra, edges = refs[-6:]
    chips = devices // CORES
    height = tiles_here * modes
    extra_at, _, _ = layout(fields, modes, tiles_here)
    edge_rows = slice(extra_at, extra_at + edges.shape[2])
    list_rows = slice(extra_at, extra_at + 5)
    me = lax.axis_index("space")
    core = lax.rem(me, CORES)
    chip = lax.div(me, CORES)
    lane = lax.broadcasted_iota(jnp.int32, (modes, TILE), 1)
    first = lane & 1 == 0
    inside = lane < 2 * fields
    kinds = (core, 1 - core)
    sources = []
    for which, kind in enumerate(kinds):
        for q in range(chips):
            if paired:
                sources.append((parts[which * chips + q].at[...], jnp.bitwise_xor(chip, q), which))
            else:
                sources.append((parts[which].at[q], q, which))

    lists, weights = [], []
    for ref, place, which in sources:
        part = pltpu.roll(ref[list_rows, :].astype(F32), TILE - LIST_AT, 1)
        lists.append(part[0:1] * tiles_here + part[1:2])
        weights.append(part[2:3] + part[3:4] + part[4:5])
        edges[which, place] = ref[edge_rows, :].astype(F32)
    lists = jnp.concatenate(lists, axis=0)
    weights = jnp.concatenate(weights, axis=0)

    def coupling(which, place):
        return pltpu.roll(edges[which, place], TILE - LINK_AT, 1)

    def device_of(source, mixed):
        first = source < chips
        place = jnp.where(first, source, source - chips)
        if mixed:
            place = jnp.bitwise_xor(place, chip)
        return CORES * place + jnp.where(first, core, 1 - core)

    inner = devices * height
    total = inner + devices * 2 * modes
    column = lax.broadcasted_iota(jnp.int32, (devices, total), 1)
    outer = column - inner
    tile = jnp.where(
        outer < 0,
        device_of(over(column, height), paired) * tiles_here + modulo(over(column, modes), tiles_here),
        device_of(over(outer, 2 * modes), False) * tiles_here + modulo(over(outer, modes), 2) * (tiles_here - 1),
    )
    matrix = weight_rows(lists, weights, tile.astype(F32), modes, length)
    both = jnp.concatenate(split(matrix), axis=0)

    for index in range(devices):
        which, q = divmod(index, chips)
        kind = kinds[which]
        place = CORES * q + kind
        before = edges[1 - which, jnp.maximum(q - 1 + kind, 0), 0:modes, :]
        after = edges[1 - which, jnp.minimum(q + kind, chips - 1), 0:modes, :]
        before = before * (place > 0).astype(F32)
        after = after * (place < devices - 1).astype(F32)
        links = coupling(which, q)
        near = jnp.where(first, before, after)
        for f in range(fields):
            terms = near * links[f : f + 1]
            left = jnp.sum(jnp.where(first & inside, terms, 0.0), axis=1, keepdims=True)
            right = jnp.sum(jnp.where(first | ~inside, 0.0, terms), axis=1, keepdims=True)
            at = index * 2 * modes
            extra[f, at : at + modes, :] = jnp.where(lane == 0, left, 0.0)
            extra[f, at + modes : at + 2 * modes, :] = jnp.where(lane == TILE - 1, right, 0.0)

    squares = jnp.zeros((devices * modes, TILE), F32)
    for f in range(fields):
        tiles = jnp.concatenate(
            [ref[f * height : (f + 1) * height, :] for ref, _, _ in sources] + [extra[f].astype(BF16)], axis=0
        )
        rows = product(both, tiles)
        rows_ref[f] = rows
        squares = squares + rows * rows
    for o in range(devices):
        square_ref[o : o + 1, :] = jnp.sum(squares[o * modes : (o + 1) * modes], axis=0, keepdims=True)

    column = lax.broadcasted_iota(jnp.int32, (devices, w_ref.shape[1]), 1)
    local = over(column, modes)
    base = me * tiles_here
    tile = jnp.where(local <= tiles_here, base + local, jnp.where(local == tiles_here + 1, base - 1, -2))
    w_ref[...] = weight_rows(lists, weights, tile.astype(F32), modes, length)
    link_ref[0] = coupling(1, jnp.minimum(chip + core, chips - 1))
    link_ref[1] = coupling(1, jnp.maximum(chip - 1 + core, 0))


def update_kernel(samples, w_ref, rows_ref, link_ref, b_ref, j_ref, *rest):
    square_refs = rest[:-4]
    out_ref, returned, lower, upper = rest[-4:]
    fields, modes, cells = b_ref.shape
    tiles_here = cells // TILE
    owners = square_refs[0].shape[0]
    square = square_refs[0][...]
    for ref in square_refs[1:]:
        square = square + ref[...]
    factor = lax.rsqrt(square / samples + EPS)
    factor = jnp.concatenate([jnp.broadcast_to(factor[o : o + 1], (modes, TILE)) for o in range(owners)], axis=0)
    both = jnp.concatenate(split(jnp.transpose(w_ref[...])), axis=0)
    for g in range(fields):
        normalized = (rows_ref[g] * factor).astype(BF16)
        returned[g] = product(both, normalized)
    for t in range(tiles_here):
        at = slice(t * TILE, (t + 1) * TILE)
        values = [returned[g, t * modes : (t + 1) * modes, :] for g in range(fields)]
        for f in range(fields):
            center = b_ref[f, :, at].astype(F32)
            below = jnp.zeros((modes, TILE), F32)
            above = jnp.zeros((modes, TILE), F32)
            for g in range(fields):
                center = center + j_ref[g * fields + f, 0:1, at] * values[g]
                below = below + j_ref[g * fields + f, 1:2, at] * values[g]
                above = above + j_ref[g * fields + f, 2:3, at] * values[g]
            out_ref[f, :, at] = center
            lower[f, :, at] = below
            upper[f, :, at] = above
    wide = lax.broadcasted_iota(jnp.int32, (modes, cells), 1)
    nexts = slice(tiles_here * modes, (tiles_here + 1) * modes)
    lasts = slice((tiles_here + 1) * modes, (tiles_here + 2) * modes)
    for f in range(fields):
        head = jnp.zeros((modes, TILE), F32)
        tail = jnp.zeros((modes, TILE), F32)
        for g in range(fields):
            head = head + link_ref[0, g : g + 1, 2 * f : 2 * f + 1] * returned[g, nexts, :]
            tail = tail + link_ref[1, g : g + 1, 2 * f + 1 : 2 * f + 2] * returned[g, lasts, :]
        below = jnp.where(wide == cells - 1, head[:, 0:1], pltpu.roll(lower[f], cells - 1, 1))
        above = jnp.where(wide == 0, tail[:, TILE - 1 : TILE], pltpu.roll(upper[f], 1, 1))
        out_ref[f] = out_ref[f] + below + above


def shards(basis, jacobian, sample_list, sample_weight):
    space = lax.axis_size("space")
    mode = lax.axis_size("mode")
    modes, fields, cells = basis.shape
    length = sample_list.shape[1]
    tiles_here = cells // TILE
    height = space * modes
    width = pl.cdiv((tiles_here + 2) * modes, TILE) * TILE
    sent_rows = layout(fields, modes, tiles_here)[-1]
    b = jnp.transpose(basis, (1, 0, 2))
    j = jnp.transpose(jacobian, (1, 2, 0, 3))

    sent, wide = pl.pallas_call(
        applied_kernel,
        out_shape=(pltpu.VMEM((sent_rows, TILE), BF16), pltpu.VMEM((fields * fields, 3, cells), F32)),
        scratch_shapes=[
            pltpu.VMEM((fields, modes, cells), F32),
            pltpu.VMEM((fields, modes, cells), F32),
            pltpu.VMEM((fields * tiles_here * modes, TILE), F32),
            pltpu.VMEM((sent_rows - fields * tiles_here * modes, TILE), F32),
        ],
        name="applied",
    )(sample_list, sample_weight, b, j)
    chips = space // CORES
    paired = chips <= PAIRED and chips & (chips - 1) == 0
    if paired:
        parts = [sent] + [
            lax.ppermute(sent, "space", [(i, i ^ (CORES * d)) for i in range(space)]) for d in range(1, chips)
        ]
    else:
        groups = [[core + CORES * q for q in range(chips)] for core in range(CORES)]
        parts = [lax.all_gather(sent, "space", axis=0, axis_index_groups=groups)]
    parts = parts + [lax.ppermute(part, "space", [(i, i ^ 1) for i in range(space)]) for part in parts]

    rows, square, matrix, links = pl.pallas_call(
        functools.partial(rows_kernel, fields, modes, tiles_here, length, space, paired),
        out_shape=(
            pltpu.VMEM((fields, height, TILE), F32),
            pltpu.VMEM((space, TILE), F32),
            pltpu.VMEM((height, width), F32),
            pltpu.VMEM((2, layout(fields, modes, tiles_here)[1], TILE), F32),
        ),
        scratch_shapes=[
            pltpu.VMEM((fields, space * 2 * modes, TILE), F32),
            pltpu.VMEM((CORES, chips, layout(fields, modes, tiles_here)[1], TILE), F32),
        ],
        name="rows",
    )(*(near(part) for part in parts))
    ring = list(range(0, mode, 2))[:1] + list(range(1, mode, 2)) + list(range(0, mode, 2))[:0:-1]
    squares = [square] + [
        lax.ppermute(square, "mode", [(ring[i], ring[(i + step) % mode]) for i in range(mode)])
        for step in range(mode - 1, 0, -1)
    ]

    update = pl.pallas_call(
        functools.partial(update_kernel, mode * modes * fields),
        out_shape=jax.ShapeDtypeStruct((fields, modes, cells), F32),
        scratch_shapes=[
            pltpu.VMEM((fields, width, TILE), F32),
            pltpu.VMEM((fields, modes, cells), F32),
            pltpu.VMEM((fields, modes, cells), F32),
        ],
        name="update",
    )(*(near(x) for x in (matrix, rows, links, b, wide, *squares)))
    return jnp.transpose(update, (1, 0, 2))


def solution(mesh):
    placed = (
        P("mode", None, "space"),
        P(None, None, None, "space"),
        P("space", None),
        P("space", None),
    )
    return jax.shard_map(
        shards, mesh=mesh, in_specs=placed, out_specs=P("mode", None, "space"), check_vma=False
    )
```

```python
import functools
import jax
import jax.numpy as jnp
from jax import lax
from jax.experimental import pallas as pl
from jax.experimental.pallas import tpu as pltpu
from jax.sharding import PartitionSpec as P

TILE = 128
EPS = 1e-05
F32 = jnp.float32
BF16 = jnp.bfloat16
CORES = 2
RINGS = (1, 2, 4)
LINK_AT = 32
LIST_AT = 64


def near(values):
    return pltpu.with_memory_space_constraint(values, pltpu.VMEM)


def over(values, by):
    return lax.shift_right_logical(values, by.bit_length() - 1) if by & (by - 1) == 0 else values // by


def modulo(values, by):
    return values & (by - 1) if by & (by - 1) == 0 else values % by


def gray(value):
    return value ^ (value >> 1)


def layout(fields, modes, tiles_here):
    extra_at = fields * tiles_here * modes
    extra = pl.cdiv(max(modes, fields, 5), 8) * 8
    return extra_at, extra, extra_at + extra


def split(values):
    high = values.astype(BF16)
    return high, (values - high.astype(F32)).astype(BF16)


def product(both, values):
    parts = jnp.dot(both, values, preferred_element_type=F32)
    height = parts.shape[0] // 2
    return parts[:height] + parts[height:]


def applied_kernel(list_ref, weight_ref, b_ref, j_ref, out_ref, link_ref, lower, upper, applied, shared):
    fields, modes, cells = b_ref.shape
    length = list_ref.shape[1]
    tiles_here = cells // TILE
    height = tiles_here * modes
    extra_at, extra, total_rows = layout(fields, modes, tiles_here)
    wide = lax.broadcasted_iota(jnp.int32, (modes, cells), 1)
    lane = lax.broadcasted_iota(jnp.int32, (modes, TILE), 1)
    edge = jnp.zeros((modes, TILE), F32)
    shared[...] = jnp.zeros(shared.shape, F32)
    for f in range(fields):
        for g in range(fields):
            link_ref[f * fields + g] = j_ref[f, g].astype(F32)
    for g in range(fields):
        values = b_ref[g].astype(F32)
        below = pltpu.roll(values, 1, 1)
        above = pltpu.roll(values, cells - 1, 1)
        edge = jnp.where(lane == 2 * g, values[:, cells - 1 :], edge)
        edge = jnp.where(lane == 2 * g + 1, values[:, 0:1], edge)
        lower[g] = jnp.where(wide == 0, 0.0, below)
        upper[g] = jnp.where(wide == cells - 1, 0.0, above)
    for t in range(tiles_here):
        at = slice(t * TILE, (t + 1) * TILE)
        center = [b_ref[g, :, at].astype(F32) for g in range(fields)]
        below = [lower[g, :, at] for g in range(fields)]
        above = [upper[g, :, at] for g in range(fields)]
        for f in range(fields):
            total = jnp.zeros((modes, TILE), F32)
            for g in range(fields):
                total = total + link_ref[f * fields + g, 0:1, at] * center[g]
                total = total + link_ref[f * fields + g, 1:2, at] * below[g]
                total = total + link_ref[f * fields + g, 2:3, at] * above[g]
            applied[f * height + t * modes : f * height + (t + 1) * modes, :] = total
    out_ref[0 : fields * height, :] = applied[...].astype(BF16)
    lane = lane[0:1]
    rows = []
    for f in range(fields):
        row = jnp.zeros((1, TILE), F32)
        for g in range(fields):
            row = jnp.where(lane == LINK_AT + 2 * g, link_ref[f * fields + g, 1:2, 0:1], row)
            row = jnp.where(lane == LINK_AT + 2 * g + 1, link_ref[f * fields + g, 2:3, cells - 1 :], row)
        rows.append(row)
    shared[0:modes, :] = edge
    shared[0:fields, :] = shared[0:fields, :] + jnp.concatenate(rows, axis=0)
    tiles = list_ref[...]
    device = over(tiles, tiles_here)
    high, low = split(weight_ref[...])
    rest = weight_ref[...] - high.astype(F32) - low.astype(F32)
    rows = [device.astype(F32), (tiles - device * tiles_here).astype(F32), high.astype(F32), low.astype(F32), rest]
    shared[0:5, LIST_AT : LIST_AT + length] = jnp.concatenate(rows, axis=0)
    out_ref[extra_at:total_rows, :] = shared[...].astype(BF16)


def weight_rows(lists, weights, tile, modes, length):
    owners = lists.shape[0]
    width = tile.shape[1]
    total = jnp.zeros((owners, width), F32)
    for entry in range(length):
        total = total + jnp.where(lists[:, entry : entry + 1] == tile, weights[:, entry : entry + 1], 0.0)
    lane = lax.broadcasted_iota(jnp.int32, (modes, width), 1)
    sub = lax.broadcasted_iota(jnp.int32, (modes, width), 0)
    same = modulo(lane, modes) == sub
    return jnp.concatenate([jnp.where(same, total[o : o + 1], 0.0) for o in range(owners)], axis=0)


def rows_kernel(fields, modes, tiles_here, length, devices, paired, *refs):
    parts = refs[:-6]
    rows_ref, square_ref, w_ref, link_ref, extra, edges = refs[-6:]
    chips = devices // CORES
    height = tiles_here * modes
    extra_at, _, _ = layout(fields, modes, tiles_here)
    edge_rows = slice(extra_at, extra_at + edges.shape[2])
    list_rows = slice(extra_at, extra_at + 5)
    me = lax.axis_index("space")
    core = lax.rem(me, CORES)
    chip = lax.div(me, CORES)
    lane = lax.broadcasted_iota(jnp.int32, (modes, TILE), 1)
    first = lane & 1 == 0
    inside = lane < 2 * fields
    kinds = (core, 1 - core)
    sources = []
    for which, kind in enumerate(kinds):
        for q in range(chips):
            if paired:
                sources.append((parts[which * chips + q].at[...], gray(modulo(gray(chip) - gray(q) + chips, chips)), which))
            else:
                sources.append((parts[which].at[q], q, which))

    lists, weights = [], []
    for ref, place, which in sources:
        part = pltpu.roll(ref[list_rows, :].astype(F32), TILE - LIST_AT, 1)
        lists.append(part[0:1] * tiles_here + part[1:2])
        weights.append(part[2:3] + part[3:4] + part[4:5])
        edges[which, place] = ref[edge_rows, :].astype(F32)
    lists = jnp.concatenate(lists, axis=0)
    weights = jnp.concatenate(weights, axis=0)

    def coupling(which, place):
        return pltpu.roll(edges[which, place], TILE - LINK_AT, 1)

    def device_of(source, mixed):
        first = source < chips
        place = jnp.where(first, source, source - chips)
        if mixed:
            place = gray(modulo(gray(chip) - gray(place) + chips, chips))
        return CORES * place + jnp.where(first, core, 1 - core)

    inner = devices * height
    total = inner + devices * 2 * modes
    column = lax.broadcasted_iota(jnp.int32, (devices, total), 1)
    outer = column - inner
    tile = jnp.where(
        outer < 0,
        device_of(over(column, height), paired) * tiles_here + modulo(over(column, modes), tiles_here),
        device_of(over(outer, 2 * modes), False) * tiles_here + modulo(over(outer, modes), 2) * (tiles_here - 1),
    )
    matrix = weight_rows(lists, weights, tile.astype(F32), modes, length)
    both = jnp.concatenate(split(matrix), axis=0)

    for index in range(devices):
        which, q = divmod(index, chips)
        kind = kinds[which]
        place = CORES * q + kind
        before = edges[1 - which, jnp.maximum(q - 1 + kind, 0), 0:modes, :]
        after = edges[1 - which, jnp.minimum(q + kind, chips - 1), 0:modes, :]
        before = before * (place > 0).astype(F32)
        after = after * (place < devices - 1).astype(F32)
        links = coupling(which, q)
        near = jnp.where(first, before, after)
        for f in range(fields):
            terms = near * links[f : f + 1]
            left = jnp.sum(jnp.where(first & inside, terms, 0.0), axis=1, keepdims=True)
            right = jnp.sum(jnp.where(first | ~inside, 0.0, terms), axis=1, keepdims=True)
            at = index * 2 * modes
            extra[f, at : at + modes, :] = jnp.where(lane == 0, left, 0.0)
            extra[f, at + modes : at + 2 * modes, :] = jnp.where(lane == TILE - 1, right, 0.0)

    squares = jnp.zeros((devices * modes, TILE), F32)
    for f in range(fields):
        tiles = jnp.concatenate(
            [ref[f * height : (f + 1) * height, :] for ref, _, _ in sources] + [extra[f].astype(BF16)], axis=0
        )
        rows = product(both, tiles)
        rows_ref[f] = rows
        squares = squares + rows * rows
    for o in range(devices):
        square_ref[o : o + 1, :] = jnp.sum(squares[o * modes : (o + 1) * modes], axis=0, keepdims=True)

    column = lax.broadcasted_iota(jnp.int32, (devices, w_ref.shape[1]), 1)
    local = over(column, modes)
    base = me * tiles_here
    tile = jnp.where(local <= tiles_here, base + local, jnp.where(local == tiles_here + 1, base - 1, -2))
    w_ref[...] = weight_rows(lists, weights, tile.astype(F32), modes, length)
    link_ref[0] = coupling(1, jnp.minimum(chip + core, chips - 1))
    link_ref[1] = coupling(1, jnp.maximum(chip - 1 + core, 0))


def update_kernel(samples, w_ref, rows_ref, link_ref, b_ref, j_ref, *rest):
    square_refs = rest[:-4]
    out_ref, returned, lower, upper = rest[-4:]
    fields, modes, cells = b_ref.shape
    tiles_here = cells // TILE
    owners = square_refs[0].shape[0]
    square = square_refs[0][...]
    for ref in square_refs[1:]:
        square = square + ref[...]
    factor = lax.rsqrt(square / samples + EPS)
    factor = jnp.concatenate([jnp.broadcast_to(factor[o : o + 1], (modes, TILE)) for o in range(owners)], axis=0)
    both = jnp.concatenate(split(jnp.transpose(w_ref[...])), axis=0)
    for g in range(fields):
        normalized = (rows_ref[g] * factor).astype(BF16)
        returned[g] = product(both, normalized)
    for t in range(tiles_here):
        at = slice(t * TILE, (t + 1) * TILE)
        values = [returned[g, t * modes : (t + 1) * modes, :] for g in range(fields)]
        for f in range(fields):
            center = b_ref[f, :, at].astype(F32)
            below = jnp.zeros((modes, TILE), F32)
            above = jnp.zeros((modes, TILE), F32)
            for g in range(fields):
                center = center + j_ref[g * fields + f, 0:1, at] * values[g]
                below = below + j_ref[g * fields + f, 1:2, at] * values[g]
                above = above + j_ref[g * fields + f, 2:3, at] * values[g]
            out_ref[f, :, at] = center
            lower[f, :, at] = below
            upper[f, :, at] = above
    wide = lax.broadcasted_iota(jnp.int32, (modes, cells), 1)
    nexts = slice(tiles_here * modes, (tiles_here + 1) * modes)
    lasts = slice((tiles_here + 1) * modes, (tiles_here + 2) * modes)
    for f in range(fields):
        head = jnp.zeros((modes, TILE), F32)
        tail = jnp.zeros((modes, TILE), F32)
        for g in range(fields):
            head = head + link_ref[0, g : g + 1, 2 * f : 2 * f + 1] * returned[g, nexts, :]
            tail = tail + link_ref[1, g : g + 1, 2 * f + 1 : 2 * f + 2] * returned[g, lasts, :]
        below = jnp.where(wide == cells - 1, head[:, 0:1], pltpu.roll(lower[f], cells - 1, 1))
        above = jnp.where(wide == 0, tail[:, TILE - 1 : TILE], pltpu.roll(upper[f], 1, 1))
        out_ref[f] = out_ref[f] + below + above


def shards(basis, jacobian, sample_list, sample_weight):
    space = lax.axis_size("space")
    mode = lax.axis_size("mode")
    modes, fields, cells = basis.shape
    length = sample_list.shape[1]
    tiles_here = cells // TILE
    height = space * modes
    width = pl.cdiv((tiles_here + 2) * modes, TILE) * TILE
    sent_rows = layout(fields, modes, tiles_here)[-1]
    b = jnp.transpose(basis, (1, 0, 2))
    j = jnp.transpose(jacobian, (1, 2, 0, 3))

    sent, wide = pl.pallas_call(
        applied_kernel,
        out_shape=(pltpu.VMEM((sent_rows, TILE), BF16), pltpu.VMEM((fields * fields, 3, cells), F32)),
        scratch_shapes=[
            pltpu.VMEM((fields, modes, cells), F32),
            pltpu.VMEM((fields, modes, cells), F32),
            pltpu.VMEM((fields * tiles_here * modes, TILE), F32),
            pltpu.VMEM((sent_rows - fields * tiles_here * modes, TILE), F32),
        ],
        name="applied",
    )(sample_list, sample_weight, b, j)
    chips = space // CORES
    paired = chips in RINGS
    if paired:
        parts = [sent]
        for q in range(1, chips):
            ahead = [gray((gray(i) + gray(q)) % chips) for i in range(chips)]
            route = [(i, CORES * ahead[i // CORES] + i % CORES) for i in range(space)]
            parts.append(lax.ppermute(sent, "space", route))
    else:
        groups = [[core + CORES * q for q in range(chips)] for core in range(CORES)]
        parts = [lax.all_gather(sent, "space", axis=0, axis_index_groups=groups)]
    parts = parts + [lax.ppermute(part, "space", [(i, i ^ 1) for i in range(space)]) for part in parts]

    rows, square, matrix, links = pl.pallas_call(
        functools.partial(rows_kernel, fields, modes, tiles_here, length, space, paired),
        out_shape=(
            pltpu.VMEM((fields, height, TILE), F32),
            pltpu.VMEM((space, TILE), F32),
            pltpu.VMEM((height, width), F32),
            pltpu.VMEM((2, layout(fields, modes, tiles_here)[1], TILE), F32),
        ),
        scratch_shapes=[
            pltpu.VMEM((fields, space * 2 * modes, TILE), F32),
            pltpu.VMEM((CORES, chips, layout(fields, modes, tiles_here)[1], TILE), F32),
        ],
        name="rows",
    )(*(near(part) for part in parts))
    ring = list(range(0, mode, 2))[:1] + list(range(1, mode, 2)) + list(range(0, mode, 2))[:0:-1]
    squares = [square] + [
        lax.ppermute(square, "mode", [(ring[i], ring[(i + step) % mode]) for i in range(mode)])
        for step in range(mode - 1, 0, -1)
    ]

    update = pl.pallas_call(
        functools.partial(update_kernel, mode * modes * fields),
        out_shape=jax.ShapeDtypeStruct((fields, modes, cells), F32),
        scratch_shapes=[
            pltpu.VMEM((fields, width, TILE), F32),
            pltpu.VMEM((fields, modes, cells), F32),
            pltpu.VMEM((fields, modes, cells), F32),
        ],
        name="update",
    )(*(near(x) for x in (matrix, rows, links, b, wide, *squares)))
    return jnp.transpose(update, (1, 0, 2))


def solution(mesh):
    placed = (
        P("mode", None, "space"),
        P(None, None, None, "space"),
        P("space", None),
        P("space", None),
    )
    return jax.shard_map(
        shards, mesh=mesh, in_specs=placed, out_specs=P("mode", None, "space"), check_vma=False
    )
```

```python
import functools
import jax
import jax.numpy as jnp
from jax import lax
from jax.experimental import pallas as pl
from jax.experimental.pallas import tpu as pltpu
from jax.sharding import PartitionSpec as P

TILE = 128
EPS = 1e-05
F32 = jnp.float32
BF16 = jnp.bfloat16
CORES = 2
PAIRED = 4
LINK_AT = 32
LIST_AT = 64


def near(values):
    return pltpu.with_memory_space_constraint(values, pltpu.VMEM)


def over(values, by):
    return lax.shift_right_logical(values, by.bit_length() - 1) if by & (by - 1) == 0 else values // by


def modulo(values, by):
    return values & (by - 1) if by & (by - 1) == 0 else values % by


def layout(fields, modes, tiles_here):
    extra_at = fields * tiles_here * modes
    extra = pl.cdiv(max(modes, fields, 5), 8) * 8
    return extra_at, extra, extra_at + extra


def split(values):
    high = values.astype(BF16)
    return high, (values - high.astype(F32)).astype(BF16)


def product(both, values):
    parts = jnp.dot(both, values, preferred_element_type=F32)
    height = parts.shape[0] // 2
    return parts[:height] + parts[height:]


def applied_kernel(
    list_hbm,
    weight_hbm,
    b_hbm,
    j_hbm,
    out_ref,
    link_ref,
    list_ref,
    weight_ref,
    b_ref,
    j_ref,
    lower,
    upper,
    applied,
    shared,
    sems,
):
    fields, modes, cells = b_ref.shape
    basis_in = [pltpu.make_async_copy(b_hbm.at[g], b_ref.at[g], sems.at[g]) for g in range(fields)]
    links_in = [pltpu.make_async_copy(j_hbm.at[f], j_ref.at[f], sems.at[fields + f]) for f in range(fields)]
    list_in = pltpu.make_async_copy(list_hbm, list_ref, sems.at[2 * fields])
    weight_in = pltpu.make_async_copy(weight_hbm, weight_ref, sems.at[2 * fields + 1])
    for copy in basis_in + links_in + [list_in, weight_in]:
        copy.start()
    length = list_ref.shape[1]
    tiles_here = cells // TILE
    height = tiles_here * modes
    extra_at, extra, total_rows = layout(fields, modes, tiles_here)
    wide = lax.broadcasted_iota(jnp.int32, (modes, cells), 1)
    lane = lax.broadcasted_iota(jnp.int32, (modes, TILE), 1)
    edge = jnp.zeros((modes, TILE), F32)
    shared[...] = jnp.zeros(shared.shape, F32)
    for g in range(fields):
        basis_in[g].wait()
        values = b_ref[g].astype(F32)
        below = pltpu.roll(values, 1, 1)
        above = pltpu.roll(values, cells - 1, 1)
        edge = jnp.where(lane == 2 * g, values[:, cells - 1 :], edge)
        edge = jnp.where(lane == 2 * g + 1, values[:, 0:1], edge)
        lower[g] = jnp.where(wide == 0, 0.0, below)
        upper[g] = jnp.where(wide == cells - 1, 0.0, above)
    for f in range(fields):
        links_in[f].wait()
        for g in range(fields):
            link_ref[f * fields + g] = j_ref[f, g].astype(F32)
    for t in range(tiles_here):
        at = slice(t * TILE, (t + 1) * TILE)
        center = [b_ref[g, :, at].astype(F32) for g in range(fields)]
        below = [lower[g, :, at] for g in range(fields)]
        above = [upper[g, :, at] for g in range(fields)]
        for f in range(fields):
            total = jnp.zeros((modes, TILE), F32)
            for g in range(fields):
                total = total + link_ref[f * fields + g, 0:1, at] * center[g]
                total = total + link_ref[f * fields + g, 1:2, at] * below[g]
                total = total + link_ref[f * fields + g, 2:3, at] * above[g]
            applied[f * height + t * modes : f * height + (t + 1) * modes, :] = total
    out_ref[0 : fields * height, :] = applied[...].astype(BF16)
    lane = lane[0:1]
    rows = []
    for f in range(fields):
        row = jnp.zeros((1, TILE), F32)
        for g in range(fields):
            row = jnp.where(lane == LINK_AT + 2 * g, link_ref[f * fields + g, 1:2, 0:1], row)
            row = jnp.where(lane == LINK_AT + 2 * g + 1, link_ref[f * fields + g, 2:3, cells - 1 :], row)
        rows.append(row)
    shared[0:modes, :] = edge
    shared[0:fields, :] = shared[0:fields, :] + jnp.concatenate(rows, axis=0)
    list_in.wait()
    weight_in.wait()
    tiles = list_ref[...]
    device = over(tiles, tiles_here)
    high, low = split(weight_ref[...])
    rest = weight_ref[...] - high.astype(F32) - low.astype(F32)
    rows = [device.astype(F32), (tiles - device * tiles_here).astype(F32), high.astype(F32), low.astype(F32), rest]
    shared[0:5, LIST_AT : LIST_AT + length] = jnp.concatenate(rows, axis=0)
    out_ref[extra_at:total_rows, :] = shared[...].astype(BF16)


def weight_rows(lists, weights, tile, modes, length):
    owners = lists.shape[0]
    width = tile.shape[1]
    total = jnp.zeros((owners, width), F32)
    for entry in range(length):
        total = total + jnp.where(lists[:, entry : entry + 1] == tile, weights[:, entry : entry + 1], 0.0)
    lane = lax.broadcasted_iota(jnp.int32, (modes, width), 1)
    sub = lax.broadcasted_iota(jnp.int32, (modes, width), 0)
    same = modulo(lane, modes) == sub
    return jnp.concatenate([jnp.where(same, total[o : o + 1], 0.0) for o in range(owners)], axis=0)


def rows_kernel(fields, modes, tiles_here, length, devices, paired, *refs):
    parts = refs[:-6]
    rows_ref, square_ref, w_ref, link_ref, extra, edges = refs[-6:]
    chips = devices // CORES
    height = tiles_here * modes
    extra_at, _, _ = layout(fields, modes, tiles_here)
    edge_rows = slice(extra_at, extra_at + edges.shape[2])
    list_rows = slice(extra_at, extra_at + 5)
    me = lax.axis_index("space")
    core = lax.rem(me, CORES)
    chip = lax.div(me, CORES)
    lane = lax.broadcasted_iota(jnp.int32, (modes, TILE), 1)
    first = lane & 1 == 0
    inside = lane < 2 * fields
    kinds = (core, 1 - core)
    sources = []
    for which, kind in enumerate(kinds):
        for q in range(chips):
            if paired:
                sources.append((parts[which * chips + q].at[...], jnp.bitwise_xor(chip, q), which))
            else:
                sources.append((parts[which].at[q], q, which))

    lists, weights = [], []
    for ref, place, which in sources:
        part = pltpu.roll(ref[list_rows, :].astype(F32), TILE - LIST_AT, 1)
        lists.append(part[0:1] * tiles_here + part[1:2])
        weights.append(part[2:3] + part[3:4] + part[4:5])
        edges[which, place] = ref[edge_rows, :].astype(F32)
    lists = jnp.concatenate(lists, axis=0)
    weights = jnp.concatenate(weights, axis=0)

    def coupling(which, place):
        return pltpu.roll(edges[which, place], TILE - LINK_AT, 1)

    def device_of(source, mixed):
        first = source < chips
        place = jnp.where(first, source, source - chips)
        if mixed:
            place = jnp.bitwise_xor(place, chip)
        return CORES * place + jnp.where(first, core, 1 - core)

    inner = devices * height
    total = inner + devices * 2 * modes
    column = lax.broadcasted_iota(jnp.int32, (devices, total), 1)
    outer = column - inner
    tile = jnp.where(
        outer < 0,
        device_of(over(column, height), paired) * tiles_here + modulo(over(column, modes), tiles_here),
        device_of(over(outer, 2 * modes), False) * tiles_here + modulo(over(outer, modes), 2) * (tiles_here - 1),
    )
    matrix = weight_rows(lists, weights, tile.astype(F32), modes, length)
    both = jnp.concatenate(split(matrix), axis=0)

    for index in range(devices):
        which, q = divmod(index, chips)
        kind = kinds[which]
        place = CORES * q + kind
        before = edges[1 - which, jnp.maximum(q - 1 + kind, 0), 0:modes, :]
        after = edges[1 - which, jnp.minimum(q + kind, chips - 1), 0:modes, :]
        before = before * (place > 0).astype(F32)
        after = after * (place < devices - 1).astype(F32)
        links = coupling(which, q)
        near = jnp.where(first, before, after)
        for f in range(fields):
            terms = near * links[f : f + 1]
            left = jnp.sum(jnp.where(first & inside, terms, 0.0), axis=1, keepdims=True)
            right = jnp.sum(jnp.where(first | ~inside, 0.0, terms), axis=1, keepdims=True)
            at = index * 2 * modes
            extra[f, at : at + modes, :] = jnp.where(lane == 0, left, 0.0)
            extra[f, at + modes : at + 2 * modes, :] = jnp.where(lane == TILE - 1, right, 0.0)

    squares = jnp.zeros((devices * modes, TILE), F32)
    for f in range(fields):
        tiles = jnp.concatenate(
            [ref[f * height : (f + 1) * height, :] for ref, _, _ in sources] + [extra[f].astype(BF16)], axis=0
        )
        rows = product(both, tiles)
        rows_ref[f] = rows
        squares = squares + rows * rows
    for o in range(devices):
        square_ref[o : o + 1, :] = jnp.sum(squares[o * modes : (o + 1) * modes], axis=0, keepdims=True)

    column = lax.broadcasted_iota(jnp.int32, (devices, w_ref.shape[1]), 1)
    local = over(column, modes)
    base = me * tiles_here
    tile = jnp.where(local <= tiles_here, base + local, jnp.where(local == tiles_here + 1, base - 1, -2))
    w_ref[...] = weight_rows(lists, weights, tile.astype(F32), modes, length)
    link_ref[0] = coupling(1, jnp.minimum(chip + core, chips - 1))
    link_ref[1] = coupling(1, jnp.maximum(chip - 1 + core, 0))


def update_kernel(samples, w_ref, rows_ref, link_ref, b_ref, j_ref, *rest):
    square_refs = rest[:-6]
    out_hbm, returned, lower, upper, out_ref, sems = rest[-6:]
    fields, modes, cells = b_ref.shape
    tiles_here = cells // TILE
    owners = square_refs[0].shape[0]
    square = square_refs[0][...]
    for ref in square_refs[1:]:
        square = square + ref[...]
    factor = lax.rsqrt(square / samples + EPS)
    factor = jnp.concatenate([jnp.broadcast_to(factor[o : o + 1], (modes, TILE)) for o in range(owners)], axis=0)
    both = jnp.concatenate(split(jnp.transpose(w_ref[...])), axis=0)
    for g in range(fields):
        normalized = (rows_ref[g] * factor).astype(BF16)
        returned[g] = product(both, normalized)
    for t in range(tiles_here):
        at = slice(t * TILE, (t + 1) * TILE)
        values = [returned[g, t * modes : (t + 1) * modes, :] for g in range(fields)]
        for f in range(fields):
            center = b_ref[f, :, at].astype(F32)
            below = jnp.zeros((modes, TILE), F32)
            above = jnp.zeros((modes, TILE), F32)
            for g in range(fields):
                center = center + j_ref[g * fields + f, 0:1, at] * values[g]
                below = below + j_ref[g * fields + f, 1:2, at] * values[g]
                above = above + j_ref[g * fields + f, 2:3, at] * values[g]
            out_ref[f, :, at] = center
            lower[f, :, at] = below
            upper[f, :, at] = above
    wide = lax.broadcasted_iota(jnp.int32, (modes, cells), 1)
    nexts = slice(tiles_here * modes, (tiles_here + 1) * modes)
    lasts = slice((tiles_here + 1) * modes, (tiles_here + 2) * modes)
    copies = []
    for f in range(fields):
        head = jnp.zeros((modes, TILE), F32)
        tail = jnp.zeros((modes, TILE), F32)
        for g in range(fields):
            head = head + link_ref[0, g : g + 1, 2 * f : 2 * f + 1] * returned[g, nexts, :]
            tail = tail + link_ref[1, g : g + 1, 2 * f + 1 : 2 * f + 2] * returned[g, lasts, :]
        below = jnp.where(wide == cells - 1, head[:, 0:1], pltpu.roll(lower[f], cells - 1, 1))
        above = jnp.where(wide == 0, tail[:, TILE - 1 : TILE], pltpu.roll(upper[f], 1, 1))
        out_ref[f] = out_ref[f] + below + above
        copies.append(pltpu.make_async_copy(out_ref.at[f], out_hbm.at[f], sems.at[f]))
        copies[f].start()
    for copy in copies:
        copy.wait()


def shards(basis, jacobian, sample_list, sample_weight):
    space = lax.axis_size("space")
    mode = lax.axis_size("mode")
    modes, fields, cells = basis.shape
    length = sample_list.shape[1]
    tiles_here = cells // TILE
    height = space * modes
    width = pl.cdiv((tiles_here + 2) * modes, TILE) * TILE
    sent_rows = layout(fields, modes, tiles_here)[-1]
    b = jnp.transpose(basis, (1, 0, 2))
    j = jnp.transpose(jacobian, (1, 2, 0, 3))

    sent, wide = pl.pallas_call(
        applied_kernel,
        out_shape=(pltpu.VMEM((sent_rows, TILE), BF16), pltpu.VMEM((fields * fields, 3, cells), F32)),
        in_specs=[pl.BlockSpec(memory_space=pl.ANY)] * 4,
        scratch_shapes=[
            pltpu.VMEM(sample_list.shape, sample_list.dtype),
            pltpu.VMEM(sample_weight.shape, F32),
            pltpu.VMEM(b.shape, BF16),
            pltpu.VMEM(j.shape, BF16),
            pltpu.VMEM((fields, modes, cells), F32),
            pltpu.VMEM((fields, modes, cells), F32),
            pltpu.VMEM((fields * tiles_here * modes, TILE), F32),
            pltpu.VMEM((sent_rows - fields * tiles_here * modes, TILE), F32),
            pltpu.SemaphoreType.DMA((2 * fields + 2,)),
        ],
        name="applied",
    )(sample_list, sample_weight, b, j)
    chips = space // CORES
    paired = chips <= PAIRED and chips & (chips - 1) == 0
    if paired:
        parts = [sent] + [
            lax.ppermute(sent, "space", [(i, i ^ (CORES * d)) for i in range(space)]) for d in range(1, chips)
        ]
    else:
        groups = [[core + CORES * q for q in range(chips)] for core in range(CORES)]
        parts = [lax.all_gather(sent, "space", axis=0, axis_index_groups=groups)]
    parts = parts + [lax.ppermute(part, "space", [(i, i ^ 1) for i in range(space)]) for part in parts]

    rows, square, matrix, links = pl.pallas_call(
        functools.partial(rows_kernel, fields, modes, tiles_here, length, space, paired),
        out_shape=(
            pltpu.VMEM((fields, height, TILE), F32),
            pltpu.VMEM((space, TILE), F32),
            pltpu.VMEM((height, width), F32),
            pltpu.VMEM((2, layout(fields, modes, tiles_here)[1], TILE), F32),
        ),
        scratch_shapes=[
            pltpu.VMEM((fields, space * 2 * modes, TILE), F32),
            pltpu.VMEM((CORES, chips, layout(fields, modes, tiles_here)[1], TILE), F32),
        ],
        name="rows",
    )(*(near(part) for part in parts))
    ring = list(range(0, mode, 2))[:1] + list(range(1, mode, 2)) + list(range(0, mode, 2))[:0:-1]
    squares = [square] + [
        lax.ppermute(square, "mode", [(ring[i], ring[(i + step) % mode]) for i in range(mode)])
        for step in range(mode - 1, 0, -1)
    ]

    update = pl.pallas_call(
        functools.partial(update_kernel, mode * modes * fields),
        out_shape=jax.ShapeDtypeStruct((fields, modes, cells), F32),
        out_specs=pl.BlockSpec(memory_space=pl.ANY),
        scratch_shapes=[
            pltpu.VMEM((fields, width, TILE), F32),
            pltpu.VMEM((fields, modes, cells), F32),
            pltpu.VMEM((fields, modes, cells), F32),
            pltpu.VMEM((fields, modes, cells), F32),
            pltpu.SemaphoreType.DMA((fields,)),
        ],
        name="update",
    )(*(near(x) for x in (matrix, rows, links, b, wide, *squares)))
    return jnp.transpose(update, (1, 0, 2))


def solution(mesh):
    placed = (
        P("mode", None, "space"),
        P(None, None, None, "space"),
        P("space", None),
        P("space", None),
    )
    return jax.shard_map(
        shards, mesh=mesh, in_specs=placed, out_specs=P("mode", None, "space"), check_vma=False
    )
```

```python
import functools
import jax
import jax.numpy as jnp
from jax import lax
from jax.experimental import pallas as pl
from jax.experimental.pallas import tpu as pltpu
from jax.sharding import PartitionSpec as P

TILE = 128
EPS = 1e-05
F32 = jnp.float32
BF16 = jnp.bfloat16
CORES = 2
PAIRED = 4
LINK_AT = 32
LIST_AT = 64


def near(values):
    return pltpu.with_memory_space_constraint(values, pltpu.VMEM)


def over(values, by):
    return lax.shift_right_logical(values, by.bit_length() - 1) if by & (by - 1) == 0 else values // by


def modulo(values, by):
    return values & (by - 1) if by & (by - 1) == 0 else values % by


def layout(fields, modes, tiles_here):
    extra_at = fields * tiles_here * modes
    extra = pl.cdiv(max(modes, fields, 5), 8) * 8
    return extra_at, extra, extra_at + extra


def split(values):
    high = values.astype(BF16)
    return high, (values - high.astype(F32)).astype(BF16)


def product(both, values):
    parts = jnp.dot(both, values, preferred_element_type=F32)
    height = parts.shape[0] // 2
    return parts[:height] + parts[height:]


def applied_kernel(list_ref, weight_ref, b_ref, j_ref, out_ref, link_ref, lower, upper, applied, shared):
    fields, modes, cells = b_ref.shape
    length = list_ref.shape[1]
    tiles_here = cells // TILE
    height = tiles_here * modes
    extra_at, extra, total_rows = layout(fields, modes, tiles_here)
    wide = lax.broadcasted_iota(jnp.int32, (modes, cells), 1)
    lane = lax.broadcasted_iota(jnp.int32, (modes, TILE), 1)
    edge = jnp.zeros((modes, TILE), F32)
    shared[...] = jnp.zeros(shared.shape, F32)
    for f in range(fields):
        for g in range(fields):
            link_ref[f * fields + g] = j_ref[f, g].astype(F32)
    for g in range(fields):
        values = b_ref[g].astype(F32)
        below = pltpu.roll(values, 1, 1)
        above = pltpu.roll(values, cells - 1, 1)
        edge = jnp.where(lane == 2 * g, values[:, cells - 1 :], edge)
        edge = jnp.where(lane == 2 * g + 1, values[:, 0:1], edge)
        lower[g] = jnp.where(wide == 0, 0.0, below)
        upper[g] = jnp.where(wide == cells - 1, 0.0, above)
    for t in range(tiles_here):
        at = slice(t * TILE, (t + 1) * TILE)
        center = [b_ref[g, :, at].astype(F32) for g in range(fields)]
        below = [lower[g, :, at] for g in range(fields)]
        above = [upper[g, :, at] for g in range(fields)]
        for f in range(fields):
            total = jnp.zeros((modes, TILE), F32)
            for g in range(fields):
                total = total + link_ref[f * fields + g, 0:1, at] * center[g]
                total = total + link_ref[f * fields + g, 1:2, at] * below[g]
                total = total + link_ref[f * fields + g, 2:3, at] * above[g]
            applied[f * height + t * modes : f * height + (t + 1) * modes, :] = total
    out_ref[0 : fields * height, :] = applied[...].astype(BF16)
    lane = lane[0:1]
    rows = []
    for f in range(fields):
        row = jnp.zeros((1, TILE), F32)
        for g in range(fields):
            row = jnp.where(lane == LINK_AT + 2 * g, link_ref[f * fields + g, 1:2, 0:1], row)
            row = jnp.where(lane == LINK_AT + 2 * g + 1, link_ref[f * fields + g, 2:3, cells - 1 :], row)
        rows.append(row)
    shared[0:modes, :] = edge
    shared[0:fields, :] = shared[0:fields, :] + jnp.concatenate(rows, axis=0)
    tiles = list_ref[...]
    device = over(tiles, tiles_here)
    high, low = split(weight_ref[...])
    rest = weight_ref[...] - high.astype(F32) - low.astype(F32)
    rows = [device.astype(F32), (tiles - device * tiles_here).astype(F32), high.astype(F32), low.astype(F32), rest]
    shared[0:5, LIST_AT : LIST_AT + length] = jnp.concatenate(rows, axis=0)
    out_ref[extra_at:total_rows, :] = shared[...].astype(BF16)


def weight_rows(lists, weights, tile, modes, length):
    owners = lists.shape[0]
    width = tile.shape[1]
    total = jnp.zeros((owners, width), F32)
    for entry in range(length):
        total = total + jnp.where(lists[:, entry : entry + 1] == tile, weights[:, entry : entry + 1], 0.0)
    lane = lax.broadcasted_iota(jnp.int32, (modes, width), 1)
    sub = lax.broadcasted_iota(jnp.int32, (modes, width), 0)
    same = modulo(lane, modes) == sub
    return jnp.concatenate([jnp.where(same, total[o : o + 1], 0.0) for o in range(owners)], axis=0)


def rows_kernel(fields, modes, tiles_here, length, devices, paired, *refs):
    parts = refs[:-6]
    rows_ref, square_ref, w_ref, link_ref, extra, edges = refs[-6:]
    chips = devices // CORES
    height = tiles_here * modes
    extra_at, _, _ = layout(fields, modes, tiles_here)
    edge_rows = slice(extra_at, extra_at + edges.shape[2])
    list_rows = slice(extra_at, extra_at + 5)
    me = lax.axis_index("space")
    core = lax.rem(me, CORES)
    chip = lax.div(me, CORES)
    lane = lax.broadcasted_iota(jnp.int32, (modes, TILE), 1)
    first = lane & 1 == 0
    inside = lane < 2 * fields
    kinds = (core, 1 - core)
    sources = []
    for which, kind in enumerate(kinds):
        for q in range(chips):
            if paired:
                sources.append((parts[which * chips + q].at[...], jnp.bitwise_xor(chip, q), which))
            else:
                sources.append((parts[which].at[q], q, which))

    lists, weights = [], []
    for ref, place, which in sources:
        part = pltpu.roll(ref[list_rows, :].astype(F32), TILE - LIST_AT, 1)
        lists.append(part[0:1] * tiles_here + part[1:2])
        weights.append(part[2:3] + part[3:4] + part[4:5])
        edges[which, place] = ref[edge_rows, :].astype(F32)
    lists = jnp.concatenate(lists, axis=0)
    weights = jnp.concatenate(weights, axis=0)

    def coupling(which, place):
        return pltpu.roll(edges[which, place], TILE - LINK_AT, 1)

    def device_of(source, mixed):
        first = source < chips
        place = jnp.where(first, source, source - chips)
        if mixed:
            place = jnp.bitwise_xor(place, chip)
        return CORES * place + jnp.where(first, core, 1 - core)

    inner = devices * height
    total = inner + devices * 2 * modes
    column = lax.broadcasted_iota(jnp.int32, (devices, total), 1)
    outer = column - inner
    tile = jnp.where(
        outer < 0,
        device_of(over(column, height), paired) * tiles_here + modulo(over(column, modes), tiles_here),
        device_of(over(outer, 2 * modes), False) * tiles_here + modulo(over(outer, modes), 2) * (tiles_here - 1),
    )
    matrix = weight_rows(lists, weights, tile.astype(F32), modes, length)
    both = jnp.concatenate(split(matrix), axis=0)

    for index in range(devices):
        which, q = divmod(index, chips)
        kind = kinds[which]
        place = CORES * q + kind
        before = edges[1 - which, jnp.maximum(q - 1 + kind, 0), 0:modes, :]
        after = edges[1 - which, jnp.minimum(q + kind, chips - 1), 0:modes, :]
        before = before * (place > 0).astype(F32)
        after = after * (place < devices - 1).astype(F32)
        links = coupling(which, q)
        near = jnp.where(first, before, after)
        for f in range(fields):
            terms = near * links[f : f + 1]
            left = jnp.sum(jnp.where(first & inside, terms, 0.0), axis=1, keepdims=True)
            right = jnp.sum(jnp.where(first | ~inside, 0.0, terms), axis=1, keepdims=True)
            at = index * 2 * modes
            extra[f, at : at + modes, :] = jnp.where(lane == 0, left, 0.0)
            extra[f, at + modes : at + 2 * modes, :] = jnp.where(lane == TILE - 1, right, 0.0)

    squares = jnp.zeros((devices * modes, TILE), F32)
    for f in range(fields):
        tiles = jnp.concatenate(
            [ref[f * height : (f + 1) * height, :] for ref, _, _ in sources] + [extra[f].astype(BF16)], axis=0
        )
        rows = product(both, tiles)
        rows_ref[f] = rows
        squares = squares + rows * rows
    for o in range(devices):
        square_ref[o : o + 1, :] = jnp.sum(squares[o * modes : (o + 1) * modes], axis=0, keepdims=True)

    column = lax.broadcasted_iota(jnp.int32, (devices, w_ref.shape[1]), 1)
    local = over(column, modes)
    base = me * tiles_here
    tile = jnp.where(local <= tiles_here, base + local, jnp.where(local == tiles_here + 1, base - 1, -2))
    w_ref[...] = weight_rows(lists, weights, tile.astype(F32), modes, length)
    link_ref[0] = coupling(1, jnp.minimum(chip + core, chips - 1))
    link_ref[1] = coupling(1, jnp.maximum(chip - 1 + core, 0))


def update_kernel(samples, w_ref, rows_ref, link_ref, b_ref, j_ref, *rest):
    square_refs = rest[:-4]
    out_ref, returned, lower, upper = rest[-4:]
    fields, modes, cells = b_ref.shape
    tiles_here = cells // TILE
    owners = square_refs[0].shape[0]
    square = square_refs[0][...]
    for ref in square_refs[1:]:
        square = square + ref[...]
    factor = lax.rsqrt(square / samples + EPS)
    factor = jnp.concatenate([jnp.broadcast_to(factor[o : o + 1], (modes, TILE)) for o in range(owners)], axis=0)
    both = jnp.concatenate(split(jnp.transpose(w_ref[...])), axis=0)
    for g in range(fields):
        normalized = (rows_ref[g] * factor).astype(BF16)
        returned[g] = product(both, normalized)
    for t in range(tiles_here):
        at = slice(t * TILE, (t + 1) * TILE)
        values = [returned[g, t * modes : (t + 1) * modes, :] for g in range(fields)]
        for f in range(fields):
            center = b_ref[f, :, at].astype(F32)
            below = jnp.zeros((modes, TILE), F32)
            above = jnp.zeros((modes, TILE), F32)
            for g in range(fields):
                center = center + j_ref[g * fields + f, 0:1, at] * values[g]
                below = below + j_ref[g * fields + f, 1:2, at] * values[g]
                above = above + j_ref[g * fields + f, 2:3, at] * values[g]
            out_ref[f, :, at] = center
            lower[f, :, at] = below
            upper[f, :, at] = above
    wide = lax.broadcasted_iota(jnp.int32, (modes, cells), 1)
    nexts = slice(tiles_here * modes, (tiles_here + 1) * modes)
    lasts = slice((tiles_here + 1) * modes, (tiles_here + 2) * modes)
    for f in range(fields):
        head = jnp.zeros((modes, TILE), F32)
        tail = jnp.zeros((modes, TILE), F32)
        for g in range(fields):
            head = head + link_ref[0, g : g + 1, 2 * f : 2 * f + 1] * returned[g, nexts, :]
            tail = tail + link_ref[1, g : g + 1, 2 * f + 1 : 2 * f + 2] * returned[g, lasts, :]
        below = jnp.where(wide == cells - 1, head[:, 0:1], pltpu.roll(lower[f], cells - 1, 1))
        above = jnp.where(wide == 0, tail[:, TILE - 1 : TILE], pltpu.roll(upper[f], 1, 1))
        out_ref[f] = out_ref[f] + below + above


def shards(basis, jacobian, sample_list, sample_weight):
    space = lax.axis_size("space")
    mode = lax.axis_size("mode")
    modes, fields, cells = basis.shape
    length = sample_list.shape[1]
    tiles_here = cells // TILE
    height = space * modes
    width = pl.cdiv((tiles_here + 2) * modes, TILE) * TILE
    sent_rows = layout(fields, modes, tiles_here)[-1]
    b = jnp.transpose(basis, (1, 0, 2))
    j = jnp.transpose(jacobian, (1, 2, 0, 3))

    sent, wide = pl.pallas_call(
        applied_kernel,
        out_shape=(pltpu.VMEM((sent_rows, TILE), BF16), pltpu.VMEM((fields * fields, 3, cells), F32)),
        scratch_shapes=[
            pltpu.VMEM((fields, modes, cells), F32),
            pltpu.VMEM((fields, modes, cells), F32),
            pltpu.VMEM((fields * tiles_here * modes, TILE), F32),
            pltpu.VMEM((sent_rows - fields * tiles_here * modes, TILE), F32),
        ],
        name="applied",
    )(*(near(x) for x in (sample_list, sample_weight, b, j)))
    chips = space // CORES
    paired = chips <= PAIRED and chips & (chips - 1) == 0
    if paired:
        parts = [sent] + [
            lax.ppermute(sent, "space", [(i, i ^ (CORES * d)) for i in range(space)]) for d in range(1, chips)
        ]
    else:
        groups = [[core + CORES * q for q in range(chips)] for core in range(CORES)]
        parts = [lax.all_gather(sent, "space", axis=0, axis_index_groups=groups)]
    parts = parts + [lax.ppermute(part, "space", [(i, i ^ 1) for i in range(space)]) for part in parts]

    rows, square, matrix, links = pl.pallas_call(
        functools.partial(rows_kernel, fields, modes, tiles_here, length, space, paired),
        out_shape=(
            pltpu.VMEM((fields, height, TILE), F32),
            pltpu.VMEM((space, TILE), F32),
            pltpu.VMEM((height, width), F32),
            pltpu.VMEM((2, layout(fields, modes, tiles_here)[1], TILE), F32),
        ),
        scratch_shapes=[
            pltpu.VMEM((fields, space * 2 * modes, TILE), F32),
            pltpu.VMEM((CORES, chips, layout(fields, modes, tiles_here)[1], TILE), F32),
        ],
        name="rows",
    )(*(near(part) for part in parts))
    ring = list(range(0, mode, 2))[:1] + list(range(1, mode, 2)) + list(range(0, mode, 2))[:0:-1]
    squares = [square] + [
        lax.ppermute(square, "mode", [(ring[i], ring[(i + step) % mode]) for i in range(mode)])
        for step in range(mode - 1, 0, -1)
    ]

    update = pl.pallas_call(
        functools.partial(update_kernel, mode * modes * fields),
        out_shape=jax.ShapeDtypeStruct((fields, modes, cells), F32),
        scratch_shapes=[
            pltpu.VMEM((fields, width, TILE), F32),
            pltpu.VMEM((fields, modes, cells), F32),
            pltpu.VMEM((fields, modes, cells), F32),
        ],
        name="update",
    )(*(near(x) for x in (matrix, rows, links, b, wide, *squares)))
    return jnp.transpose(update, (1, 0, 2))


def solution(mesh):
    placed = (
        P("mode", None, "space"),
        P(None, None, None, "space"),
        P("space", None),
        P("space", None),
    )
    return jax.shard_map(
        shards, mesh=mesh, in_specs=placed, out_specs=P("mode", None, "space"), check_vma=False
    )
```

```python
import functools
import jax
import jax.numpy as jnp
from jax import lax
from jax.experimental import pallas as pl
from jax.experimental.pallas import tpu as pltpu
from jax.sharding import PartitionSpec as P

TILE = 128
EPS = 1e-05
F32 = jnp.float32
BF16 = jnp.bfloat16
CORES = 2
PAIRED = 4
LINK_AT = 32
LIST_AT = 64


def near(values):
    return pltpu.with_memory_space_constraint(values, pltpu.VMEM)


def over(values, by):
    return lax.shift_right_logical(values, by.bit_length() - 1) if by & (by - 1) == 0 else values // by


def modulo(values, by):
    return values & (by - 1) if by & (by - 1) == 0 else values % by


def layout(fields, modes, tiles_here):
    extra_at = fields * tiles_here * modes
    extra = pl.cdiv(max(modes, fields, 5), 8) * 8
    return extra_at, extra, extra_at + extra


def split(values):
    high = values.astype(BF16)
    return high, (values - high.astype(F32)).astype(BF16)


def product(both, values):
    parts = jnp.dot(both, values, preferred_element_type=F32)
    height = parts.shape[0] // 2
    return parts[:height] + parts[height:]


def applied_kernel(list_ref, weight_ref, b_ref, j_ref, out_ref, link_ref, lower, upper, applied, shared):
    fields, modes, cells = b_ref.shape
    length = list_ref.shape[1]
    tiles_here = cells // TILE
    height = tiles_here * modes
    extra_at, extra, total_rows = layout(fields, modes, tiles_here)
    wide = lax.broadcasted_iota(jnp.int32, (modes, cells), 1)
    lane = lax.broadcasted_iota(jnp.int32, (modes, TILE), 1)
    edge = jnp.zeros((modes, TILE), F32)
    shared[...] = jnp.zeros(shared.shape, F32)
    for f in range(fields):
        for g in range(fields):
            link_ref[f * fields + g] = j_ref[f, g].astype(F32)
    for g in range(fields):
        values = b_ref[g].astype(F32)
        below = pltpu.roll(values, 1, 1)
        above = pltpu.roll(values, cells - 1, 1)
        edge = jnp.where(lane == 2 * g, values[:, cells - 1 :], edge)
        edge = jnp.where(lane == 2 * g + 1, values[:, 0:1], edge)
        lower[g] = jnp.where(wide == 0, 0.0, below)
        upper[g] = jnp.where(wide == cells - 1, 0.0, above)
    for t in range(tiles_here):
        at = slice(t * TILE, (t + 1) * TILE)
        center = [b_ref[g, :, at].astype(F32) for g in range(fields)]
        below = [lower[g, :, at] for g in range(fields)]
        above = [upper[g, :, at] for g in range(fields)]
        for f in range(fields):
            total = jnp.zeros((modes, TILE), F32)
            for g in range(fields):
                total = total + link_ref[f * fields + g, 0:1, at] * center[g]
                total = total + link_ref[f * fields + g, 1:2, at] * below[g]
                total = total + link_ref[f * fields + g, 2:3, at] * above[g]
            applied[f * height + t * modes : f * height + (t + 1) * modes, :] = total
    out_ref[0 : fields * height, :] = applied[...].astype(BF16)
    lane = lane[0:1]
    rows = []
    for f in range(fields):
        row = jnp.zeros((1, TILE), F32)
        for g in range(fields):
            row = jnp.where(lane == LINK_AT + 2 * g, link_ref[f * fields + g, 1:2, 0:1], row)
            row = jnp.where(lane == LINK_AT + 2 * g + 1, link_ref[f * fields + g, 2:3, cells - 1 :], row)
        rows.append(row)
    shared[0:modes, :] = edge
    shared[0:fields, :] = shared[0:fields, :] + jnp.concatenate(rows, axis=0)
    tiles = list_ref[...]
    device = over(tiles, tiles_here)
    high, low = split(weight_ref[...])
    rest = weight_ref[...] - high.astype(F32) - low.astype(F32)
    rows = [device.astype(F32), (tiles - device * tiles_here).astype(F32), high.astype(F32), low.astype(F32), rest]
    shared[0:5, LIST_AT : LIST_AT + length] = jnp.concatenate(rows, axis=0)
    out_ref[extra_at:total_rows, :] = shared[...].astype(BF16)


def weight_rows(lists, weights, tile, modes, length):
    owners = lists.shape[0]
    width = tile.shape[1]
    total = jnp.zeros((owners, width), F32)
    for entry in range(length):
        total = total + jnp.where(lists[:, entry : entry + 1] == tile, weights[:, entry : entry + 1], 0.0)
    lane = lax.broadcasted_iota(jnp.int32, (modes, width), 1)
    sub = lax.broadcasted_iota(jnp.int32, (modes, width), 0)
    same = modulo(lane, modes) == sub
    return jnp.concatenate([jnp.where(same, total[o : o + 1], 0.0) for o in range(owners)], axis=0)


def rows_kernel(fields, modes, tiles_here, length, devices, paired, *refs):
    parts = refs[:-6]
    rows_ref, square_ref, list_ref, link_ref, extra, edges = refs[-6:]
    chips = devices // CORES
    height = tiles_here * modes
    extra_at, _, _ = layout(fields, modes, tiles_here)
    edge_rows = slice(extra_at, extra_at + edges.shape[2])
    list_rows = slice(extra_at, extra_at + 5)
    me = lax.axis_index("space")
    core = lax.rem(me, CORES)
    chip = lax.div(me, CORES)
    lane = lax.broadcasted_iota(jnp.int32, (modes, TILE), 1)
    first = lane & 1 == 0
    inside = lane < 2 * fields
    kinds = (core, 1 - core)
    sources = []
    for which, kind in enumerate(kinds):
        for q in range(chips):
            if paired:
                sources.append((parts[which * chips + q].at[...], jnp.bitwise_xor(chip, q), which))
            else:
                sources.append((parts[which].at[q], q, which))

    lists, weights = [], []
    for ref, place, which in sources:
        part = pltpu.roll(ref[list_rows, :].astype(F32), TILE - LIST_AT, 1)
        lists.append(part[0:1] * tiles_here + part[1:2])
        weights.append(part[2:3] + part[3:4] + part[4:5])
        edges[which, place] = ref[edge_rows, :].astype(F32)
    lists = jnp.concatenate(lists, axis=0)
    weights = jnp.concatenate(weights, axis=0)

    def coupling(which, place):
        return pltpu.roll(edges[which, place], TILE - LINK_AT, 1)

    def device_of(source, mixed):
        first = source < chips
        place = jnp.where(first, source, source - chips)
        if mixed:
            place = jnp.bitwise_xor(place, chip)
        return CORES * place + jnp.where(first, core, 1 - core)

    inner = devices * height
    total = inner + devices * 2 * modes
    column = lax.broadcasted_iota(jnp.int32, (devices, total), 1)
    outer = column - inner
    tile = jnp.where(
        outer < 0,
        device_of(over(column, height), paired) * tiles_here + modulo(over(column, modes), tiles_here),
        device_of(over(outer, 2 * modes), False) * tiles_here + modulo(over(outer, modes), 2) * (tiles_here - 1),
    )
    matrix = weight_rows(lists, weights, tile.astype(F32), modes, length)
    both = jnp.concatenate(split(matrix), axis=0)

    for index in range(devices):
        which, q = divmod(index, chips)
        kind = kinds[which]
        place = CORES * q + kind
        before = edges[1 - which, jnp.maximum(q - 1 + kind, 0), 0:modes, :]
        after = edges[1 - which, jnp.minimum(q + kind, chips - 1), 0:modes, :]
        before = before * (place > 0).astype(F32)
        after = after * (place < devices - 1).astype(F32)
        links = coupling(which, q)
        near = jnp.where(first, before, after)
        for f in range(fields):
            terms = near * links[f : f + 1]
            left = jnp.sum(jnp.where(first & inside, terms, 0.0), axis=1, keepdims=True)
            right = jnp.sum(jnp.where(first | ~inside, 0.0, terms), axis=1, keepdims=True)
            at = index * 2 * modes
            extra[f, at : at + modes, :] = jnp.where(lane == 0, left, 0.0)
            extra[f, at + modes : at + 2 * modes, :] = jnp.where(lane == TILE - 1, right, 0.0)

    squares = jnp.zeros((devices * modes, TILE), F32)
    for f in range(fields):
        tiles = jnp.concatenate(
            [ref[f * height : (f + 1) * height, :] for ref, _, _ in sources] + [extra[f].astype(BF16)], axis=0
        )
        rows = product(both, tiles)
        rows_ref[f] = rows
        squares = squares + rows * rows
    for o in range(devices):
        square_ref[o : o + 1, :] = jnp.sum(squares[o * modes : (o + 1) * modes], axis=0, keepdims=True)

    list_ref[0] = lists
    list_ref[1] = weights
    link_ref[0] = coupling(1, jnp.minimum(chip + core, chips - 1))
    link_ref[1] = coupling(1, jnp.maximum(chip - 1 + core, 0))


def return_kernel(modes, tiles_here, length, list_ref, both_ref):
    devices = list_ref.shape[1]
    width = both_ref.shape[0] // 2
    column = lax.broadcasted_iota(jnp.int32, (devices, width), 1)
    local = over(column, modes)
    base = lax.axis_index("space") * tiles_here
    tile = jnp.where(local <= tiles_here, base + local, jnp.where(local == tiles_here + 1, base - 1, -2))
    matrix = weight_rows(list_ref[0], list_ref[1], tile.astype(F32), modes, length)
    high, low = split(jnp.transpose(matrix))
    both_ref[0:width, :] = high
    both_ref[width:, :] = low


def update_kernel(samples, w_ref, rows_ref, link_ref, b_ref, j_ref, *rest):
    square_refs = rest[:-4]
    out_ref, returned, lower, upper = rest[-4:]
    fields, modes, cells = b_ref.shape
    tiles_here = cells // TILE
    owners = square_refs[0].shape[0]
    square = square_refs[0][...]
    for ref in square_refs[1:]:
        square = square + ref[...]
    factor = lax.rsqrt(square / samples + EPS)
    factor = jnp.concatenate([jnp.broadcast_to(factor[o : o + 1], (modes, TILE)) for o in range(owners)], axis=0)
    both = w_ref[...]
    for g in range(fields):
        normalized = (rows_ref[g] * factor).astype(BF16)
        returned[g] = product(both, normalized)
    for t in range(tiles_here):
        at = slice(t * TILE, (t + 1) * TILE)
        values = [returned[g, t * modes : (t + 1) * modes, :] for g in range(fields)]
        for f in range(fields):
            center = b_ref[f, :, at].astype(F32)
            below = jnp.zeros((modes, TILE), F32)
            above = jnp.zeros((modes, TILE), F32)
            for g in range(fields):
                center = center + j_ref[g * fields + f, 0:1, at] * values[g]
                below = below + j_ref[g * fields + f, 1:2, at] * values[g]
                above = above + j_ref[g * fields + f, 2:3, at] * values[g]
            out_ref[f, :, at] = center
            lower[f, :, at] = below
            upper[f, :, at] = above
    wide = lax.broadcasted_iota(jnp.int32, (modes, cells), 1)
    nexts = slice(tiles_here * modes, (tiles_here + 1) * modes)
    lasts = slice((tiles_here + 1) * modes, (tiles_here + 2) * modes)
    for f in range(fields):
        head = jnp.zeros((modes, TILE), F32)
        tail = jnp.zeros((modes, TILE), F32)
        for g in range(fields):
            head = head + link_ref[0, g : g + 1, 2 * f : 2 * f + 1] * returned[g, nexts, :]
            tail = tail + link_ref[1, g : g + 1, 2 * f + 1 : 2 * f + 2] * returned[g, lasts, :]
        below = jnp.where(wide == cells - 1, head[:, 0:1], pltpu.roll(lower[f], cells - 1, 1))
        above = jnp.where(wide == 0, tail[:, TILE - 1 : TILE], pltpu.roll(upper[f], 1, 1))
        out_ref[f] = out_ref[f] + below + above


def shards(basis, jacobian, sample_list, sample_weight):
    space = lax.axis_size("space")
    mode = lax.axis_size("mode")
    modes, fields, cells = basis.shape
    length = sample_list.shape[1]
    tiles_here = cells // TILE
    height = space * modes
    width = pl.cdiv((tiles_here + 2) * modes, TILE) * TILE
    sent_rows = layout(fields, modes, tiles_here)[-1]
    b = jnp.transpose(basis, (1, 0, 2))
    j = jnp.transpose(jacobian, (1, 2, 0, 3))

    sent, wide = pl.pallas_call(
        applied_kernel,
        out_shape=(pltpu.VMEM((sent_rows, TILE), BF16), pltpu.VMEM((fields * fields, 3, cells), F32)),
        scratch_shapes=[
            pltpu.VMEM((fields, modes, cells), F32),
            pltpu.VMEM((fields, modes, cells), F32),
            pltpu.VMEM((fields * tiles_here * modes, TILE), F32),
            pltpu.VMEM((sent_rows - fields * tiles_here * modes, TILE), F32),
        ],
        name="applied",
    )(sample_list, sample_weight, b, j)
    chips = space // CORES
    paired = chips <= PAIRED and chips & (chips - 1) == 0
    if paired:
        parts = [sent] + [
            lax.ppermute(sent, "space", [(i, i ^ (CORES * d)) for i in range(space)]) for d in range(1, chips)
        ]
    else:
        groups = [[core + CORES * q for q in range(chips)] for core in range(CORES)]
        parts = [lax.all_gather(sent, "space", axis=0, axis_index_groups=groups)]
    parts = parts + [lax.ppermute(part, "space", [(i, i ^ 1) for i in range(space)]) for part in parts]

    rows, square, lists, links = pl.pallas_call(
        functools.partial(rows_kernel, fields, modes, tiles_here, length, space, paired),
        out_shape=(
            pltpu.VMEM((fields, height, TILE), F32),
            pltpu.VMEM((space, TILE), F32),
            pltpu.VMEM((2, space, TILE), F32),
            pltpu.VMEM((2, layout(fields, modes, tiles_here)[1], TILE), F32),
        ),
        scratch_shapes=[
            pltpu.VMEM((fields, space * 2 * modes, TILE), F32),
            pltpu.VMEM((CORES, chips, layout(fields, modes, tiles_here)[1], TILE), F32),
        ],
        name="rows",
    )(*(near(part) for part in parts))
    ring = list(range(0, mode, 2))[:1] + list(range(1, mode, 2)) + list(range(0, mode, 2))[:0:-1]
    squares = [square] + [
        lax.ppermute(square, "mode", [(ring[i], ring[(i + step) % mode]) for i in range(mode)])
        for step in range(mode - 1, 0, -1)
    ]

    matrix = pl.pallas_call(
        functools.partial(return_kernel, modes, tiles_here, length),
        out_shape=pltpu.VMEM((2 * width, height), BF16),
        name="back",
    )(near(lists))
    update = pl.pallas_call(
        functools.partial(update_kernel, mode * modes * fields),
        out_shape=jax.ShapeDtypeStruct((fields, modes, cells), F32),
        scratch_shapes=[
            pltpu.VMEM((fields, width, TILE), F32),
            pltpu.VMEM((fields, modes, cells), F32),
            pltpu.VMEM((fields, modes, cells), F32),
        ],
        name="update",
    )(*(near(x) for x in (matrix, rows, links, b, wide, *squares)))
    return jnp.transpose(update, (1, 0, 2))


def solution(mesh):
    placed = (
        P("mode", None, "space"),
        P(None, None, None, "space"),
        P("space", None),
        P("space", None),
    )
    return jax.shard_map(
        shards, mesh=mesh, in_specs=placed, out_specs=P("mode", None, "space"), check_vma=False
    )
```

```python
import functools
import jax
import jax.numpy as jnp
from jax import lax
from jax.experimental import pallas as pl
from jax.experimental.pallas import tpu as pltpu
from jax.sharding import PartitionSpec as P

TILE = 128
EPS = 1e-05
F32 = jnp.float32
BF16 = jnp.bfloat16
CORES = 2
PAIRED = 4
LINK_AT = 32
LIST_AT = 64


def near(values):
    return pltpu.with_memory_space_constraint(values, pltpu.VMEM)


def over(values, by):
    return lax.shift_right_logical(values, by.bit_length() - 1) if by & (by - 1) == 0 else values // by


def modulo(values, by):
    return values & (by - 1) if by & (by - 1) == 0 else values % by


def layout(fields, modes, tiles_here):
    extra_at = fields * tiles_here * modes
    extra = pl.cdiv(max(modes, fields, 5), 8) * 8
    return extra_at, extra, extra_at + extra


def split(values):
    high = values.astype(BF16)
    return high, (values - high.astype(F32)).astype(BF16)


def product(both, values):
    parts = jnp.dot(both, values, preferred_element_type=F32)
    height = parts.shape[0] // 2
    return parts[:height] + parts[height:]


def applied_kernel(list_ref, weight_ref, b_ref, j_ref, out_ref, link_ref, lower, upper, applied, shared):
    fields, modes, cells = b_ref.shape
    length = list_ref.shape[1]
    tiles_here = cells // TILE
    height = tiles_here * modes
    extra_at, extra, total_rows = layout(fields, modes, tiles_here)
    wide = lax.broadcasted_iota(jnp.int32, (modes, cells), 1)
    lane = lax.broadcasted_iota(jnp.int32, (modes, TILE), 1)
    edge = jnp.zeros((modes, TILE), F32)
    shared[...] = jnp.zeros(shared.shape, F32)
    for f in range(fields):
        for g in range(fields):
            link_ref[f * fields + g] = j_ref[f, g].astype(F32)
    for g in range(fields):
        values = b_ref[g].astype(F32)
        below = pltpu.roll(values, 1, 1)
        above = pltpu.roll(values, cells - 1, 1)
        edge = jnp.where(lane == 2 * g, values[:, cells - 1 :], edge)
        edge = jnp.where(lane == 2 * g + 1, values[:, 0:1], edge)
        lower[g] = jnp.where(wide == 0, 0.0, below)
        upper[g] = jnp.where(wide == cells - 1, 0.0, above)
    for t in range(tiles_here):
        at = slice(t * TILE, (t + 1) * TILE)
        center = [b_ref[g, :, at].astype(F32) for g in range(fields)]
        below = [lower[g, :, at] for g in range(fields)]
        above = [upper[g, :, at] for g in range(fields)]
        for f in range(fields):
            total = jnp.zeros((modes, TILE), F32)
            for g in range(fields):
                total = total + link_ref[f * fields + g, 0:1, at] * center[g]
                total = total + link_ref[f * fields + g, 1:2, at] * below[g]
                total = total + link_ref[f * fields + g, 2:3, at] * above[g]
            applied[f * height + t * modes : f * height + (t + 1) * modes, :] = total
    out_ref[0 : fields * height, :] = applied[...].astype(BF16)
    lane = lane[0:1]
    rows = []
    for f in range(fields):
        row = jnp.zeros((1, TILE), F32)
        for g in range(fields):
            row = jnp.where(lane == LINK_AT + 2 * g, link_ref[f * fields + g, 1:2, 0:1], row)
            row = jnp.where(lane == LINK_AT + 2 * g + 1, link_ref[f * fields + g, 2:3, cells - 1 :], row)
        rows.append(row)
    shared[0:modes, :] = edge
    shared[0:fields, :] = shared[0:fields, :] + jnp.concatenate(rows, axis=0)
    tiles = list_ref[...]
    device = over(tiles, tiles_here)
    high, low = split(weight_ref[...])
    rest = weight_ref[...] - high.astype(F32) - low.astype(F32)
    rows = [device.astype(F32), (tiles - device * tiles_here).astype(F32), high.astype(F32), low.astype(F32), rest]
    shared[0:5, LIST_AT : LIST_AT + length] = jnp.concatenate(rows, axis=0)
    out_ref[extra_at:total_rows, :] = shared[...].astype(BF16)


def weight_rows(lists, weights, tile, modes, length):
    owners = lists.shape[0]
    width = tile.shape[1]
    total = jnp.zeros((owners, width), F32)
    for entry in range(length):
        total = total + jnp.where(lists[:, entry : entry + 1] == tile, weights[:, entry : entry + 1], 0.0)
    lane = lax.broadcasted_iota(jnp.int32, (modes, width), 1)
    sub = lax.broadcasted_iota(jnp.int32, (modes, width), 0)
    same = modulo(lane, modes) == sub
    return jnp.concatenate([jnp.where(same, total[o : o + 1], 0.0) for o in range(owners)], axis=0)


def rows_kernel(fields, modes, tiles_here, length, devices, paired, *refs):
    parts = refs[:-6]
    rows_ref, square_ref, list_ref, link_ref, extra, edges = refs[-6:]
    chips = devices // CORES
    height = tiles_here * modes
    extra_at, _, _ = layout(fields, modes, tiles_here)
    edge_rows = slice(extra_at, extra_at + edges.shape[2])
    list_rows = slice(extra_at, extra_at + 5)
    me = lax.axis_index("space")
    core = lax.rem(me, CORES)
    chip = lax.div(me, CORES)
    lane = lax.broadcasted_iota(jnp.int32, (modes, TILE), 1)
    first = lane & 1 == 0
    inside = lane < 2 * fields
    kinds = (core, 1 - core)
    sources = []
    for which, kind in enumerate(kinds):
        for q in range(chips):
            if paired:
                sources.append((parts[which * chips + q].at[...], jnp.bitwise_xor(chip, q), which))
            else:
                sources.append((parts[which].at[q], q, which))

    lists, weights = [], []
    for ref, place, which in sources:
        part = pltpu.roll(ref[list_rows, :].astype(F32), TILE - LIST_AT, 1)
        lists.append(part[0:1] * tiles_here + part[1:2])
        weights.append(part[2:3] + part[3:4] + part[4:5])
        edges[which, place] = ref[edge_rows, :].astype(F32)
    lists = jnp.concatenate(lists, axis=0)
    weights = jnp.concatenate(weights, axis=0)

    def coupling(which, place):
        return pltpu.roll(edges[which, place], TILE - LINK_AT, 1)

    def device_of(source, mixed):
        first = source < chips
        place = jnp.where(first, source, source - chips)
        if mixed:
            place = jnp.bitwise_xor(place, chip)
        return CORES * place + jnp.where(first, core, 1 - core)

    inner = devices * height
    total = inner + devices * 2 * modes
    column = lax.broadcasted_iota(jnp.int32, (devices, total), 1)
    outer = column - inner
    tile = jnp.where(
        outer < 0,
        device_of(over(column, height), paired) * tiles_here + modulo(over(column, modes), tiles_here),
        device_of(over(outer, 2 * modes), False) * tiles_here + modulo(over(outer, modes), 2) * (tiles_here - 1),
    )
    matrix = weight_rows(lists, weights, tile.astype(F32), modes, length)
    both = jnp.concatenate(split(matrix), axis=0)

    for index in range(devices):
        which, q = divmod(index, chips)
        kind = kinds[which]
        place = CORES * q + kind
        before = edges[1 - which, jnp.maximum(q - 1 + kind, 0), 0:modes, :]
        after = edges[1 - which, jnp.minimum(q + kind, chips - 1), 0:modes, :]
        before = before * (place > 0).astype(F32)
        after = after * (place < devices - 1).astype(F32)
        links = coupling(which, q)
        near = jnp.where(first, before, after)
        for f in range(fields):
            terms = near * links[f : f + 1]
            left = jnp.sum(jnp.where(first & inside, terms, 0.0), axis=1, keepdims=True)
            right = jnp.sum(jnp.where(first | ~inside, 0.0, terms), axis=1, keepdims=True)
            at = index * 2 * modes
            extra[f, at : at + modes, :] = jnp.where(lane == 0, left, 0.0)
            extra[f, at + modes : at + 2 * modes, :] = jnp.where(lane == TILE - 1, right, 0.0)

    squares = jnp.zeros((devices * modes, TILE), F32)
    for f in range(fields):
        tiles = jnp.concatenate(
            [ref[f * height : (f + 1) * height, :] for ref, _, _ in sources] + [extra[f].astype(BF16)], axis=0
        )
        rows = product(both, tiles)
        rows_ref[f] = rows
        squares = squares + rows * rows
    for o in range(devices):
        square_ref[o : o + 1, :] = jnp.sum(squares[o * modes : (o + 1) * modes], axis=0, keepdims=True)

    list_ref[0] = lists
    list_ref[1] = weights
    link_ref[0] = coupling(1, jnp.minimum(chip + core, chips - 1))
    link_ref[1] = coupling(1, jnp.maximum(chip - 1 + core, 0))


def return_kernel(modes, tiles_here, length, list_ref, both_ref):
    devices = list_ref.shape[1]
    width = both_ref.shape[0] // 2
    column = lax.broadcasted_iota(jnp.int32, (devices, width), 1)
    local = over(column, modes)
    base = lax.axis_index("space") * tiles_here
    tile = jnp.where(local <= tiles_here, base + local, jnp.where(local == tiles_here + 1, base - 1, -2))
    matrix = weight_rows(list_ref[0], list_ref[1], tile.astype(F32), modes, length)
    high, low = split(jnp.transpose(matrix))
    both_ref[0:width, :] = high
    both_ref[width:, :] = low


def update_kernel(samples, w_ref, rows_ref, link_ref, b_ref, j_ref, *rest):
    square_refs = rest[:-4]
    out_ref, returned, lower, upper = rest[-4:]
    fields, modes, cells = b_ref.shape
    tiles_here = cells // TILE
    owners = square_refs[0].shape[0]
    square = square_refs[0][...]
    for ref in square_refs[1:]:
        square = square + ref[...]
    factor = lax.rsqrt(square / samples + EPS)
    factor = jnp.concatenate([jnp.broadcast_to(factor[o : o + 1], (modes, TILE)) for o in range(owners)], axis=0)
    both = w_ref[...]
    for g in range(fields):
        normalized = (rows_ref[g] * factor).astype(BF16)
        returned[g] = product(both, normalized)
    for t in range(tiles_here):
        at = slice(t * TILE, (t + 1) * TILE)
        values = [returned[g, t * modes : (t + 1) * modes, :] for g in range(fields)]
        for f in range(fields):
            center = b_ref[f, :, at].astype(F32)
            below = jnp.zeros((modes, TILE), F32)
            above = jnp.zeros((modes, TILE), F32)
            for g in range(fields):
                center = center + j_ref[g * fields + f, 0:1, at] * values[g]
                below = below + j_ref[g * fields + f, 1:2, at] * values[g]
                above = above + j_ref[g * fields + f, 2:3, at] * values[g]
            out_ref[f, :, at] = center
            lower[f, :, at] = below
            upper[f, :, at] = above
    wide = lax.broadcasted_iota(jnp.int32, (modes, cells), 1)
    nexts = slice(tiles_here * modes, (tiles_here + 1) * modes)
    lasts = slice((tiles_here + 1) * modes, (tiles_here + 2) * modes)
    for f in range(fields):
        head = jnp.zeros((modes, TILE), F32)
        tail = jnp.zeros((modes, TILE), F32)
        for g in range(fields):
            head = head + link_ref[0, g : g + 1, 2 * f : 2 * f + 1] * returned[g, nexts, :]
            tail = tail + link_ref[1, g : g + 1, 2 * f + 1 : 2 * f + 2] * returned[g, lasts, :]
        below = jnp.where(wide == cells - 1, head[:, 0:1], pltpu.roll(lower[f], cells - 1, 1))
        above = jnp.where(wide == 0, tail[:, TILE - 1 : TILE], pltpu.roll(upper[f], 1, 1))
        out_ref[f] = out_ref[f] + below + above


def shards(basis, jacobian, sample_list, sample_weight):
    space = lax.axis_size("space")
    mode = lax.axis_size("mode")
    modes, fields, cells = basis.shape
    length = sample_list.shape[1]
    tiles_here = cells // TILE
    height = space * modes
    width = pl.cdiv((tiles_here + 2) * modes, TILE) * TILE
    sent_rows = layout(fields, modes, tiles_here)[-1]
    b = jnp.transpose(basis, (1, 0, 2))
    j = jnp.transpose(jacobian, (1, 2, 0, 3))

    sent, wide = pl.pallas_call(
        applied_kernel,
        out_shape=(pltpu.VMEM((sent_rows, TILE), BF16), pltpu.VMEM((fields * fields, 3, cells), F32)),
        scratch_shapes=[
            pltpu.VMEM((fields, modes, cells), F32),
            pltpu.VMEM((fields, modes, cells), F32),
            pltpu.VMEM((fields * tiles_here * modes, TILE), F32),
            pltpu.VMEM((sent_rows - fields * tiles_here * modes, TILE), F32),
        ],
        name="applied",
    )(sample_list, sample_weight, b, j)
    chips = space // CORES
    paired = chips <= PAIRED and chips & (chips - 1) == 0
    if paired:
        parts = [sent] + [
            lax.ppermute(sent, "space", [(i, i ^ (CORES * d)) for i in range(space)]) for d in range(1, chips)
        ]
    else:
        groups = [[core + CORES * q for q in range(chips)] for core in range(CORES)]
        parts = [lax.all_gather(sent, "space", axis=0, axis_index_groups=groups)]
    parts = parts + [lax.ppermute(part, "space", [(i, i ^ 1) for i in range(space)]) for part in parts]

    rows, square, lists, links = pl.pallas_call(
        functools.partial(rows_kernel, fields, modes, tiles_here, length, space, paired),
        out_shape=(
            pltpu.VMEM((fields, height, TILE), F32),
            pltpu.VMEM((space, TILE), F32),
            pltpu.VMEM((2, space, TILE), F32),
            pltpu.VMEM((2, layout(fields, modes, tiles_here)[1], TILE), F32),
        ),
        scratch_shapes=[
            pltpu.VMEM((fields, space * 2 * modes, TILE), F32),
            pltpu.VMEM((CORES, chips, layout(fields, modes, tiles_here)[1], TILE), F32),
        ],
        name="rows",
    )(*(near(part) for part in parts))
    ring = list(range(mode))
    squares = [square] + [
        lax.ppermute(square, "mode", [(ring[i], ring[(i + step) % mode]) for i in range(mode)])
        for step in range(mode - 1, 0, -1)
    ]

    matrix = pl.pallas_call(
        functools.partial(return_kernel, modes, tiles_here, length),
        out_shape=pltpu.VMEM((2 * width, height), BF16),
        name="back",
    )(near(lists))
    update = pl.pallas_call(
        functools.partial(update_kernel, mode * modes * fields),
        out_shape=jax.ShapeDtypeStruct((fields, modes, cells), F32),
        scratch_shapes=[
            pltpu.VMEM((fields, width, TILE), F32),
            pltpu.VMEM((fields, modes, cells), F32),
            pltpu.VMEM((fields, modes, cells), F32),
        ],
        name="update",
    )(*(near(x) for x in (matrix, rows, links, b, wide, *squares)))
    return jnp.transpose(update, (1, 0, 2))


def solution(mesh):
    placed = (
        P("mode", None, "space"),
        P(None, None, None, "space"),
        P("space", None),
        P("space", None),
    )
    return jax.shard_map(
        shards, mesh=mesh, in_specs=placed, out_specs=P("mode", None, "space"), check_vma=False
    )
```
